32 devices in a mesh: dp: 8 (over y, x, core), tensor: 4 (over z).
Axes of the slice: x: 2, y: 2, z: 4, core: 2. Of those that a mesh axis runs over, the one named last changes fastest.
Arguments:
- inputs: bfloat16 [24, 1024, 768], P('dp', 'tensor'), may hold values from -6 to 6
- condition: bfloat16 [24, 128], P('dp'), may hold values from -6 to 6
- doc_ids: int32 [24, 1024], P('dp'), may hold values from 0 to 7, as said below
- positions: int32 [24, 1024], P('dp'), may hold values from 0 to 1023, as said below
- w_qkv: bfloat16 [3, 768, 768], P(None, 'dp', 'tensor'), may hold values from -0.21875 to 0.21875
- w_out: bfloat16 [768, 768], P('tensor', 'dp'), may hold values from -1.75 to 1.75
- w_up: bfloat16 [768, 3072], P('dp', 'tensor'), may hold values from -0.21875 to 0.21875
- bias_up: bfloat16 [4, 768], P('tensor', 'dp'), may hold values from -3 to 3
- w_down: bfloat16 [3072, 768], P('tensor', 'dp'), may hold values from -0.109375 to 0.109375
- bias_down: bfloat16 [768], P('dp'), may hold values from -3 to 3
- gain_one: bfloat16 [768], P('dp'), may hold values from 0.5 to 1.5
- gain_two: bfloat16 [768], P('dp'), may hold values from 0.5 to 1.5
- w_ada: bfloat16 [128, 4608], P(None, 'dp'), may hold values from -0.5 to 0.5
- bias_ada: bfloat16 [4608], P('dp'), may hold values from -2 to 2
- out_grad: bfloat16 [24, 1024, 768], P('dp', 'tensor'), may hold values from -6 to 6
Outputs:
- block_out: bfloat16 [24, 1024, 768], P('dp', 'tensor')
- input_grad: bfloat16 [24, 1024, 768], P('dp', 'tensor')
- cond_grad: float32 [24, 128], P('dp')
- grad_qkv: float32 [3, 768, 768], P(None, 'dp', 'tensor')
- grad_out: float32 [768, 768], P('tensor', 'dp')
- grad_up: float32 [768, 3072], P('dp', 'tensor')
- grad_bias_up: float32 [4, 768], P('tensor', 'dp')
- grad_down: float32 [3072, 768], P('tensor', 'dp')
- grad_bias_down: float32 [768], P('dp')
- grad_gain_one: float32 [768], P('dp')
- grad_gain_two: float32 [768], P('dp')
- grad_ada: float32 [128, 4608], P(None, 'dp')
- grad_bias_ada: float32 [4608], P('dp')
The draws below stay inside these ranges and needn't reach their ends.
Inputs may be any that keep to these rules, and one draw needn't show every extreme that they name: `doc_ids`: within each sequence the document numbers begin at 0 at the first token and rise by one at the first token of each further document; each document is a run of consecutive tokens; a sequence holds at most 8 documents. `positions`: each token's offset from the first token of its document.
All inputs are finite; a program needn't handle non-finite values.
Results may differ from the reference program's by a relative error of at most 0.013.
The reference program's roundings to bfloat16 on the way count: a program that leaves them out, or rounds other values in their place, can miss the bound.
Values may be sent and summed in bfloat16 or wider, within the bound.
No kernel may reach another device: no remote copies, remote signals or barrier semaphores. Data moves between devices by JAX's collectives and lax.ppermute only.
A program may use at most 128 MiB of HBM per device.

```python
import jax
import jax.numpy as jnp
from jax import lax

D = 768
HEADS = 12
HEAD = 64
FF = 3072
COND = 128
SEQ = 1024
SEQS = 24
N_TENSOR = 4


def doc_layout(key):
    column = jnp.arange(SEQ, dtype=jnp.int32)[None, :]
    row_index = jnp.arange(SEQS, dtype=jnp.int32)[:, None]
    opening = jax.random.randint(jax.random.fold_in(key, 7), (SEQS, SEQ), 0, max(SEQ // 4, 2)) == 0
    opening = jnp.logical_and(opening, row_index != 0)
    even_cuts = jnp.logical_and(row_index == SEQS - 1, column % (SEQ // 8) == 0)
    opening = jnp.logical_or(opening, even_cuts)
    opening = jnp.logical_or(opening, column == 0)
    raw_number = jnp.cumsum(opening.astype(jnp.int32), axis=1) - 1
    kept = jnp.logical_and(opening, raw_number <= 7)
    doc_number = jnp.minimum(raw_number, 7)
    start_at = lax.cummax(jnp.where(kept, column, 0), axis=1)
    return (doc_number.astype(jnp.int32), (column - start_at).astype(jnp.int32))


def draw_doc_ids(key, part):
    return doc_layout(key)[0]


def draw_positions(key, part):
    return doc_layout(key)[1]


def shard_levels(rng, shape, pieces, least, top_value):
    def one(dim, shards_of):
        steps = jax.random.uniform(jax.random.fold_in(jax.random.fold_in(rng, 6), dim), (shards_of,), jnp.float32, least / len(pieces), top_value / len(pieces))
        return jnp.repeat(jnp.exp(steps), shape[dim] // shards_of).reshape((-1,) + (1,) * (len(shape) - dim - 1))

    loudness = one(*pieces[0])
    for cut in pieces[1:]:
        loudness = loudness * one(*cut)
    return loudness


def bell_draw(stream_key, dims, deviation, reach, pieces=(), kind=jnp.bfloat16):
    level = shard_levels(stream_key, dims, pieces, -0.22, 0.18) if pieces else 1.0
    values = jax.random.normal(stream_key, dims, jnp.float32) * deviation * level
    return jnp.minimum(jnp.maximum(values, -reach), reach).astype(kind)


def setup_inputs(seed: int = 0) -> dict:
    streams_of = jax.random.split(jax.random.key(seed), 16)
    inputs = bell_draw(streams_of[0], (SEQS, SEQ, D), 1.0, 6.0, ((0, 8), (1, 4)))
    condition = bell_draw(streams_of[1], (SEQS, COND), 1.0, 6.0, ((0, 8),))
    doc_ids = draw_doc_ids(jax.random.fold_in(streams_of[15], 71), 0)
    positions = draw_positions(jax.random.fold_in(streams_of[15], 71), 0)
    w_qkv = bell_draw(streams_of[4], (3, D, D), D ** -0.5, 0.21875, ((1, 8), (2, 4)))
    w_out = bell_draw(streams_of[5], (D, D), (D // 64) ** -0.5, 1.75, ((0, 4), (1, 8)))
    w_up = bell_draw(streams_of[6], (D, FF), D ** -0.5, 0.21875, ((0, 8), (1, 4)))
    bias_up = bell_draw(streams_of[7], (N_TENSOR, FF // N_TENSOR), 0.5, 3.0, ((0, 4), (1, 8)))
    w_down = bell_draw(streams_of[8], (FF, D), FF ** -0.5, 0.109375, ((0, 4), (1, 8)))
    bias_down = bell_draw(streams_of[9], (D,), 0.5, 3.0, ((0, 8),))
    gain_one = jnp.clip(1.0 + 0.1 * jax.random.normal(streams_of[10], (D,), jnp.float32), 0.5, 1.5).astype(jnp.bfloat16)
    gain_two = jnp.clip(1.0 + 0.1 * jax.random.normal(streams_of[11], (D,), jnp.float32), 0.5, 1.5).astype(jnp.bfloat16)
    w_ada = bell_draw(streams_of[12], (COND, 6 * D), COND ** -0.5, 0.5, ((1, 8),))
    bias_ada = bell_draw(streams_of[13], (6 * D,), 0.3, 2.0, ((0, 8),))
    out_grad = bell_draw(streams_of[14], (SEQS, SEQ, D), 1.0, 6.0, ((0, 8), (1, 4)))
    return {"inputs": inputs, "condition": condition, "doc_ids": doc_ids, "positions": positions, "w_qkv": w_qkv, "w_out": w_out, "w_up": w_up, "bias_up": bias_up, "w_down": w_down, "bias_down": bias_down, "gain_one": gain_one, "gain_two": gain_two, "w_ada": w_ada, "bias_ada": bias_ada, "out_grad": out_grad}


PRECISE = lax.Precision.HIGHEST
EPSILON = 1e-05

@jax.custom_vjp
def low(v):
    return lax.optimization_barrier(v.astype(jnp.bfloat16)).astype(jnp.float32)

@jax.custom_vjp
def low_back(v):
    return v

def low_keep(v):
    return (low(v), None)

def low_pass(kept, grad):
    return (grad,)

def back_keep(v):
    return (v, None)

def back_low(kept, grad):
    return (low(grad),)
low.defvjp(low_keep, low_pass)
low_back.defvjp(back_keep, back_low)

def product(left, right):
    return jnp.dot(left, right, precision=PRECISE, preferred_element_type=jnp.float32)

def layer_norm(features, gain_vec):
    average = lax.optimization_barrier(jnp.mean(features, axis=-1, keepdims=True))
    centred = features - average
    spread = lax.optimization_barrier(jnp.mean(centred * centred, axis=-1, keepdims=True))
    return centred * lax.rsqrt(spread + EPSILON) * gain_vec

def norm_mod(features, gain_vec, scale_vec, shift_vec):
    return layer_norm(features, gain_vec) * (1.0 + scale_vec) + shift_vec

def angles(places):
    half_size = HEAD // 2
    frequencies = 10000.0 ** (-2.0 * jnp.arange(half_size, dtype=jnp.float32) / HEAD)
    turned = places.astype(jnp.float32)[:, None] * frequencies[None, :]
    return (jnp.cos(turned)[:, None, :], jnp.sin(turned)[:, None, :])

def rotate(vectors, cosine, sine_vals):
    half_size = vectors.shape[-1] // 2
    first_half = vectors[..., :half_size]
    second_half = vectors[..., half_size:]
    return jnp.concatenate([first_half * cosine - second_half * sine_vals, second_half * cosine + first_half * sine_vals], axis=-1)

def block_layer(tokens, cond_row, documents, places, w_qkv, w_out, w_up, bias_up, w_down, bias_down, gain_one, gain_two, w_ada, bias_ada):
    modulation = product(jax.nn.silu(cond_row)[None, :], w_ada)[0] + bias_ada
    shift_one, scale_one, gate_one, shift_two, scale_two, gate_two = jnp.split(modulation, 6)
    length = tokens.shape[0]
    normed = low(norm_mod(tokens, gain_one, scale_one, shift_one))
    cosine, sine_vals = angles(places)
    queries = low_back(product(normed, w_qkv[0])).reshape(length, HEADS, HEAD)
    key_rows = low_back(product(normed, w_qkv[1])).reshape(length, HEADS, HEAD)
    values = low_back(product(normed, w_qkv[2])).reshape(length, HEADS, HEAD)
    queries = low(rotate(queries, cosine, sine_vals))
    key_rows = low(rotate(key_rows, cosine, sine_vals))
    values = low(values)
    block_rows = min(512, length)
    block_count = length // block_rows

    def attend(block_index):
        first_row = block_index * block_rows
        query_blk = lax.dynamic_slice_in_dim(queries, first_row, block_rows, 0)
        doc_blk = lax.dynamic_slice_in_dim(documents, first_row, block_rows, 0)
        scores = low_back(jnp.einsum('qhe,khe->hqk', query_blk, key_rows, precision=PRECISE) * HEAD ** (-0.5))
        same_doc = (doc_blk[:, None] == documents[None, :])[None]
        scores = jnp.where(same_doc, scores, -1e+30)
        log_total = jax.nn.logsumexp(scores, axis=-1, keepdims=True)
        probabilities = low(jnp.exp(scores - log_total))
        return jnp.einsum('hqk,khe->qhe', probabilities, values, precision=PRECISE)
    mixture = lax.map(jax.checkpoint(attend), jnp.arange(block_count, dtype=jnp.int32))
    mixture = low_back(low(mixture.reshape(length, HEADS * HEAD)))
    attention = low_back(product(mixture, w_out))
    middle = tokens + gate_one * attention
    normed_two = low(norm_mod(middle, gain_two, scale_two, shift_two))
    hidden = low_back(product(normed_two, w_up) + bias_up)
    activated = low(jax.nn.gelu(hidden, approximate=True))
    down_sum = low_back(product(activated, w_down)) + bias_down
    return middle + gate_two * down_sum

def reference(inputs, condition, doc_ids, positions, w_qkv, w_out, w_up, bias_up, w_down, bias_down, gain_one, gain_two, w_ada, bias_ada, out_grad):
    params = tuple((weight.astype(jnp.float32) for weight in (w_qkv, w_out, w_up, bias_up.reshape(-1), w_down, bias_down, gain_one, gain_two, w_ada, bias_ada)))

    def one_sequence(running, items):
        tokens, cond_row, documents, places, cotangent = items

        def forward(token_vals, cond_vals, *weights):
            return block_layer(token_vals, cond_vals, documents, places, *weights)
        result, pull_back = jax.vjp(forward, tokens.astype(jnp.float32), cond_row.astype(jnp.float32), *params)
        grads = pull_back(cotangent.astype(jnp.float32))
        running = tuple((old + new for old, new in zip(running, grads[2:])))
        return (running, (result.astype(jnp.bfloat16), grads[0].astype(jnp.bfloat16), grads[1]))
    zeros = tuple((jnp.zeros_like(weight) for weight in params))
    totals, (outputs, input_grads, cond_grads) = lax.scan(one_sequence, zeros, (inputs, condition, doc_ids, positions, out_grad))
    return (outputs, input_grads, cond_grads, totals[0], totals[1], totals[2], totals[3].reshape(bias_up.shape), totals[4], totals[5], totals[6], totals[7], totals[8], totals[9])
```

```python
from functools import partial

import jax
import jax.numpy as jnp
import numpy as np
from jax import lax
from jax.experimental import pallas as pl
from jax.experimental.pallas import tpu as pltpu
from jax.sharding import PartitionSpec as P

HEAD = 64
PRECISE = lax.Precision.HIGHEST
EPSILON = 1e-05
F32 = jnp.float32
BF16 = jnp.bfloat16
PAIR = 2 * HEAD
BOTH = ("dp", "tensor")
ANY = pl.BlockSpec(memory_space=pl.ANY)
VMEM = pl.BlockSpec(memory_space=pltpu.VMEM)
SMEM = pl.BlockSpec(memory_space=pltpu.SMEM)


def dot_nn(a, b):
    return jnp.dot(a, b, preferred_element_type=F32)


def dot_nt(a, b):
    return lax.dot_general(a, b, (((1,), (1,)), ((), ())), preferred_element_type=F32)


def params(**more):
    return pltpu.CompilerParams(vmem_limit_bytes=58 << 20, **more)


def cost(flops, nbytes, trans=0):
    return pl.CostEstimate(flops=int(flops), bytes_accessed=int(nbytes), transcendentals=int(trans))


def shape(dims, kind):
    return jax.ShapeDtypeStruct(tuple(dims), kind)


def row_at(me_ref, index, rows):
    return pl.multiple_of((me_ref[0] ^ index) * rows, rows)


def qkv_kernel(blocks, me, *refs):
    x_refs, refs = refs[:4], refs[4:]
    (mul, add, cosine, sin_a, sin_b), refs = refs[:5], refs[5:]
    qk_refs, v_refs, refs = refs[:blocks], refs[blocks : 2 * blocks], refs[2 * blocks :]
    (n_t, q_out, k_out, v_out, q_t, k_t, v_t), (w_buf, n_buf, sems) = refs[:7], refs[7:]
    rows = qk_refs[0].shape[1]
    copies = []
    for j in range(blocks):
        at = row_at(me, j, rows)
        copies.append(
            pltpu.make_async_copy(qk_refs[j], w_buf.at[0:2, pl.ds(at, rows), :], sems.at[0, j])
        )
        copies.append(
            pltpu.make_async_copy(v_refs[j].at[0], w_buf.at[2, pl.ds(at, rows), :], sems.at[1, j])
        )
    for copy in copies:
        copy.start()
    part = x_refs[0].shape[0]
    for b, x_ref in enumerate(x_refs):
        x = x_ref[...].astype(F32)
        centred = x - jnp.mean(x, axis=-1, keepdims=True)
        spread = jnp.mean(centred * centred, axis=-1, keepdims=True)
        n_buf[b * part : (b + 1) * part, :] = (
            centred * lax.rsqrt(spread + EPSILON) * mul[...] + add[...]
        ).astype(BF16)
    normed = n_buf[...]
    n_t[...] = normed.T
    for copy in copies:
        copy.wait()
    width = q_out.shape[1]
    for c, (flat, turned, factor) in enumerate(((q_out, q_t, HEAD**-0.5), (k_out, k_t, 1.0))):
        proj = dot_nn(normed, w_buf[c])
        for p in range(width // PAIR):
            lanes = slice(p * PAIR, (p + 1) * PAIR)
            r = proj[:, lanes]
            spun = (
                r * cosine[...]
                + pltpu.roll(r, PAIR - HEAD // 2, 1) * sin_a[...]
                + pltpu.roll(r, HEAD // 2, 1) * sin_b[...]
            )
            spun = spun.astype(BF16) * BF16(factor)
            flat[:, lanes] = spun
            turned[lanes, :] = spun.T
    values = dot_nn(normed, w_buf[2]).astype(BF16)
    v_out[...] = values
    v_t[...] = values.T


def qkv(me, x_parts, mul, add, cosine, sin_a, sin_b, qk_pieces, v_pieces):
    blocks = len(qk_pieces)
    part, width = x_parts[0].shape
    length = 4 * part
    cols = qk_pieces[0].shape[2]
    flat, turned = shape((length, cols), BF16), shape((cols, length), BF16)
    return pl.pallas_call(
        partial(qkv_kernel, blocks),
        out_shape=[shape((width, length), BF16), flat, flat, flat, turned, turned, turned],
        in_specs=[SMEM] + [VMEM] * 9 + [ANY] * (2 * blocks),
        out_specs=[VMEM] * 7,
        scratch_shapes=[
            pltpu.VMEM((3, width, cols), BF16),
            pltpu.VMEM((length, width), BF16),
            pltpu.SemaphoreType.DMA((2, blocks)),
        ],
        compiler_params=params(),
        cost_estimate=cost(6 * length * width * cols, 16e6),
        name="qkv",
    )(me, *x_parts, mul, add, cosine, sin_a, sin_b, *qk_pieces, *v_pieces)


def head_mask(ref, head):
    lane = lax.broadcasted_iota(jnp.int32, (1, PAIR), 1)
    return jnp.where((lane // HEAD) == head, ref[...], jnp.zeros((), BF16))


def same_doc_bias(bias, doc_row, doc_col):
    bias[...] = jnp.where(doc_col[...] == doc_row[...], 0.0, -1e30)


def attend_kernel(q, k, v_t, doc_row, doc_col, mix_t, log_sum, bias):
    @pl.when(pl.program_id(0) == 0)
    def _():
        same_doc_bias(bias, doc_row, doc_col)

    for h in range(2):
        rows = slice(h * HEAD, (h + 1) * HEAD)
        scores = dot_nt(head_mask(k, h), q[...]) + bias[...]
        top = jnp.max(scores, axis=0, keepdims=True)
        weights = jnp.exp(scores - top)
        total = jnp.sum(weights, axis=0, keepdims=True)
        mixed = dot_nn(v_t[rows, :], weights.astype(BF16))
        mix_t[rows, :] = (mixed / total).astype(BF16)
        log_sum[0, h : h + 1, :] = top + jnp.log(total)


def attend(q, k, v_t, doc_row, doc_col):
    length, width = q.shape
    pairs = width // PAIR
    flat = pl.BlockSpec((length, PAIR), lambda i: (0, i))
    turned = pl.BlockSpec((PAIR, length), lambda i: (i, 0))
    return pl.pallas_call(
        attend_kernel,
        grid=(pairs,),
        in_specs=[
            flat,
            flat,
            turned,
            pl.BlockSpec((1, length), lambda i: (0, 0)),
            pl.BlockSpec((length, 1), lambda i: (0, 0)),
        ],
        out_specs=[turned, pl.BlockSpec((1, 2, length), lambda i: (i, 0, 0))],
        out_shape=[shape((width, length), BF16), shape((pairs, 2, length), F32)],
        scratch_shapes=[pltpu.VMEM((length, length), F32)],
        compiler_params=params(),
        cost_estimate=cost(16 * length * length * width, 8e6),
        name="attend",
    )(q, k, v_t, doc_row, doc_col)


def load_out_weight(me, pieces, buf, sems):
    rows = pieces[0].shape[1]
    copies = [
        pltpu.make_async_copy(
            piece.at[1], buf.at[pl.ds(row_at(me, j, rows), rows), :], sems.at[j]
        )
        for j, piece in enumerate(pieces)
    ]
    for copy in copies:
        copy.start()
    return copies


def middle_kernel(blocks, me, *refs):
    x_refs, g_refs, refs = refs[:4], refs[4:8], refs[8:]
    (mix_t, gate_one, mul, add, gate_two), refs = refs[:5], refs[5:]
    pieces, refs = refs[:blocks], refs[blocks:]
    (att, n_two, n_two_t, d_down, d_down_t, d_bias), (w_buf, sems) = refs[:6], refs[6:]
    copies = load_out_weight(me, pieces, w_buf, sems)
    part = x_refs[0].shape[0]
    total = jnp.zeros(gate_two.shape, F32)
    for b, g_ref in enumerate(g_refs):
        scaled = g_ref[...].astype(F32) * gate_two[...]
        total += jnp.sum(scaled, axis=0, keepdims=True)
        d_down[b * part : (b + 1) * part, :] = scaled.astype(BF16)
    d_bias[...] = total
    d_down_t[...] = d_down[...].T
    mixture = mix_t[...].T
    for copy in copies:
        copy.wait()
    for b, x_ref in enumerate(x_refs):
        rows = slice(b * part, (b + 1) * part)
        attention = dot_nt(mixture[rows, :], w_buf[...])
        att[rows, :] = attention
        mid = x_ref[...].astype(F32) + gate_one[...] * attention
        centred = mid - jnp.mean(mid, axis=-1, keepdims=True)
        spread = jnp.mean(centred * centred, axis=-1, keepdims=True)
        n_two[rows, :] = (
            centred * lax.rsqrt(spread + EPSILON) * mul[...] + add[...]
        ).astype(BF16)
    n_two_t[...] = n_two[...].T


def middle(me, x_parts, g_parts, mix_t, gate_one, mul, add, gate_two, pieces):
    blocks = len(pieces)
    part, width = x_parts[0].shape
    length = 4 * part
    inner = mix_t.shape[0]
    flat, turned = shape((length, width), BF16), shape((width, length), BF16)
    return pl.pallas_call(
        partial(middle_kernel, blocks),
        out_shape=[shape((length, width), F32), flat, turned, flat, turned, shape((1, width), F32)],
        in_specs=[SMEM] + [VMEM] * 13 + [ANY] * blocks,
        out_specs=[VMEM] * 6,
        scratch_shapes=[pltpu.VMEM((width, inner), BF16), pltpu.SemaphoreType.DMA((blocks,))],
        compiler_params=params(),
        cost_estimate=cost(2 * length * width * inner, 16e6),
        name="middle",
    )(me, *x_parts, *g_parts, mix_t, gate_one, mul, add, gate_two, *pieces)


def spread_rows(me, value, stage, keep, send):
    blocks, rows = stage.shape[0], stage.shape[1]
    for j in range(blocks):
        stage[j] = value[j * rows : (j + 1) * rows, :].astype(BF16)
    for j in range(blocks):
        block = stage[me[0] ^ j]
        if j % 2 == 0:
            keep[j // 2] = block
        else:
            send[j // 2] = block


C_ROOT = 0.7978845608028654
C_CUBE = 0.044715


def feed_kernel(blocks, steps, first, me, *refs):
    (n_two, n_two_t, d_down, d_down_t, bias), refs = refs[:5], refs[5:]
    if not first:
        (down_in, d_n_in), refs = refs[:2], refs[2:]
    up_refs, down_refs, refs = refs[:blocks], refs[blocks : 2 * blocks], refs[2 * blocks :]
    outs = 5 + 2 * (blocks > 1)
    (down, d_n, d_bias, up_keep, dn_keep), sends = refs[:5], refs[5:outs]
    (w_buf, stage, sems) = refs[outs:]
    step = pl.program_id(0)
    rows = up_refs[0].shape[0]
    chunk = w_buf.shape[3]
    offset = 0 if first else steps * chunk

    def copies(s):
        out = []
        for m, group in enumerate((up_refs, down_refs)):
            for j, piece in enumerate(group):
                out.append(
                    pltpu.make_async_copy(
                        piece.at[:, pl.ds(offset + s * chunk, chunk)],
                        w_buf.at[m, s, pl.ds(row_at(me, j, rows), rows), :],
                        sems.at[m, s, j],
                    )
                )
        return out

    @pl.when(step == 0)
    def _():
        for s in range(steps):
            for copy in copies(s):
                copy.start()
        if first:
            down[...] = jnp.zeros_like(down)
            d_n[...] = jnp.zeros_like(d_n)
        else:
            down[...] = down_in[...]
            d_n[...] = d_n_in[...]

    for s in range(steps):

        @pl.when(step == s)
        def _():
            for copy in copies(s):
                copy.wait()

    w_up = w_buf[0, step]
    w_down_t = w_buf[1, step]
    h = dot_nn(n_two[...], w_up) + bias[0]
    square = h * h
    t = jnp.tanh(C_ROOT * h * (1.0 + C_CUBE * square))
    half = 0.5 + 0.5 * t
    act = (h * half).astype(BF16)
    slope = half + (0.5 * C_ROOT) * h * (1.0 - t * t) * (1.0 + (3.0 * C_CUBE) * square)
    d_h = (dot_nn(d_down[...], w_down_t) * slope).astype(BF16)
    d_bias[0] = jnp.sum(d_h.astype(F32), axis=0, keepdims=True)
    down[...] += dot_nt(act, w_down_t)
    d_n[...] += dot_nt(d_h, w_up)
    up_send, dn_send = sends if sends else (None, None)
    spread_rows(me, dot_nn(n_two_t[...], d_h), stage, up_keep, up_send)
    spread_rows(me, dot_nn(d_down_t[...], act), stage, dn_keep, dn_send)


def feed(me, n_two, n_two_t, d_down, d_down_t, bias, up_pieces, down_pieces, start, before, units):
    blocks = len(up_pieces)
    length, width = n_two.shape
    chunk = 512 if units % 512 == 0 else units
    steps = units // chunk
    first = before is None
    rows = up_pieces[0].shape[0]
    one = pl.Buffered(1)
    flat = pl.BlockSpec((length, width), lambda i: (0, 0), pipeline_mode=one)
    turned = pl.BlockSpec((width, length), lambda i: (0, 0), pipeline_mode=one)
    held = pl.BlockSpec((length, width), lambda i: (0, 0))
    half = max(blocks // 2, 1)
    grad = pl.BlockSpec((half, rows, chunk), lambda i: (0, 0, i))
    grads = 2 if blocks == 1 else 4
    bias_spec = pl.BlockSpec((1, 1, chunk), lambda i: (i + start // chunk, 0, 0))
    return pl.pallas_call(
        partial(feed_kernel, blocks, steps, first),
        grid=(steps,),
        in_specs=[SMEM, flat, turned, flat, turned, bias_spec]
        + ([] if first else [flat, flat])
        + [ANY] * (2 * blocks),
        out_specs=[held, held, pl.BlockSpec((1, 1, chunk), lambda i: (i, 0, 0))] + [grad] * grads,
        out_shape=[shape((length, width), F32)] * 2
        + [shape((steps, 1, chunk), F32)]
        + [shape((half, rows, units), BF16)] * grads,
        scratch_shapes=[
            pltpu.VMEM((2, steps, width, chunk), BF16),
            pltpu.VMEM((blocks, rows, chunk), BF16),
            pltpu.SemaphoreType.DMA((2, steps, blocks)),
        ],
        compiler_params=params(),
        cost_estimate=cost(12 * length * width * units, 20e6),
        name="feed",
    )(
        me,
        n_two,
        n_two_t,
        d_down,
        d_down_t,
        bias.reshape(-1, 1, chunk),
        *(() if first else before),
        *up_pieces,
        *down_pieces,
    )


def turn_kernel(blocks, me, *refs):
    x_refs, g_refs, refs = refs[:4], refs[4:8], refs[8:]
    (att, down, d_n, mix_t, gate_one, mul, gate_two, bias), refs = refs[:8], refs[8:]
    pieces, refs = refs[:blocks], refs[blocks:]
    outs = 9 + (blocks > 1)
    out_refs, (d_mid, d_mix, d_mix_t, sums, keep), sends = refs[:4], refs[4:9], refs[9:outs]
    (w_buf, d_att, stage, sems) = refs[outs:]
    copies = load_out_weight(me, pieces, w_buf, sems)
    part = x_refs[0].shape[0]
    totals = [jnp.zeros(gate_two.shape, F32) for _ in range(4)]
    for b in range(4):
        rows = slice(b * part, (b + 1) * part)
        g = g_refs[b][...].astype(F32)
        attention = att[rows, :]
        mid = x_refs[b][...].astype(F32) + gate_one[...] * attention
        branch = down[rows, :] + bias[...]
        out_refs[b][...] = (mid + gate_two[...] * branch).astype(BF16)
        centred = mid - jnp.mean(mid, axis=-1, keepdims=True)
        inverse = lax.rsqrt(jnp.mean(centred * centred, axis=-1, keepdims=True) + EPSILON)
        unit = centred * inverse
        dn = d_n[rows, :]
        dn_unit = dn * unit
        du = dn * mul[...]
        dm = g + inverse * (
            du
            - jnp.mean(du, axis=-1, keepdims=True)
            - unit * jnp.mean(dn_unit * mul[...], axis=-1, keepdims=True)
        )
        d_mid[rows, :] = dm
        d_att[rows, :] = (dm * gate_one[...]).astype(BF16)
        for n, term in enumerate((g * branch, dn_unit, dn, dm * attention)):
            totals[n] += jnp.sum(term, axis=0, keepdims=True)
    for n in range(4):
        sums[n : n + 1, :] = totals[n]
    for copy in copies:
        copy.wait()
    d_mix[...] = dot_nn(d_att[...], w_buf[...]).astype(BF16)
    d_mix_t[...] = d_mix[...].T
    grad = dot_nt(d_att[...].T, mix_t[...])
    spread_rows(me, grad, stage, keep, sends[0] if sends else None)


def turn(me, x_parts, g_parts, att, down, d_n, mix_t, gate_one, mul, gate_two, bias, pieces):
    blocks = len(pieces)
    part, width = x_parts[0].shape
    length = 4 * part
    inner = mix_t.shape[0]
    rows = pieces[0].shape[1]
    half = max(blocks // 2, 1)
    grads = 1 if blocks == 1 else 2
    return pl.pallas_call(
        partial(turn_kernel, blocks),
        out_shape=[shape((part, width), BF16)] * 4
        + [
            shape((length, width), F32),
            shape((length, inner), BF16),
            shape((inner, length), BF16),
            shape((4, width), F32),
        ]
        + [shape((half, rows, inner), BF16)] * grads,
        in_specs=[SMEM] + [VMEM] * 16 + [ANY] * blocks,
        out_specs=[VMEM] * (8 + grads),
        scratch_shapes=[
            pltpu.VMEM((width, inner), BF16),
            pltpu.VMEM((length, width), BF16),
            pltpu.VMEM((blocks, rows, inner), BF16),
            pltpu.SemaphoreType.DMA((blocks,)),
        ],
        compiler_params=params(),
        cost_estimate=cost(4 * length * width * inner, 24e6),
        name="turn",
    )(
        me, *x_parts, *g_parts, att, down, d_n, mix_t, gate_one, mul, gate_two, bias, *pieces
    )


def attend_back_kernel(
    q, k, v, d_mix, q_t, k_t, d_mix_t, mix_t, log_sum, doc_row, doc_col, cos_t, sin_t,
    dq_t, dk_t, dv_t, bias, dq_acc, dk_acc, dv_acc,
):
    @pl.when(pl.program_id(0) == 0)
    def _():
        same_doc_bias(bias, doc_row, doc_col)

    length = q.shape[0]
    block = 256 if length % 256 == 0 else length
    for h in range(2):
        rows = slice(h * HEAD, (h + 1) * HEAD)
        keys = head_mask(k, h)
        values = head_mask(v, h)
        row_dot = jnp.sum(
            d_mix_t[rows, :].astype(F32) * mix_t[rows, :].astype(F32), axis=0, keepdims=True
        )
        for b in range(length // block):
            c = slice(b * block, (b + 1) * block)
            probs = jnp.exp(dot_nt(keys, q[c, :]) + bias[:, c] - log_sum[0, h : h + 1, c])
            d_scores = (probs * (dot_nt(values, d_mix[c, :]) - row_dot[:, c])).astype(BF16)
            dv_part = dot_nt(d_mix_t[rows, c], probs.astype(BF16))
            dk_part = dot_nt(q_t[rows, c], d_scores)
            if b == 0:
                dv_acc[rows, :] = dv_part
                dk_acc[rows, :] = dk_part
            else:
                dv_acc[rows, :] += dv_part
                dk_acc[rows, :] += dk_part
            dq_acc[rows, c] = dot_nn(k_t[rows, :], d_scores)
    half = HEAD // 2
    for h in range(2):
        one = slice(h * HEAD, h * HEAD + half)
        two = slice(h * HEAD + half, (h + 1) * HEAD)
        for acc, out, factor in ((dq_acc, dq_t, HEAD**-0.5), (dk_acc, dk_t, 1.0)):
            a, b = acc[one, :] * factor, acc[two, :] * factor
            out[one, :] = (a * cos_t[...] + b * sin_t[...]).astype(BF16)
            out[two, :] = (b * cos_t[...] - a * sin_t[...]).astype(BF16)
    dv_t[...] = dv_acc[...].astype(BF16)


def attend_back(q, k, v, d_mix, q_t, k_t, d_mix_t, mix_t, log_sum, doc_row, doc_col, cos_t, sin_t, start, count):
    length, width = q.shape
    flat = pl.BlockSpec((length, PAIR), lambda i: (0, i + start))
    turned = pl.BlockSpec((PAIR, length), lambda i: (i + start, 0))
    out = pl.BlockSpec((PAIR, length), lambda i: (i, 0))
    fixed = lambda a: pl.BlockSpec(a.shape, lambda i: (0, 0))
    return pl.pallas_call(
        attend_back_kernel,
        grid=(count,),
        in_specs=[flat] * 4
        + [turned] * 4
        + [pl.BlockSpec((1, 2, length), lambda i: (i + start, 0, 0))]
        + [fixed(a) for a in (doc_row, doc_col, cos_t, sin_t)],
        out_specs=[out] * 3,
        out_shape=[shape((count * PAIR, length), BF16)] * 3,
        scratch_shapes=[pltpu.VMEM((length, length), F32)] + [pltpu.VMEM((PAIR, length), F32)] * 3,
        compiler_params=params(),
        cost_estimate=cost(28 * length * length * count * PAIR, 14e6 * count * PAIR / width),
        name="attend_back",
    )(q, k, v, d_mix, q_t, k_t, d_mix_t, mix_t, log_sum, doc_row, doc_col, cos_t, sin_t)


def first_kernel(blocks, me, *refs):
    x_refs, refs = refs[:4], refs[4:]
    (d_mid, mul, dq_t, dk_t, dv_t), refs = refs[:5], refs[5:]
    qk_refs, v_refs, refs = refs[:blocks], refs[blocks : 2 * blocks], refs[2 * blocks :]
    out_refs, (sums, w_buf, sems) = refs[:4], refs[4:]
    rows = qk_refs[0].shape[1]
    copies = []
    for j in range(blocks):
        at = row_at(me, j, rows)
        copies.append(
            pltpu.make_async_copy(qk_refs[j], w_buf.at[0:2, pl.ds(at, rows), :], sems.at[0, j])
        )
        copies.append(
            pltpu.make_async_copy(v_refs[j].at[0], w_buf.at[2, pl.ds(at, rows), :], sems.at[1, j])
        )
    for copy in copies:
        copy.start()
    for copy in copies:
        copy.wait()
    d_n_t = (
        dot_nn(w_buf[0], dq_t[...]) + dot_nn(w_buf[1], dk_t[...]) + dot_nn(w_buf[2], dv_t[...])
    )
    part = x_refs[0].shape[0]
    totals = [jnp.zeros(mul.shape, F32) for _ in range(2)]
    for b in range(4):
        r = slice(b * part, (b + 1) * part)
        dn = d_n_t[:, r].T
        x = x_refs[b][...].astype(F32)
        centred = x - jnp.mean(x, axis=-1, keepdims=True)
        inverse = lax.rsqrt(jnp.mean(centred * centred, axis=-1, keepdims=True) + EPSILON)
        unit = centred * inverse
        dn_unit = dn * unit
        du = dn * mul[...]
        out_refs[b][...] = (
            d_mid[r, :]
            + inverse
            * (
                du
                - jnp.mean(du, axis=-1, keepdims=True)
                - unit * jnp.mean(dn_unit * mul[...], axis=-1, keepdims=True)
            )
        ).astype(BF16)
        for n, term in enumerate((dn_unit, dn)):
            totals[n] += jnp.sum(term, axis=0, keepdims=True)
    for n in range(2):
        sums[n : n + 1, :] = totals[n]


def first(me, x_parts, d_mid, mul, dq_t, dk_t, dv_t, qk_pieces, v_pieces):
    blocks = len(qk_pieces)
    part, width = x_parts[0].shape
    length = 4 * part
    cols = dq_t.shape[0]
    return pl.pallas_call(
        partial(first_kernel, blocks),
        out_shape=[shape((part, width), BF16)] * 4 + [shape((2, width), F32)],
        in_specs=[SMEM] + [VMEM] * 9 + [ANY] * (2 * blocks),
        out_specs=[VMEM] * 5,
        scratch_shapes=[pltpu.VMEM((3, width, cols), BF16), pltpu.SemaphoreType.DMA((2, blocks))],
        compiler_params=params(),
        cost_estimate=cost(6 * length * width * cols, 20e6),
        name="first",
    )(me, *x_parts, d_mid, mul, dq_t, dk_t, dv_t, *qk_pieces, *v_pieces)


def qkv_grad_kernel(blocks, me, *refs):
    (n_t, dq_t, dk_t, dv_t), refs = refs[:4], refs[4:]
    outs = 1 + (blocks > 1)
    keep, sends, (stage,) = refs[0], refs[1:outs], refs[outs:]
    rows = stage.shape[1]
    for c, d_t in enumerate((dq_t, dk_t, dv_t)):
        grad = dot_nt(n_t[...], d_t[...])
        for j in range(blocks):
            stage[j] = grad[j * rows : (j + 1) * rows, :].astype(BF16)
        for j in range(blocks):
            block = stage[me[0] ^ j]
            if j % 2 == 0:
                keep[j // 2, c] = block
            else:
                sends[0][j // 2, c] = block


def qkv_grad(me, n_t, dq_t, dk_t, dv_t, blocks):
    width, length = n_t.shape
    cols = dq_t.shape[0]
    rows = width // blocks
    half = max(blocks // 2, 1)
    grads = 1 if blocks == 1 else 2
    return pl.pallas_call(
        partial(qkv_grad_kernel, blocks),
        out_shape=[shape((half, 3, rows, cols), BF16)] * grads,
        in_specs=[SMEM] + [VMEM] * 4,
        out_specs=[VMEM] * grads,
        scratch_shapes=[pltpu.VMEM((blocks, rows, cols), BF16)],
        compiler_params=params(),
        cost_estimate=cost(6 * length * width * cols, 10e6),
        name="qkv_grad",
    )(me, n_t, dq_t, dk_t, dv_t)


class Group:
    def __init__(self, dp_count, tensor_count, per_dp):
        self.dp, self.tensor, self.per_dp = dp_count, tensor_count, per_dp
        self.d, self.r = lax.axis_index("dp"), lax.axis_index("tensor")
        self.paired = dp_count == 8

    def bit(self, v, b):
        return lax.ppermute(v, "dp", [(i, i ^ (1 << b)) for i in range(self.dp)])

    def step(self, v, k):
        return lax.ppermute(v, "dp", [(i, i ^ k) for i in range(self.dp)])

    def z(self, v, k):
        return lax.ppermute(v, "tensor", [(i, i ^ k) for i in range(self.tensor)])

    def owns(self, d, r):
        return 0 <= r - d % 2 < self.per_dp

    def to_owner(self, rows, zero_idle):
        mine = self.r - self.d % 2
        top = self.per_dp - 1
        own = lax.dynamic_index_in_dim(rows, jnp.clip(mine, 0, top), 0, keepdims=False)
        if zero_idle:
            own = jnp.where((mine >= 0) & (mine <= top), own, jnp.zeros_like(own))
        parts = [own]
        for k in range(1, self.tensor):
            want = (self.r ^ k) - self.d % 2
            sent = lax.dynamic_index_in_dim(rows, jnp.clip(want, 0, top), 0, keepdims=False)
            pairs = [
                (d * self.tensor + r, d * self.tensor + (r ^ k))
                for d in range(self.dp)
                for r in range(self.tensor)
                if self.owns(d, r ^ k)
            ]
            parts.append(lax.ppermute(sent, BOTH, pairs))
        return parts

    def from_owner(self, parts):
        came = [parts[0]]
        for k in range(1, self.tensor):
            pairs = [
                (d * self.tensor + r, d * self.tensor + (r ^ k))
                for d in range(self.dp)
                for r in range(self.tensor)
                if self.owns(d, r)
            ]
            came.append(lax.ppermute(parts[k], BOTH, pairs))
        stack = jnp.stack(came)
        return jnp.stack(
            [
                lax.dynamic_index_in_dim(stack, self.r ^ (j + self.d % 2), 0, keepdims=False)
                for j in range(self.per_dp)
            ]
        )

    def z_join(self, v):
        return jnp.concatenate([v] + [self.z(v, k) for k in range(1, self.tensor)], axis=-1)

    def gather(self, v, order):
        if not self.paired:
            return [lax.all_gather(v, "dp", axis=v.ndim - 2, tiled=True)]
        held = {0: v}
        for b in order:
            held |= {j ^ (1 << b): self.bit(p, b) for j, p in held.items()}
        return [held[j] for j in range(self.dp)]

    def reduce(self, keep, *more):
        if not self.paired:
            value = keep[0].astype(F32)
            return lax.psum_scatter(value, "dp", scatter_dimension=value.ndim - 2, tiled=True)
        send, order = more
        got = self.bit(send, 0)
        total = {2 * j: keep[j].astype(F32) + got[j].astype(F32) for j in range(self.dp // 2)}
        for b in order:
            step = 1 << b
            out = {j: p.astype(BF16) for j, p in total.items() if j & step}
            total = {
                j: p + self.bit(out[j ^ step], b).astype(F32)
                for j, p in total.items()
                if not j & step
            }
        return total[0]

    def reduce_two(self, one, two, *sends):
        if not self.paired:
            return self.reduce(one), self.reduce(two)
        return self.reduce(one, sends[0], (1, 2)), self.reduce(two, sends[1], (2, 1))

    def z_reduce(self, v):
        size = v.shape[-1] // self.tensor
        total = v[..., :size]
        for k in range(1, self.tensor):
            out = v[..., k * size : (k + 1) * size].astype(BF16)
            total = total + self.z(out, k).astype(F32)
        return total

    def small_gather(self, v):
        if not self.paired:
            return lax.all_gather(v, "dp", axis=0)
        stack = jnp.stack([v] + [self.step(v, k) for k in range(1, self.dp)])
        return jnp.take(stack, self.d ^ jnp.arange(self.dp), axis=0)

    def small_swap(self, v):
        if not self.paired:
            return lax.all_to_all(v, "dp", split_axis=0, concat_axis=0, tiled=True)
        relative = jnp.take(v, self.d ^ jnp.arange(self.dp), axis=0)
        stack = jnp.stack(
            [relative[0]] + [self.step(relative[k], k) for k in range(1, self.dp)]
        )
        return jnp.take(stack, self.d ^ jnp.arange(self.dp), axis=0)


def silu_slope(c):
    sig = jax.nn.sigmoid(c)
    return sig * (1.0 + c * (1.0 - sig))


def shards(
    inputs, condition, doc_ids, positions, w_qkv, w_out, w_up, bias_up, w_down, bias_down,
    gain_one, gain_two, w_ada, bias_ada, out_grad,
):
    dp_count = lax.axis_size("dp")
    tensor_count = lax.axis_size("tensor")
    per_dp, part, width = inputs.shape
    length = doc_ids.shape[1]
    rows = w_up.shape[0]
    group = Group(dp_count, tensor_count, per_dp)
    blocks = dp_count if group.paired else 1
    d, r = group.d, group.r
    me = jnp.where(group.paired, d, 0).astype(jnp.int32).reshape(1)
    mine = jnp.clip(r - d % 2, 0, per_dp - 1)

    early = jnp.concatenate([w_qkv, w_out.T[None]], axis=0)
    late = jnp.stack([w_up, w_down.T])
    early = group.z_join(early)
    x_parts = group.to_owner(inputs, False)
    late = group.z_join(late)
    g_parts = group.to_owner(out_grad, True)
    qk_pieces = group.gather(early[:2], (1, 2, 0))
    v_pieces = group.gather(early[2:], (2, 1, 0))
    up_pieces = group.gather(late[0], (1, 2, 0))
    down_pieces = group.gather(late[1], (2, 1, 0))

    cond_size = condition.shape[1]
    pad = lambda v: jnp.pad(v, ((0, 0), (0, cond_size - v.shape[1])))
    small = jnp.concatenate(
        [pad(bias_up), pad(bias_down[None]), pad(gain_one[None]), pad(gain_two[None]), condition]
    )
    small = group.small_gather(small)
    whole = lambda i: small[:, i, :rows].reshape(1, width)
    bias_hidden = group.z_join(whole(0)).astype(F32)
    bias_out, gain_1, gain_2 = (whole(i).astype(F32) for i in (1, 2, 3))
    cond_all = small[:, 4:, :].astype(F32)
    act_all = jax.nn.silu(cond_all)
    mod_part = (
        jnp.dot(
            act_all.reshape(-1, cond_size),
            w_ada.astype(F32),
            precision=PRECISE,
            preferred_element_type=F32,
        )
        + bias_ada.astype(F32)
    ).reshape(dp_count, per_dp, -1)
    wanted = jnp.clip(r - jnp.arange(dp_count) % 2, 0, per_dp - 1)
    modulation = group.small_swap(mod_part[jnp.arange(dp_count), wanted])
    shift_1, scale_1, gate_1, shift_2, scale_2, gate_2 = modulation.reshape(6, 1, width)
    mul_1 = gain_1 * (1.0 + scale_1)
    mul_2 = gain_2 * (1.0 + scale_2)

    order = r ^ jnp.arange(tensor_count)
    mixed = lambda v: lax.dynamic_index_in_dim(v, mine, 0, keepdims=False).reshape(
        tensor_count, part
    )[order].reshape(-1)
    docs, places = mixed(doc_ids), mixed(positions)
    doc_row, doc_col = docs[None, :], docs[:, None]
    frequencies = 10000.0 ** (-2.0 * jnp.arange(HEAD // 2, dtype=F32) / HEAD)
    turned = places.astype(F32)[:, None] * frequencies[None, :]
    cosine, sine = jnp.cos(turned), jnp.sin(turned)
    nothing = jnp.zeros_like(sine)
    cos_flat = jnp.concatenate([cosine] * 4, axis=1)
    sin_a = jnp.concatenate([-sine, nothing] * 2, axis=1)
    sin_b = jnp.concatenate([nothing, sine] * 2, axis=1)
    cos_t, sin_t = cosine.T, sine.T

    n_t, q, k, v, q_t, k_t, v_t = qkv(
        me, x_parts, mul_1, shift_1, cos_flat, sin_a, sin_b, qk_pieces, v_pieces
    )
    mix_t, log_sum = attend(q, k, v_t, doc_row, doc_col)
    att, n_two, n_two_t, d_down, d_down_t, d_bias_down = middle(
        me, x_parts, g_parts, mix_t, gate_1, mul_2, shift_2, gate_2, v_pieces
    )
    units = w_up.shape[1] * tensor_count // 2
    feed_args = (me, n_two, n_two_t, d_down, d_down_t, bias_hidden, up_pieces, down_pieces)
    down_a, d_n_a, d_bias_a, *grads_a = feed(*feed_args, 0, None, units)
    down, d_n, d_bias_b, *grads_b = feed(*feed_args, units, (down_a, d_n_a), units)

    up_a, dn_a = group.reduce_two(*grads_a)
    up_b, dn_b = group.reduce_two(*grads_b)

    *out_parts, d_mid, d_mix, d_mix_t, sums = (
        turned_back := turn(
            me, x_parts, g_parts, att, down, d_n, mix_t, gate_1, mul_2, gate_2, bias_out, v_pieces
        )
    )[:8]
    out_sum = group.reduce(*turned_back[8:], (1, 2))
    block_out = group.from_owner(out_parts)

    pairs = q.shape[1] // PAIR
    dq_t, dk_t, dv_t = attend_back(
        q, k, v, d_mix, q_t, k_t, d_mix_t, mix_t, log_sum, doc_row, doc_col, cos_t, sin_t, 0, pairs
    )
    qkv_sum = group.reduce(*qkv_grad(me, n_t, dq_t, dk_t, dv_t, blocks), (2, 1))
    *in_parts, sums_one = first(
        me, x_parts, d_mid, mul_1, dq_t, dk_t, dv_t, qk_pieces, v_pieces
    )
    input_grad = group.from_owner(in_parts)

    grad_qkv = group.z_reduce(qkv_sum)
    grad_out = group.z_reduce(out_sum).T
    grad_up = group.z_reduce(jnp.concatenate([up_a, up_b], axis=-1))
    grad_down = group.z_reduce(jnp.concatenate([dn_a, dn_b], axis=-1)).T

    d_gate_2, norm_2, d_shift_2, d_gate_1 = (sums[n : n + 1] for n in range(4))
    norm_1, d_shift_1 = (sums_one[n : n + 1] for n in range(2))
    d_modulation = jnp.concatenate(
        [d_shift_1, norm_1 * gain_1, d_gate_1, d_shift_2, norm_2 * gain_2, d_gate_2], axis=1
    )
    d_hidden_bias = jnp.concatenate([d_bias_a.reshape(-1), d_bias_b.reshape(-1)])
    sliced = lambda t: t.reshape(dp_count, -1)
    payload = jnp.concatenate(
        [
            sliced(d_modulation),
            sliced(norm_1 * (1.0 + scale_1)),
            sliced(norm_2 * (1.0 + scale_2)),
            sliced(d_bias_down),
            d_hidden_bias.reshape(tensor_count, dp_count, rows)
            .transpose(1, 0, 2)
            .reshape(dp_count, -1),
        ],
        axis=1,
    )
    payload = group.small_swap(payload)
    relative = [payload] + [group.z(payload, k) for k in range(1, tensor_count)]
    mod_width = w_ada.shape[1]
    base = mod_width + 3 * rows
    grad_bias_up = sum(
        jnp.sum(p[:, base + k * rows : base + (k + 1) * rows], axis=0, keepdims=True)
        for k, p in enumerate(relative)
    )
    every = jnp.stack([p[:, :base] for p in relative])[order]
    d_mod_all = every[:, :, :mod_width]
    gains = jnp.sum(every[:, :, mod_width:], axis=(0, 1))
    grad_gain_one, grad_gain_two, grad_bias_down = (
        gains[n * rows : (n + 1) * rows] for n in range(3)
    )
    grad_bias_ada = jnp.sum(d_mod_all, axis=(0, 1))
    grid = np.arange(tensor_count)[:, None] - np.arange(dp_count)[None, :] % 2
    act_used = act_all[np.arange(dp_count)[None, :], np.clip(grid, 0, per_dp - 1)]
    flat_mod = d_mod_all.reshape(tensor_count * dp_count, mod_width)
    grad_ada = lax.dot_general(
        act_used.reshape(tensor_count * dp_count, cond_size),
        flat_mod,
        (((0,), (0,)), ((), ())),
        precision=PRECISE,
        preferred_element_type=F32,
    )
    d_act = lax.dot_general(
        flat_mod,
        w_ada.astype(F32),
        (((1,), (1,)), ((), ())),
        precision=PRECISE,
        preferred_element_type=F32,
    ).reshape(tensor_count, dp_count, cond_size)
    owner = np.arange(per_dp)[None, :] + np.arange(dp_count)[:, None] % 2
    d_act = d_act[owner, np.arange(dp_count)[:, None]]
    d_act = jnp.sum(group.small_swap(d_act), axis=0)
    cond_grad = d_act * silu_slope(condition.astype(F32))
    return (
        block_out,
        input_grad,
        cond_grad,
        grad_qkv,
        grad_out,
        grad_up,
        grad_bias_up,
        grad_down,
        grad_bias_down,
        grad_gain_one,
        grad_gain_two,
        grad_ada,
        grad_bias_ada,
    )


def solution(mesh):
    return jax.shard_map(
        shards,
        mesh=mesh,
        in_specs=(
            P("dp", "tensor", None),
            P("dp", None),
            P("dp", None),
            P("dp", None),
            P(None, "dp", "tensor"),
            P("tensor", "dp"),
            P("dp", "tensor"),
            P("tensor", "dp"),
            P("tensor", "dp"),
            P("dp"),
            P("dp"),
            P("dp"),
            P(None, "dp"),
            P("dp"),
            P("dp", "tensor", None),
        ),
        out_specs=(
            P("dp", "tensor", None),
            P("dp", "tensor", None),
            P("dp", None),
            P(None, "dp", "tensor"),
            P("tensor", "dp"),
            P("dp", "tensor"),
            P("tensor", "dp"),
            P("tensor", "dp"),
            P("dp"),
            P("dp"),
            P("dp"),
            P(None, "dp"),
            P("dp"),
        ),
        check_vma=False,
    )
```

```python
from functools import partial

import jax
import jax.numpy as jnp
import numpy as np
from jax import lax
from jax.experimental import pallas as pl
from jax.experimental.pallas import tpu as pltpu
from jax.sharding import PartitionSpec as P

HEAD = 64
PRECISE = lax.Precision.HIGHEST
EPSILON = 1e-05
SHIFT_1, SCALE_1, GATE_1, SHIFT_2, SCALE_2, GATE_2, BIAS_OUT, GAIN_1, GAIN_2 = range(9)
F32 = jnp.float32
BF16 = jnp.bfloat16
PAIR = 2 * HEAD
BOTH = ("dp", "tensor")
ANY = pl.BlockSpec(memory_space=pl.ANY)
VMEM = pl.BlockSpec(memory_space=pltpu.VMEM)
SMEM = pl.BlockSpec(memory_space=pltpu.SMEM)


def dot_nn(a, b):
    return jnp.dot(a, b, preferred_element_type=F32)


def dot_nt(a, b):
    return lax.dot_general(a, b, (((1,), (1,)), ((), ())), preferred_element_type=F32)


def params(**more):
    return pltpu.CompilerParams(vmem_limit_bytes=58 << 20, **more)


def cost(flops, nbytes, trans=0):
    return pl.CostEstimate(flops=int(flops), bytes_accessed=int(nbytes), transcendentals=int(trans))


def shape(dims, kind):
    return jax.ShapeDtypeStruct(tuple(dims), kind)


def row_at(me_ref, index, rows):
    return pl.multiple_of((me_ref[0] ^ index) * rows, rows)


def vec_row(vec, n):
    return vec[n : n + 1, :]


def norm_scale(vec, gain, scale):
    return vec_row(vec, gain) * (1.0 + vec_row(vec, scale))


class Held:
    def __init__(self, parts, rels):
        self.parts, self.rels = parts, rels

    def blocks(self, refs):
        n = 0
        for ref, rel in zip(refs, self.rels):
            for i, j in enumerate(rel):
                yield ref.at[i], j, n
                n += 1

    @property
    def count(self):
        return sum(len(rel) for rel in self.rels)


def qkv_copies(me, qk, vo, refs, w_buf, sems, rows):
    out = []
    parts = len(qk.parts)
    for held, group, planes in ((qk, refs[:parts], (0, 1)), (vo, refs[parts:], (2,))):
        for block, j, n in held.blocks(group):
            for c, plane in enumerate(planes):
                out.append(
                    pltpu.make_async_copy(
                        block.at[pl.ds(c * rows, rows), :],
                        w_buf.at[plane, pl.ds(row_at(me, j, rows), rows), :],
                        sems.at[plane, n],
                    )
                )
    return out


def qkv_kernel(qk, vo, me, *refs):
    x_refs, refs = refs[:4], refs[4:]
    (vec, cosine, sin_a, sin_b), refs = refs[:4], refs[4:]
    mul, add = norm_scale(vec, GAIN_1, SCALE_1), vec_row(vec, SHIFT_1)
    held, refs = refs[: 2 * len(qk.parts)], refs[2 * len(qk.parts) :]
    (n_t, q_out, k_out, v_out, q_t, k_t, v_t), (w_buf, n_buf, sems) = refs[:7], refs[7:]
    copies = qkv_copies(me, qk, vo, held, w_buf, sems, w_buf.shape[1] // qk.count)
    for copy in copies:
        copy.start()
    part = x_refs[0].shape[0]
    for b, x_ref in enumerate(x_refs):
        x = x_ref[...].astype(F32)
        centred = x - jnp.mean(x, axis=-1, keepdims=True)
        spread = jnp.mean(centred * centred, axis=-1, keepdims=True)
        n_buf[b * part : (b + 1) * part, :] = (
            centred * lax.rsqrt(spread + EPSILON) * mul + add
        ).astype(BF16)
    normed = n_buf[...]
    n_t[...] = normed.T
    for copy in copies:
        copy.wait()
    width = q_out.shape[1]
    for c, (flat, turned, factor) in enumerate(((q_out, q_t, HEAD**-0.5), (k_out, k_t, 1.0))):
        proj = dot_nn(normed, w_buf[c])
        for p in range(width // PAIR):
            lanes = slice(p * PAIR, (p + 1) * PAIR)
            r = proj[:, lanes]
            spun = (
                r * cosine[...]
                + pltpu.roll(r, PAIR - HEAD // 2, 1) * sin_a[...]
                + pltpu.roll(r, HEAD // 2, 1) * sin_b[...]
            )
            spun = spun.astype(BF16) * BF16(factor)
            flat[:, lanes] = spun
            turned[lanes, :] = spun.T
    values = dot_nn(normed, w_buf[2]).astype(BF16)
    v_out[...] = values
    v_t[...] = values.T


def qkv(me, x_parts, vec, cosine, sin_a, sin_b, qk, vo):
    part, width = x_parts[0].shape
    length = 4 * part
    cols = qk.parts[0].shape[2]
    flat, turned = shape((length, cols), BF16), shape((cols, length), BF16)
    return pl.pallas_call(
        partial(qkv_kernel, qk, vo),
        out_shape=[shape((width, length), BF16), flat, flat, flat, turned, turned, turned],
        in_specs=[SMEM] + [VMEM] * 8 + [ANY] * (2 * len(qk.parts)),
        out_specs=[VMEM] * 7,
        scratch_shapes=[
            pltpu.VMEM((3, width, cols), BF16),
            pltpu.VMEM((length, width), BF16),
            pltpu.SemaphoreType.DMA((3, qk.count)),
        ],
        compiler_params=params(),
        cost_estimate=cost(6 * length * width * cols, 16e6),
        name="qkv",
    )(me, *x_parts, vec, cosine, sin_a, sin_b, *qk.parts, *vo.parts)


def head_mask(ref, head):
    lane = lax.broadcasted_iota(jnp.int32, (1, PAIR), 1)
    return jnp.where((lane // HEAD) == head, ref[...], jnp.zeros((), BF16))


def same_doc_bias(bias, doc_row, doc_col):
    bias[...] = jnp.where(doc_col[...] == doc_row[...], 0.0, -1e30)


def attend_kernel(q, k, v_t, doc_row, doc_col, mix_t, log_sum, bias):
    @pl.when(pl.program_id(0) == 0)
    def _():
        same_doc_bias(bias, doc_row, doc_col)

    for h in range(2):
        rows = slice(h * HEAD, (h + 1) * HEAD)
        scores = dot_nt(head_mask(k, h), q[...]) + bias[...]
        top = jnp.max(scores, axis=0, keepdims=True)
        weights = jnp.exp(scores - top)
        total = jnp.sum(weights, axis=0, keepdims=True)
        mixed = dot_nn(v_t[rows, :], weights.astype(BF16))
        mix_t[rows, :] = (mixed / total).astype(BF16)
        log_sum[0, h : h + 1, :] = top + jnp.log(total)


def attend(q, k, v_t, doc_row, doc_col):
    length, width = q.shape
    pairs = width // PAIR
    flat = pl.BlockSpec((length, PAIR), lambda i: (0, i))
    turned = pl.BlockSpec((PAIR, length), lambda i: (i, 0))
    return pl.pallas_call(
        attend_kernel,
        grid=(pairs,),
        in_specs=[
            flat,
            flat,
            turned,
            pl.BlockSpec((1, length), lambda i: (0, 0)),
            pl.BlockSpec((length, 1), lambda i: (0, 0)),
        ],
        out_specs=[turned, pl.BlockSpec((1, 2, length), lambda i: (i, 0, 0))],
        out_shape=[shape((width, length), BF16), shape((pairs, 2, length), F32)],
        scratch_shapes=[pltpu.VMEM((length, length), F32)],
        compiler_params=params(),
        cost_estimate=cost(16 * length * length * width, 8e6),
        name="attend",
    )(q, k, v_t, doc_row, doc_col)


def load_out_weight(me, vo, refs, buf, sems):
    rows = buf.shape[0] // vo.count
    copies = [
        pltpu.make_async_copy(
            block.at[pl.ds(rows, rows), :], buf.at[pl.ds(row_at(me, j, rows), rows), :], sems.at[n]
        )
        for block, j, n in vo.blocks(refs)
    ]
    for copy in copies:
        copy.start()
    return copies


def middle_kernel(vo, me, *refs):
    x_refs, g_refs, refs = refs[:4], refs[4:8], refs[8:]
    (mix_t, vec), refs = refs[:2], refs[2:]
    mul, add = norm_scale(vec, GAIN_2, SCALE_2), vec_row(vec, SHIFT_2)
    gate_one, gate_two = vec_row(vec, GATE_1), vec_row(vec, GATE_2)
    pieces, refs = refs[: len(vo.parts)], refs[len(vo.parts) :]
    (att, n_two, n_two_t, d_down, d_down_t, d_bias), (w_buf, sems) = refs[:6], refs[6:]
    copies = load_out_weight(me, vo, pieces, w_buf, sems)
    part = x_refs[0].shape[0]
    total = jnp.zeros(gate_two.shape, F32)
    for b, g_ref in enumerate(g_refs):
        scaled = g_ref[...].astype(F32) * gate_two
        total += jnp.sum(scaled, axis=0, keepdims=True)
        d_down[b * part : (b + 1) * part, :] = scaled.astype(BF16)
    d_bias[...] = total
    d_down_t[...] = d_down[...].T
    mixture = mix_t[...].T
    for copy in copies:
        copy.wait()
    for b, x_ref in enumerate(x_refs):
        rows = slice(b * part, (b + 1) * part)
        attention = dot_nt(mixture[rows, :], w_buf[...])
        att[rows, :] = attention
        mid = x_ref[...].astype(F32) + gate_one * attention
        centred = mid - jnp.mean(mid, axis=-1, keepdims=True)
        spread = jnp.mean(centred * centred, axis=-1, keepdims=True)
        n_two[rows, :] = (
            centred * lax.rsqrt(spread + EPSILON) * mul + add
        ).astype(BF16)
    n_two_t[...] = n_two[...].T


def middle(me, x_parts, g_parts, mix_t, vec, vo):
    part, width = x_parts[0].shape
    length = 4 * part
    inner = mix_t.shape[0]
    flat, turned = shape((length, width), BF16), shape((width, length), BF16)
    return pl.pallas_call(
        partial(middle_kernel, vo),
        out_shape=[shape((length, width), F32), flat, turned, flat, turned, shape((1, width), F32)],
        in_specs=[SMEM] + [VMEM] * 10 + [ANY] * len(vo.parts),
        out_specs=[VMEM] * 6,
        scratch_shapes=[pltpu.VMEM((width, inner), BF16), pltpu.SemaphoreType.DMA((vo.count,))],
        compiler_params=params(),
        cost_estimate=cost(2 * length * width * inner, 16e6),
        name="middle",
    )(me, *x_parts, *g_parts, mix_t, vec, *vo.parts)


def spread_rows(me, value, stage, keep, send=None):
    blocks, rows = stage.shape[0], stage.shape[1]
    for j in range(blocks):
        stage[j] = value[j * rows : (j + 1) * rows, :].astype(BF16)
    for j in range(blocks):
        block = stage[me[0] ^ j]
        if j % 2 == 0:
            keep(j // 2, block)
        else:
            send(j // 2, block)


def writer(ref, *lead):
    def put(slot, block):
        ref[(lead[0], slot, *lead[1:])] = block

    return put


def split_writer(ref, *lead):
    def put(slot, block):
        half = block.shape[-1] // 2
        for s in range(2):
            ref[(s, slot, *lead)] = block[:, s * half : (s + 1) * half]

    return put


C_ROOT = 0.7978845608028654
C_CUBE = 0.044715


def feed_kernel(up, dn, steps, first, me, *refs):
    (n_two, n_two_t, d_down, d_down_t, bias), refs = refs[:5], refs[5:]
    if not first:
        (down_in, d_n_in), refs = refs[:2], refs[2:]
    parts = len(up.parts)
    up_refs, down_refs, refs = refs[:parts], refs[parts : 2 * parts], refs[2 * parts :]
    (down, d_n, d_bias, *grads), (w_buf, stage, sems) = refs[:-3], refs[-3:]
    step = pl.program_id(0)
    rows = up_refs[0].shape[1]
    chunk = w_buf.shape[3]
    offset = 0 if first else steps * chunk

    def copies(s):
        out = []
        for m, (held, group) in enumerate(((up, up_refs), (dn, down_refs))):
            for block, j, n in held.blocks(group):
                out.append(
                    pltpu.make_async_copy(
                        block.at[:, pl.ds(offset + s * chunk, chunk)],
                        w_buf.at[m, s, pl.ds(row_at(me, j, rows), rows), :],
                        sems.at[m, s, n],
                    )
                )
        return out

    @pl.when(step == 0)
    def _():
        for s in range(steps):
            for copy in copies(s):
                copy.start()
        if first:
            down[...] = jnp.zeros_like(down)
            d_n[...] = jnp.zeros_like(d_n)
        else:
            down[...] = down_in[...]
            d_n[...] = d_n_in[...]

    for s in range(steps):

        @pl.when(step == s)
        def _():
            for copy in copies(s):
                copy.wait()

    w_up = w_buf[0, step]
    w_down_t = w_buf[1, step]
    h = dot_nn(n_two[...], w_up) + bias[0]
    square = h * h
    t = jnp.tanh(C_ROOT * h * (1.0 + C_CUBE * square))
    half = 0.5 + 0.5 * t
    act = (h * half).astype(BF16)
    slope = half + (0.5 * C_ROOT) * h * (1.0 - t * t) * (1.0 + (3.0 * C_CUBE) * square)
    d_h = (dot_nn(d_down[...], w_down_t) * slope).astype(BF16)
    d_bias[0] = jnp.sum(d_h.astype(F32), axis=0, keepdims=True)
    down[...] += dot_nt(act, w_down_t)
    d_n[...] += dot_nt(d_h, w_up)
    for m, grad in ((0, dot_nn(n_two_t[...], d_h)), (1, dot_nn(d_down_t[...], act))):
        spread_rows(me, grad, stage, *(writer(ref, m) for ref in grads))


def feed(me, n_two, n_two_t, d_down, d_down_t, bias, up, dn, start, before, units):
    blocks = up.count
    length, width = n_two.shape
    chunk = 512 if units % 512 == 0 else units
    steps = units // chunk
    first = before is None
    rows = width // blocks
    one = pl.Buffered(1)
    flat = pl.BlockSpec((length, width), lambda i: (0, 0), pipeline_mode=one)
    turned = pl.BlockSpec((width, length), lambda i: (0, 0), pipeline_mode=one)
    held = pl.BlockSpec((length, width), lambda i: (0, 0))
    half = max(blocks // 2, 1)
    grad = pl.BlockSpec((2, half, rows, chunk), lambda i: (0, 0, 0, i))
    grads = 1 if blocks == 1 else 2
    bias_spec = pl.BlockSpec((1, 1, chunk), lambda i: (i + start // chunk, 0, 0))
    return pl.pallas_call(
        partial(feed_kernel, up, dn, steps, first),
        grid=(steps,),
        in_specs=[SMEM, flat, turned, flat, turned, bias_spec]
        + ([] if first else [flat, flat])
        + [ANY] * (2 * len(up.parts)),
        out_specs=[held, held, pl.BlockSpec((1, 1, chunk), lambda i: (i, 0, 0))] + [grad] * grads,
        out_shape=[shape((length, width), F32)] * 2
        + [shape((steps, 1, chunk), F32)]
        + [shape((2, half, rows, units), BF16)] * grads,
        scratch_shapes=[
            pltpu.VMEM((2, steps, width, chunk), BF16),
            pltpu.VMEM((blocks, rows, chunk), BF16),
            pltpu.SemaphoreType.DMA((2, steps, blocks)),
        ],
        compiler_params=params(),
        cost_estimate=cost(12 * length * width * units, 20e6),
        name="feed",
    )(
        me,
        n_two,
        n_two_t,
        d_down,
        d_down_t,
        bias.reshape(-1, 1, chunk),
        *(() if first else before),
        *up.parts,
        *dn.parts,
    )


def turn_kernel(vo, me, *refs):
    x_refs, g_refs, refs = refs[:4], refs[4:8], refs[8:]
    (att, down, d_n, mix_t, vec), refs = refs[:5], refs[5:]
    mul, bias = norm_scale(vec, GAIN_2, SCALE_2), vec_row(vec, BIAS_OUT)
    gate_one, gate_two = vec_row(vec, GATE_1), vec_row(vec, GATE_2)
    pieces, refs = refs[: len(vo.parts)], refs[len(vo.parts) :]
    out_refs, (d_mid, d_mix, d_mix_t, sums, d_att_t), (w_buf, d_att, sems) = (
        refs[:4],
        refs[4:9],
        refs[9:],
    )
    copies = load_out_weight(me, vo, pieces, w_buf, sems)
    part = x_refs[0].shape[0]
    totals = [jnp.zeros(gate_two.shape, F32) for _ in range(4)]
    for b in range(4):
        rows = slice(b * part, (b + 1) * part)
        g = g_refs[b][...].astype(F32)
        attention = att[rows, :]
        mid = x_refs[b][...].astype(F32) + gate_one * attention
        branch = down[rows, :] + bias
        out_refs[b][...] = (mid + gate_two * branch).astype(BF16)
        centred = mid - jnp.mean(mid, axis=-1, keepdims=True)
        inverse = lax.rsqrt(jnp.mean(centred * centred, axis=-1, keepdims=True) + EPSILON)
        unit = centred * inverse
        dn = d_n[rows, :]
        dn_unit = dn * unit
        du = dn * mul
        dm = g + inverse * (
            du
            - jnp.mean(du, axis=-1, keepdims=True)
            - unit * jnp.mean(dn_unit * mul, axis=-1, keepdims=True)
        )
        d_mid[rows, :] = dm
        d_att[rows, :] = (dm * gate_one).astype(BF16)
        for n, term in enumerate((g * branch, dn_unit, dn, dm * attention)):
            totals[n] += jnp.sum(term, axis=0, keepdims=True)
    for n in range(4):
        sums[n : n + 1, :] = totals[n]
    for copy in copies:
        copy.wait()
    d_mix[...] = dot_nn(d_att[...], w_buf[...]).astype(BF16)
    d_mix_t[...] = d_mix[...].T
    d_att_t[...] = d_att[...].T


def turn(me, x_parts, g_parts, att, down, d_n, mix_t, vec, vo):
    part, width = x_parts[0].shape
    length = 4 * part
    inner = mix_t.shape[0]
    return pl.pallas_call(
        partial(turn_kernel, vo),
        out_shape=[shape((part, width), BF16)] * 4
        + [
            shape((length, width), F32),
            shape((length, inner), BF16),
            shape((inner, length), BF16),
            shape((4, width), F32),
            shape((width, length), BF16),
        ],
        in_specs=[SMEM] + [VMEM] * 13 + [ANY] * len(vo.parts),
        out_specs=[VMEM] * 9,
        scratch_shapes=[
            pltpu.VMEM((width, inner), BF16),
            pltpu.VMEM((length, width), BF16),
            pltpu.SemaphoreType.DMA((vo.count,)),
        ],
        compiler_params=params(),
        cost_estimate=cost(2 * length * width * inner, 24e6),
        name="turn",
    )(
        me, *x_parts, *g_parts, att, down, d_n, mix_t, vec, *vo.parts
    )


def attend_back_kernel(
    q, k, v, d_mix, q_t, k_t, d_mix_t, mix_t, log_sum, doc_row, doc_col, cos_t, sin_t,
    dq_t, dk_t, dv_t, bias, dq_acc, dk_acc, dv_acc,
):
    @pl.when(pl.program_id(0) == 0)
    def _():
        same_doc_bias(bias, doc_row, doc_col)

    length = q.shape[0]
    block = 256 if length % 256 == 0 else length
    for h in range(2):
        rows = slice(h * HEAD, (h + 1) * HEAD)
        keys = head_mask(k, h)
        values = head_mask(v, h)
        row_dot = jnp.sum(
            d_mix_t[rows, :].astype(F32) * mix_t[rows, :].astype(F32), axis=0, keepdims=True
        )
        for b in range(length // block):
            c = slice(b * block, (b + 1) * block)
            probs = jnp.exp(dot_nt(keys, q[c, :]) + bias[:, c] - log_sum[0, h : h + 1, c])
            d_scores = (probs * (dot_nt(values, d_mix[c, :]) - row_dot[:, c])).astype(BF16)
            dv_part = dot_nt(d_mix_t[rows, c], probs.astype(BF16))
            dk_part = dot_nt(q_t[rows, c], d_scores)
            if b == 0:
                dv_acc[rows, :] = dv_part
                dk_acc[rows, :] = dk_part
            else:
                dv_acc[rows, :] += dv_part
                dk_acc[rows, :] += dk_part
            dq_acc[rows, c] = dot_nn(k_t[rows, :], d_scores)
    half = HEAD // 2
    for h in range(2):
        one = slice(h * HEAD, h * HEAD + half)
        two = slice(h * HEAD + half, (h + 1) * HEAD)
        for acc, out, factor in ((dq_acc, dq_t, HEAD**-0.5), (dk_acc, dk_t, 1.0)):
            a, b = acc[one, :] * factor, acc[two, :] * factor
            out[one, :] = (a * cos_t[...] + b * sin_t[...]).astype(BF16)
            out[two, :] = (b * cos_t[...] - a * sin_t[...]).astype(BF16)
    dv_t[...] = dv_acc[...].astype(BF16)


def attend_back(q, k, v, d_mix, q_t, k_t, d_mix_t, mix_t, log_sum, doc_row, doc_col, cos_t, sin_t, start, count):
    length, width = q.shape
    flat = pl.BlockSpec((length, PAIR), lambda i: (0, i + start))
    turned = pl.BlockSpec((PAIR, length), lambda i: (i + start, 0))
    out = pl.BlockSpec((PAIR, length), lambda i: (i, 0))
    fixed = lambda a: pl.BlockSpec(a.shape, lambda i: (0, 0))
    return pl.pallas_call(
        attend_back_kernel,
        grid=(count,),
        in_specs=[flat] * 4
        + [turned] * 4
        + [pl.BlockSpec((1, 2, length), lambda i: (i + start, 0, 0))]
        + [fixed(a) for a in (doc_row, doc_col, cos_t, sin_t)],
        out_specs=[out] * 3,
        out_shape=[shape((count * PAIR, length), BF16)] * 3,
        scratch_shapes=[pltpu.VMEM((length, length), F32)] + [pltpu.VMEM((PAIR, length), F32)] * 3,
        compiler_params=params(),
        cost_estimate=cost(28 * length * length * count * PAIR, 14e6 * count * PAIR / width),
        name="attend_back",
    )(q, k, v, d_mix, q_t, k_t, d_mix_t, mix_t, log_sum, doc_row, doc_col, cos_t, sin_t)


def first_kernel(qk, vo, me, *refs):
    x_refs, refs = refs[:4], refs[4:]
    (d_mid, vec, dq_t, dk_t, dv_t), refs = refs[:5], refs[5:]
    mul = norm_scale(vec, GAIN_1, SCALE_1)
    held, refs = refs[: 2 * len(qk.parts)], refs[2 * len(qk.parts) :]
    out_refs, (sums, w_buf, sems) = refs[:4], refs[4:]
    copies = qkv_copies(me, qk, vo, held, w_buf, sems, w_buf.shape[1] // qk.count)
    for copy in copies:
        copy.start()
    for copy in copies:
        copy.wait()
    d_n_t = (
        dot_nn(w_buf[0], dq_t[...]) + dot_nn(w_buf[1], dk_t[...]) + dot_nn(w_buf[2], dv_t[...])
    )
    part = x_refs[0].shape[0]
    totals = [jnp.zeros(mul.shape, F32) for _ in range(2)]
    for b in range(4):
        r = slice(b * part, (b + 1) * part)
        dn = d_n_t[:, r].T
        x = x_refs[b][...].astype(F32)
        centred = x - jnp.mean(x, axis=-1, keepdims=True)
        inverse = lax.rsqrt(jnp.mean(centred * centred, axis=-1, keepdims=True) + EPSILON)
        unit = centred * inverse
        dn_unit = dn * unit
        du = dn * mul
        out_refs[b][...] = (
            d_mid[r, :]
            + inverse
            * (
                du
                - jnp.mean(du, axis=-1, keepdims=True)
                - unit * jnp.mean(dn_unit * mul, axis=-1, keepdims=True)
            )
        ).astype(BF16)
        for n, term in enumerate((dn_unit, dn)):
            totals[n] += jnp.sum(term, axis=0, keepdims=True)
    for n in range(2):
        sums[n : n + 1, :] = totals[n]


def first(me, x_parts, d_mid, vec, dq_t, dk_t, dv_t, qk, vo):
    part, width = x_parts[0].shape
    length = 4 * part
    cols = dq_t.shape[0]
    return pl.pallas_call(
        partial(first_kernel, qk, vo),
        out_shape=[shape((part, width), BF16)] * 4 + [shape((2, width), F32)],
        in_specs=[SMEM] + [VMEM] * 9 + [ANY] * (2 * len(qk.parts)),
        out_specs=[VMEM] * 5,
        scratch_shapes=[
            pltpu.VMEM((3, width, cols), BF16),
            pltpu.SemaphoreType.DMA((3, qk.count)),
        ],
        compiler_params=params(),
        cost_estimate=cost(6 * length * width * cols, 20e6),
        name="first",
    )(me, *x_parts, d_mid, vec, dq_t, dk_t, dv_t, *qk.parts, *vo.parts)


def three_terms(v):
    rows = []
    for _ in range(3):
        rows.append(v.astype(BF16).astype(F32))
        v = v - rows[-1]
    rows += [jnp.zeros_like(v)] * 5
    return jnp.concatenate(rows, axis=0).astype(BF16)


def modulate_kernel(qk, vo, zones, me, act, *refs):
    parts = len(qk.parts)
    qk_refs, vo_refs, (vec, bias, ada, small, sems) = refs[:parts], refs[parts:-5], refs[-5:]
    count = qk.count
    rows = ada.shape[0] // count
    cut = rows // 2
    copies = []
    for h, (held, group) in enumerate(((qk, qk_refs), (vo, vo_refs))):
        for block, j, n in held.blocks(group):
            at = row_at(me, j, rows) + h * cut
            copies.append(
                pltpu.make_async_copy(
                    block.at[pl.ds(2 * rows, cut), :], ada.at[pl.ds(at, cut), :], sems.at[h, n]
                )
            )
            if h:
                copies.append(
                    pltpu.make_async_copy(
                        block.at[pl.ds(2 * rows + cut, 16), :],
                        small.at[pl.ds(row_at(me, j, 16), 16), :],
                        sems.at[2, n],
                    )
                )
    for copy in copies:
        copy.start()
    for copy in copies:
        copy.wait()
    kinds = ada.shape[1] // act.shape[1]
    act3 = three_terms(act[...])
    across = vec.shape[1] // rows
    vec[...] = jnp.zeros_like(vec)
    for k in range(kinds):
        lanes = slice(k * act.shape[1], (k + 1) * act.shape[1])
        found = jnp.sum(dot_nt(act3, ada[:, lanes]), axis=0, keepdims=True)
        for d in range(count):
            m = d * kinds + k
            at = (m % across) * rows
            extra = small[d * 16 : (d + 1) * 16, :].astype(F32)
            vec[m // across : m // across + 1, at : at + rows] = (
                found[:, d * rows : (d + 1) * rows] + extra[1:2, k * rows : (k + 1) * rows]
            )
    for d in range(count):
        extra = small[d * 16 : (d + 1) * 16, :].astype(F32)
        here = slice(d * rows, (d + 1) * rows)
        for n in range(3):
            vec[BIAS_OUT + n : BIAS_OUT + n + 1, here] = extra[2:3, n * rows : (n + 1) * rows]
        for n in range(zones):
            far = (n - zones // 2) % zones
            at = n * (extra.shape[1] // zones)
            bias[far : far + 1, here] = extra[0:1, at : at + rows]


def modulate(me, act, qk, vo, zones, rows):
    width = qk.parts[0].shape[2]
    return pl.pallas_call(
        partial(modulate_kernel, qk, vo, zones),
        out_shape=[
            shape((16, width), F32),
            shape((zones, width), F32),
            shape((qk.count * rows, width), BF16),
        ],
        in_specs=[SMEM, VMEM] + [ANY] * (len(qk.parts) + len(vo.parts)),
        out_specs=[VMEM] * 3,
        scratch_shapes=[
            pltpu.VMEM((qk.count * 16, width), BF16),
            pltpu.SemaphoreType.DMA((3, qk.count)),
        ],
        compiler_params=params(),
        cost_estimate=cost(2e7, 4e6),
        name="modulate",
    )(me, act, *qk.parts, *vo.parts)


def gather_up_kernel(count, vec, ada, sums, sums_one, d_bias_down, bias_grad, act, cond, out, spread):
    width = vec.shape[1]
    rows = width // count
    size = act.shape[1]
    kinds = ada.shape[1] // size
    norm_1, norm_2 = sums_one[0:1, :], sums[1:2, :]
    d_mod = (
        sums_one[1:2, :],
        norm_1 * vec_row(vec, GAIN_1),
        sums[3:4, :],
        sums[2:3, :],
        norm_2 * vec_row(vec, GAIN_2),
        sums[0:1, :],
    )
    others = (
        norm_1 * (1.0 + vec_row(vec, SCALE_1)),
        norm_2 * (1.0 + vec_row(vec, SCALE_2)),
        d_bias_down[...],
    )
    out[...] = jnp.zeros_like(out)
    base = (kinds + 3) * rows
    for d in range(count):
        here = slice(d * rows, (d + 1) * rows)
        for k in range(kinds):
            m = d * kinds + k
            at = (m % count) * rows
            piece = d_mod[m // count][:, at : at + rows]
            out[d : d + 1, k * rows : (k + 1) * rows] = piece
            spread[k : k + 1, here] = piece
        for n, value in enumerate(others):
            at = (kinds + n) * rows
            out[d : d + 1, at : at + rows] = value[:, here]
        for n in range(bias_grad.shape[0]):
            at = base + n * rows
            out[d : d + 1, at : at + rows] = bias_grad[n : n + 1, here]
        out[d : d + 1, out.shape[1] - size :] = act[...]
    total = jnp.zeros(act.shape, F32)
    for k in range(kinds):
        three = three_terms(spread[k : k + 1, :])
        total += jnp.sum(dot_nn(three, ada[:, k * size : (k + 1) * size]), axis=0, keepdims=True)
    c = cond[...]
    sig = 1.0 / (1.0 + jnp.exp(-c))
    out[count : count + 1, :size] = total * (sig * (1.0 + c * (1.0 - sig)))


def gather_up(vec, ada, sums, sums_one, d_bias_down, bias_grad, act, cond, count, length):
    return pl.pallas_call(
        partial(gather_up_kernel, count),
        out_shape=shape((2 * count, length), F32),
        in_specs=[VMEM] * 8,
        out_specs=VMEM,
        scratch_shapes=[pltpu.VMEM((8, vec.shape[1]), F32)],
        compiler_params=params(),
        cost_estimate=cost(2e7, 4e6),
        name="gather_up",
    )(vec, ada, sums, sums_one, d_bias_down, bias_grad, act, cond)


def weight_grads_kernel(me, n_t, dq_t, dk_t, dv_t, d_att_t, mix_t, *refs):
    grads, stage = refs[:-1], refs[-1]
    pairs = (n_t, dq_t), (n_t, dk_t), (n_t, dv_t), (d_att_t, mix_t)
    for c, (a, b) in enumerate(pairs):
        grad = dot_nt(a[...], b[...])
        spread_rows(me, grad, stage, *(split_writer(ref, c) for ref in grads))


def weight_grads(me, n_t, dq_t, dk_t, dv_t, d_att_t, mix_t, blocks):
    width, length = n_t.shape
    cols = dq_t.shape[0]
    rows = width // blocks
    half = max(blocks // 2, 1)
    grads = 1 if blocks == 1 else 2
    return pl.pallas_call(
        weight_grads_kernel,
        out_shape=[shape((2, half, 4, rows, cols // 2), BF16)] * grads,
        in_specs=[SMEM] + [VMEM] * 6,
        out_specs=[VMEM] * grads,
        scratch_shapes=[pltpu.VMEM((blocks, rows, cols), BF16)],
        compiler_params=params(),
        cost_estimate=cost(8 * length * width * cols, 14e6),
        name="weight_grads",
    )(me, n_t, dq_t, dk_t, dv_t, d_att_t, mix_t)


class Group:
    def __init__(self, dp_count, tensor_count, per_dp):
        self.dp, self.tensor, self.per_dp = dp_count, tensor_count, per_dp
        self.d, self.r = lax.axis_index("dp"), lax.axis_index("tensor")
        self.paired = dp_count == 8

    def bit(self, v, b):
        return lax.ppermute(v, "dp", [(i, i ^ (1 << b)) for i in range(self.dp)])

    def step(self, v, k):
        return lax.ppermute(v, "dp", [(i, i ^ k) for i in range(self.dp)])

    def z(self, v, k):
        return lax.ppermute(v, "tensor", [(i, i ^ k) for i in range(self.tensor)])

    def owns(self, d, r):
        return 0 <= r - d % 2 < self.per_dp

    def to_owner(self, rows, zero_idle):
        mine = self.r - self.d % 2
        top = self.per_dp - 1
        own = lax.dynamic_index_in_dim(rows, jnp.clip(mine, 0, top), 0, keepdims=False)
        if zero_idle:
            own = jnp.where((mine >= 0) & (mine <= top), own, jnp.zeros_like(own))
        parts = [own]
        for k in range(1, self.tensor):
            want = (self.r ^ k) - self.d % 2
            sent = lax.dynamic_index_in_dim(rows, jnp.clip(want, 0, top), 0, keepdims=False)
            pairs = [
                (d * self.tensor + r, d * self.tensor + (r ^ k))
                for d in range(self.dp)
                for r in range(self.tensor)
                if self.owns(d, r ^ k)
            ]
            parts.append(lax.ppermute(sent, BOTH, pairs))
        return parts

    def to_holder(self, parts):
        came = [parts[0]]
        for k in range(1, self.tensor):
            pairs = [
                (d * self.tensor + r, d * self.tensor + (r ^ k))
                for d in range(self.dp)
                for r in range(self.tensor)
                if self.owns(d, r)
            ]
            came.append(lax.ppermute(parts[k], BOTH, pairs))
        return came

    def held_rows(self, came):
        stack = jnp.stack(came)
        return jnp.stack(
            [
                lax.dynamic_index_in_dim(stack, self.r ^ (j + self.d % 2), 0, keepdims=False)
                for j in range(self.per_dp)
            ]
        )

    def z_pair(self, v, got):
        return jnp.concatenate([v, got], axis=-1)

    def gather_pair(self, v, got, order):
        pair = jnp.stack([v, got])
        return [pair, self.bit(pair, order[1])]

    def gather_cores(self, parts, order):
        one, two = (1 << b for b in order)
        rels = [(0, one), (two, one ^ two)]
        if len(parts) == 1:
            rels = [rels[0] + rels[1]]
        rels += [tuple(j ^ 1 for j in rel) for rel in rels]
        return Held(parts + [self.bit(p, 0) for p in parts], rels)

    def whole(self, v, axis):
        return lax.all_gather(v, "dp", axis=axis, tiled=True)

    def swap(self, v):
        if not self.paired:
            return lax.all_to_all(v, "dp", split_axis=0, concat_axis=0, tiled=True)
        v = jnp.take(v, self.d ^ jnp.arange(self.dp), axis=0)[None]
        for b in range(3):
            v = v.reshape(v.shape[0], v.shape[1] // 2, 2, *v.shape[2:])
            v = jnp.concatenate([v[:, :, 0], self.bit(v[:, :, 1], b)])
        return v[:, 0]


class Flight:
    def __init__(self, value):
        self.value = value


class Sum:
    def __init__(self, group, keep, send=None):
        self.group, self.stage, self.flights = group, 0, []
        if not group.paired:
            value = keep[:, 0].astype(F32)
            value = lax.psum_scatter(value, "dp", scatter_dimension=value.ndim - 2, tiled=True)
            self.total = [value[0], value[1]]
            return
        self.total = [keep[0], keep[1]]
        flight = Flight(group.bit(send, 0))
        self.flights = [(flight, 0), (flight, 1)]

    def settle(self):
        if self.flights:
            self.total = [
                t.astype(F32) + flight.value[at].astype(F32)
                for t, (flight, at) in zip(self.total, self.flights)
            ]
        if self.stage == 2:
            self.total = [t[0] for t in self.total]
        self.flights = []

    def split(self):
        out = []
        for n, order in enumerate(((1, 2), (2, 1))):
            t, b = self.total[n], order[self.stage]
            if self.stage == 0:
                t = t.reshape(2, 2, *t.shape[1:])
                stay, go = (t[:, 0], t[:, 1]) if b == 1 else (t[0], t[1])
            else:
                stay, go = t[:1], t[1:]
            self.total[n] = stay
            out.append((b, go.astype(BF16)))
        self.stage += 1
        self.flights = [None, None]
        return out


def exchange(*sums):
    links = {}
    for t in sums:
        t.settle()
        if t.group.paired:
            for n, (b, go) in enumerate(t.split()):
                links.setdefault(b, []).append((t, n, go))
    for b, items in links.items():
        blocks = [go for _, _, go in items]
        blocks = blocks[0] if len(blocks) == 1 else jnp.concatenate(blocks)
        flight, at = Flight(items[0][0].group.bit(blocks, b)), 0
        for t, n, go in items:
            t.flights[n] = (flight, slice(at, at + go.shape[0]))
            at += go.shape[0]


def tie(value, *sums):
    flights = {id(f): f for t in sums for f, _ in t.flights}
    flights = list(flights.values())
    value, arrived = lax.optimization_barrier((value, [f.value for f in flights]))
    for flight, v in zip(flights, arrived):
        flight.value = v
    return value


def silu_slope(c):
    sig = jax.nn.sigmoid(c)
    return sig * (1.0 + c * (1.0 - sig))


def shards(
    inputs, condition, doc_ids, positions, w_qkv, w_out, w_up, bias_up, w_down, bias_down,
    gain_one, gain_two, w_ada, bias_ada, out_grad,
):
    dp_count = lax.axis_size("dp")
    tensor_count = lax.axis_size("tensor")
    per_dp, part, width = inputs.shape
    length = doc_ids.shape[1]
    rows = w_up.shape[0]
    group = Group(dp_count, tensor_count, per_dp)
    blocks = dp_count if group.paired else 1
    d, r = group.d, group.r
    me = jnp.where(group.paired, d, 0).astype(jnp.int32).reshape(1)
    mine = jnp.clip(r - d % 2, 0, per_dp - 1)
    own_row = lambda v: lax.dynamic_index_in_dim(v, mine, 0, keepdims=False)
    join = lambda parts: jnp.concatenate(parts, axis=-1)

    cols, cond_size, mod_width = w_qkv.shape[2], w_ada.shape[0], w_ada.shape[1]
    ways = (1, 2), (2, 1)
    cond = own_row(condition).astype(F32)[None]
    act = jax.nn.silu(cond)
    early = jnp.concatenate([w_qkv.reshape(-1, cols), w_out.T])
    late = jnp.concatenate([w_up, w_down.T])
    if group.paired:
        early = jnp.concatenate([early, jnp.pad(bias_up, ((0, 15), (0, cols - rows)))])
    if group.paired:
        ada = w_ada.T.reshape(-1, rows, cond_size).transpose(1, 0, 2).reshape(rows, width)
        cut, top = rows // 2, 2 * rows
        wide = lambda v: jnp.pad(v, (0, width - v.shape[0]))[None]
    early = group.z_pair(early, group.z(early, 1))
    early = join([early, group.z(early, 2)])
    late, early = lax.optimization_barrier((late, early))
    late_got = group.z(late, 1)
    if group.paired:
        small = jnp.concatenate(
            [
                early[2 * top : 2 * top + 1],
                wide(bias_ada),
                wide(jnp.concatenate([bias_down, gain_one, gain_two])),
                early[2 * top + 3 :],
            ]
        )
        firsts = (
            jnp.concatenate([early[:top], ada[:cut]]),
            jnp.concatenate([early[top : 2 * top], ada[cut:], small]),
        )
        came = [group.bit(v, way[0]) for v, way in zip(firsts, ways)]
        late_got, came = lax.optimization_barrier((late_got, came))
        late = group.z_pair(late, late_got)
        late_far = group.z(late, 2)
        near = [group.gather_pair(v, got, way) for v, got, way in zip(firsts, came, ways)]
        inputs, late_far, near = lax.optimization_barrier((inputs, late_far, near))
        x_parts = group.to_owner(inputs, False)
        qk, vo = (group.gather_cores([jnp.concatenate(p)], way) for p, way in zip(near, ways))
        late = join([late_far, late])
        late, qk.parts, vo.parts = lax.optimization_barrier((late, qk.parts, vo.parts))
        lates = late[:rows], late[rows:]
        came = [group.bit(v, way[0]) for v, way in zip(lates, ways)]
        vec, bias_hidden, ada_all = modulate(me, act, qk, vo, tensor_count, rows)
        out_grad, x_parts, came = lax.optimization_barrier((out_grad, x_parts, came))
        g_parts = group.to_owner(out_grad, True)
        near = [group.gather_pair(v, got, way) for v, got, way in zip(lates, came, ways)]
    else:
        x_parts = group.to_owner(inputs, False)
        g_parts = group.to_owner(out_grad, True)
        late = group.z_pair(late, late_got)
        late = join([group.z(late, 2), late])
        flat = lambda v: group.whole(v.reshape(2, rows, width), 1).reshape(1, 2 * width, width)
        qk, vo = Held([flat(early[: 2 * rows])], [(0,)]), Held([flat(early[2 * rows :])], [(0,)])
        up, dn = (Held([group.whole(v, 0)[None]], [(0,)]) for v in (late[:rows], late[rows:]))
        w_all = group.whole(w_ada, 1)
        modulation = jnp.dot(
            act, w_all.astype(F32), precision=PRECISE, preferred_element_type=F32
        ) + group.whole(bias_ada, 0).astype(F32)
        small = group.whole(jnp.stack([bias_down, gain_one, gain_two]), 1).astype(F32)
        vec = jnp.concatenate([modulation.reshape(6, width), small, jnp.zeros((7, width), F32)])
        bias_hidden = group.whole(bias_up, 1)
        bias_hidden = jnp.concatenate([group.z(bias_hidden, k) for k in (2, 3, 0, 1)]).astype(F32)

    order = r ^ jnp.arange(tensor_count)
    mixed = lambda v: own_row(v).reshape(tensor_count, part)[order].reshape(-1)
    docs, places = mixed(doc_ids), mixed(positions)
    doc_row, doc_col = docs[None, :], docs[:, None]
    frequencies = 10000.0 ** (-2.0 * jnp.arange(HEAD // 2, dtype=F32) / HEAD)
    turned = places.astype(F32)[:, None] * frequencies[None, :]
    cosine, sine = jnp.cos(turned), jnp.sin(turned)
    nothing = jnp.zeros_like(sine)
    cos_flat = jnp.concatenate([cosine] * 4, axis=1)
    sin_a = jnp.concatenate([-sine, nothing] * 2, axis=1)
    sin_b = jnp.concatenate([nothing, sine] * 2, axis=1)
    cos_t, sin_t = cosine.T, sine.T

    n_t, q, k, v, q_t, k_t, v_t = qkv(me, x_parts, vec, cos_flat, sin_a, sin_b, qk, vo)
    mix_t, log_sum = attend(q, k, v_t, doc_row, doc_col)
    if group.paired:
        mix_t, near, g_parts = lax.optimization_barrier((mix_t, near, g_parts))
        up, dn = (group.gather_cores(p, way) for p, way in zip(near, ways))
    att, n_two, n_two_t, d_down, d_down_t, d_bias_down = middle(
        me, x_parts, g_parts, mix_t, vec, vo
    )
    size = w_up.shape[1]
    feed_args = (me, n_two, n_two_t, d_down, d_down_t, bias_hidden, up, dn)

    down, d_n, d_bias_a, *grads = feed(*feed_args, 0, None, 2 * size)
    sum_a = Sum(group, *grads)
    down, d_n, d_bias_b, *grads = feed(*feed_args, 2 * size, (down, d_n), 2 * size)
    down = tie(down, sum_a)
    exchange(sum_a)
    sum_b = Sum(group, *grads)
    *out_parts, d_mid, d_mix, d_mix_t, sums, d_att_t = turn(
        me, x_parts, g_parts, att, down, d_n, mix_t, vec, vo
    )
    d_mix, out_parts = tie((d_mix, out_parts), sum_a, sum_b)
    came = group.to_holder(out_parts)
    exchange(sum_a, sum_b)
    dq_t, dk_t, dv_t = attend_back(
        q, k, v, d_mix, q_t, k_t, d_mix_t, mix_t, log_sum, doc_row, doc_col, cos_t, sin_t, 0,
        q.shape[1] // PAIR,
    )
    dq_t, came = tie((dq_t, came), sum_a, sum_b)
    block_out = group.held_rows(came)
    sum_a.settle()
    exchange(sum_b)
    far_up = group.z(sum_a.total[0].astype(BF16), 2)
    grads = weight_grads(me, n_t, dq_t, dk_t, dv_t, d_att_t, mix_t, blocks)
    d_mid, grads, far_up, last = tie((d_mid, grads, far_up, sum_a.total[1]), sum_b)
    far_dn = group.z(last.astype(BF16), 2)
    sum_w = Sum(group, *grads)
    *in_parts, sums_one = first(me, x_parts, d_mid, vec, dq_t, dk_t, dv_t, qk, vo)

    in_parts, sums_one, far_dn = tie((in_parts, sums_one, far_dn), sum_w)
    came = group.to_holder(in_parts)
    exchange(sum_w)
    sum_b.settle()
    near = jnp.stack(sum_b.total) + jnp.stack([far_up, far_dn]).astype(F32)
    sums_one, near = tie((sums_one, near), sum_w)
    exchange(sum_w)
    d_bias = jnp.concatenate([d_bias_b.reshape(2, -1), d_bias_a.reshape(2, -1)])
    edge = mod_width + 3 * rows
    if group.paired:
        table = gather_up(
            vec, ada_all, sums, sums_one, d_bias_down, d_bias, act, cond, dp_count,
            edge + tensor_count * rows + 2 * cond_size - (edge + tensor_count * rows) % cond_size,
        )
    else:
        d_gate_2, norm_2, d_shift_2, d_gate_1 = (sums[n : n + 1] for n in range(4))
        norm_1, d_shift_1 = sums_one[:1], sums_one[1:]
        d_mod = [
            d_shift_1, norm_1 * vec[GAIN_1], d_gate_1, d_shift_2, norm_2 * vec[GAIN_2], d_gate_2
        ]
        others = [norm_1 * (1.0 + vec[SCALE_1]), norm_2 * (1.0 + vec[SCALE_2]), d_bias_down]
        sliced = lambda t: t.reshape(dp_count, -1)
        d_mod = jnp.concatenate(d_mod, axis=1)
        d_cond = lax.dot_general(
            d_mod,
            w_all.astype(F32),
            (((1,), (1,)), ((), ())),
            precision=PRECISE,
            preferred_element_type=F32,
        ) * silu_slope(cond)
        table = jnp.concatenate(
            [sliced(d_mod)]
            + [sliced(t) for t in others]
            + [sliced(t) for t in d_bias]
            + [jnp.broadcast_to(act, (dp_count, cond_size))],
            axis=1,
        )
        last = jnp.pad(d_cond, ((0, 0), (0, table.shape[1] - cond_size)))
        table = jnp.concatenate([table, last])
    table, came = tie((table, came), sum_w)
    sum_w.settle()
    input_grad = group.held_rows(came)
    half = near.shape[-1] // 2
    table_got = group.z(table, 1)
    feeds = group.z(near[..., half:].astype(BF16), 1)
    near_w, far_w = sum_w.total
    far_w = group.z(far_w.astype(BF16), 2)
    table_got, far_w, feeds = lax.optimization_barrier((table_got, far_w, feeds))
    grad_up, grad_down = near[..., :half] + feeds.astype(F32)
    near_w = near_w + far_w.astype(F32)
    grad = near_w[..., :cols] + group.z(near_w[..., cols:].astype(BF16), 1).astype(F32)
    grad_qkv, grad_out = grad[:3], grad[3].T
    tables = jnp.stack([table, table_got])
    tables = jnp.concatenate([tables, group.z(tables, 2)]).transpose(1, 0, 2)[:, order]
    arrived = group.swap(tables[:dp_count])
    totals = jnp.sum(arrived[..., :edge], axis=(0, 1))
    biases = arrived[..., edge : edge + tensor_count * rows].reshape(
        dp_count, tensor_count, tensor_count, rows
    )
    wanted = (jnp.arange(tensor_count) == order[:, None])[None, :, :, None]
    grad_bias_up = jnp.sum(jnp.where(wanted, biases, 0.0), axis=(0, 1, 2))
    grad_bias_ada = totals[:mod_width]
    grad_gain_one, grad_gain_two, grad_bias_down = (
        totals[mod_width + n * rows : mod_width + (n + 1) * rows] for n in range(3)
    )
    arrived = arrived.reshape(dp_count * tensor_count, -1)
    grad_ada = lax.dot_general(
        arrived[:, -cond_size:],
        arrived[:, :mod_width],
        (((0,), (0,)), ((), ())),
        precision=PRECISE,
        preferred_element_type=F32,
    )
    cond_grad = jnp.take(
        tables[dp_count, :, :cond_size], jnp.arange(per_dp) + d % 2, axis=0
    )
    return (
        block_out,
        input_grad,
        cond_grad,
        grad_qkv,
        grad_out,
        grad_up,
        grad_bias_up[None],
        grad_down.T,
        grad_bias_down,
        grad_gain_one,
        grad_gain_two,
        grad_ada,
        grad_bias_ada,
    )


def solution(mesh):
    return jax.shard_map(
        shards,
        mesh=mesh,
        in_specs=(
            P("dp", "tensor", None),
            P("dp", None),
            P("dp", None),
            P("dp", None),
            P(None, "dp", "tensor"),
            P("tensor", "dp"),
            P("dp", "tensor"),
            P("tensor", "dp"),
            P("tensor", "dp"),
            P("dp"),
            P("dp"),
            P("dp"),
            P(None, "dp"),
            P("dp"),
            P("dp", "tensor", None),
        ),
        out_specs=(
            P("dp", "tensor", None),
            P("dp", "tensor", None),
            P("dp", None),
            P(None, "dp", "tensor"),
            P("tensor", "dp"),
            P("dp", "tensor"),
            P("tensor", "dp"),
            P("tensor", "dp"),
            P("dp"),
            P("dp"),
            P("dp"),
            P(None, "dp"),
            P("dp"),
        ),
        check_vma=False,
    )
```

```python
from functools import partial

import jax
import jax.numpy as jnp
import numpy as np
from jax import lax
from jax.experimental import pallas as pl
from jax.experimental.pallas import tpu as pltpu
from jax.sharding import PartitionSpec as P

HEAD = 64
PRECISE = lax.Precision.HIGHEST
EPSILON = 1e-05
SHIFT_1, SCALE_1, GATE_1, SHIFT_2, SCALE_2, GATE_2, BIAS_OUT, GAIN_1, GAIN_2 = range(9)
F32 = jnp.float32
BF16 = jnp.bfloat16
PAIR = 2 * HEAD
BOTH = ("dp", "tensor")
ANY = pl.BlockSpec(memory_space=pl.ANY)
VMEM = pl.BlockSpec(memory_space=pltpu.VMEM)
SMEM = pl.BlockSpec(memory_space=pltpu.SMEM)


def dot_nn(a, b):
    return jnp.dot(a, b, preferred_element_type=F32)


def dot_nt(a, b):
    return lax.dot_general(a, b, (((1,), (1,)), ((), ())), preferred_element_type=F32)


def params(**more):
    return pltpu.CompilerParams(vmem_limit_bytes=58 << 20, **more)


def cost(flops, nbytes, trans=0):
    return pl.CostEstimate(flops=int(flops), bytes_accessed=int(nbytes), transcendentals=int(trans))


def shape(dims, kind):
    return jax.ShapeDtypeStruct(tuple(dims), kind)


def row_at(me_ref, index, rows):
    return pl.multiple_of((me_ref[0] ^ index) * rows, rows)


def at_step(n, act):
    pl.when(pl.program_id(0) == n)(act)


def pick(refs, out, each=1):
    rows = refs[0].shape[0]
    for n, ref in enumerate(refs):
        at = pl.ds(n % each * rows, rows)
        at_step(n // each, lambda ref=ref, at=at: out.__setitem__((at, slice(None)), ref[...]))
    return out[...].astype(F32)


def put(refs, value):
    for n, ref in enumerate(refs):
        at_step(n, lambda ref=ref: ref.__setitem__(..., value))


def add_row(ref, n, value):
    at_step(0, lambda: ref.__setitem__((slice(n, n + 1), slice(None)), jnp.zeros_like(value)))
    ref[n : n + 1, :] += value


def start_all(copies):
    def act():
        for copy in copies:
            copy.start()

    at_step(0, act)


def wait_all(copies):
    def act():
        for copy in copies:
            copy.wait()

    at_step(0, act)


def row_block(rows, cols):
    return pl.BlockSpec((rows, cols), lambda i: (i, 0))


def col_block(rows, cols):
    return pl.BlockSpec((rows, cols), lambda i: (0, i))


def vec_row(vec, n):
    return vec[n : n + 1, :]


def norm_scale(vec, gain, scale):
    return vec_row(vec, gain) * (1.0 + vec_row(vec, scale))


def rotary_kernel(places, frequencies, cos_flat, sin_a, sin_b, cos_t, sin_t):
    angle = frequencies[...] * places[...]
    cosine, sine = jnp.cos(angle), jnp.sin(angle)
    cos_t[...], sin_t[...] = cosine, sine
    nothing = jnp.zeros_like(sine)
    cos_flat[...] = jnp.concatenate([cosine] * 4, axis=0).T
    sin_a[...] = jnp.concatenate([-sine, nothing] * 2, axis=0).T
    sin_b[...] = jnp.concatenate([nothing, sine] * 2, axis=0).T


def rotary(places, frequencies):
    length, half = places.shape[1], frequencies.shape[0]
    return pl.pallas_call(
        rotary_kernel,
        out_shape=[shape((length, 4 * half), F32)] * 3 + [shape((half, length), F32)] * 2,
        in_specs=[VMEM] * 2,
        out_specs=[VMEM] * 5,
        compiler_params=params(),
        cost_estimate=cost(6e6, 2e6),
        name="rotary",
    )(places, frequencies)


class Held:
    def __init__(self, parts, rels, offset=0):
        self.parts, self.rels, self.offset = parts, rels, offset

    def blocks(self, refs):
        n = 0
        for ref, rel in zip(refs, self.rels):
            for i, j in enumerate(rel):
                yield ref.at[i + self.offset], j, n
                n += 1

    @property
    def count(self):
        return sum(len(rel) for rel in self.rels)


def qkv_copies(me, qk, vo, refs, w_buf, sems, rows):
    out = []
    parts = len(qk.parts)
    for held, group, planes in ((qk, refs[:parts], (0, 1)), (vo, refs[parts:], (2,))):
        for block, j, n in held.blocks(group):
            for c, plane in enumerate(planes):
                out.append(
                    pltpu.make_async_copy(
                        block.at[pl.ds(c * rows, rows), :],
                        w_buf.at[plane, pl.ds(row_at(me, j, rows), rows), :],
                        sems.at[plane, n],
                    )
                )
    return out


def qkv_kernel(qk, vo, me, *refs):
    x_refs, refs = refs[:4], refs[4:]
    (vec, cosine, sin_a, sin_b), refs = refs[:4], refs[4:]
    mul, add = norm_scale(vec, GAIN_1, SCALE_1), vec_row(vec, SHIFT_1)
    held, refs = refs[: 2 * len(qk.parts)], refs[2 * len(qk.parts) :]
    (n_t, k_out, v_out, q_t, k_t, v_t), (w_buf, x_buf, sems) = refs[:6], refs[6:]
    copies = qkv_copies(me, qk, vo, held, w_buf, sems, w_buf.shape[1] // qk.count)
    start_all(copies)
    x = pick(x_refs, x_buf, 2)
    centred = x - jnp.mean(x, axis=-1, keepdims=True)
    spread = jnp.mean(centred * centred, axis=-1, keepdims=True)
    normed = (centred * lax.rsqrt(spread + EPSILON) * mul + add).astype(BF16)
    n_t[...] = normed.T
    wait_all(copies)
    width = k_out.shape[1]
    for c, (flat, turned, factor) in enumerate(((None, q_t, HEAD**-0.5), (k_out, k_t, 1.0))):
        proj = dot_nn(normed, w_buf[c])
        for p in range(width // PAIR):
            lanes = slice(p * PAIR, (p + 1) * PAIR)
            r = proj[:, lanes]
            spun = (
                r * cosine[...]
                + pltpu.roll(r, PAIR - HEAD // 2, 1) * sin_a[...]
                + pltpu.roll(r, HEAD // 2, 1) * sin_b[...]
            )
            spun = spun.astype(BF16) * BF16(factor)
            if flat is not None:
                flat[:, lanes] = spun
            turned[lanes, :] = spun.T
    values = dot_nn(normed, w_buf[2]).astype(BF16)
    v_out[...] = values
    v_t[...] = values.T


def qkv(me, x_parts, vec, cosine, sin_a, sin_b, qk, vo):
    part, width = x_parts[0].shape
    length = 4 * part
    cols = qk.parts[0].shape[2]
    flat, turned = shape((length, cols), BF16), shape((cols, length), BF16)
    return pl.pallas_call(
        partial(qkv_kernel, qk, vo),
        grid=(2,),
        out_shape=[shape((width, length), BF16), flat, flat, turned, turned, turned],
        in_specs=[SMEM]
        + [VMEM] * 5
        + [row_block(2 * part, PAIR)] * 3
        + [ANY] * (2 * len(qk.parts)),
        out_specs=[col_block(width, 2 * part)]
        + [row_block(2 * part, cols)] * 2
        + [col_block(cols, 2 * part)] * 3,
        scratch_shapes=[
            pltpu.VMEM((3, width, cols), BF16),
            pltpu.VMEM((2 * part, width), BF16),
            pltpu.SemaphoreType.DMA((3, qk.count)),
        ],
        compiler_params=params(),
        cost_estimate=cost(6 * length * width * cols, 16e6),
        name="qkv",
    )(me, *x_parts, vec, cosine, sin_a, sin_b, *qk.parts, *vo.parts)


def three_terms(v):
    rows = []
    for _ in range(3):
        rows.append(v.astype(BF16).astype(F32))
        v = v - rows[-1]
    rows += [jnp.zeros_like(v)] * 5
    return jnp.concatenate(rows, axis=0).astype(BF16)


DOCS, TERMS = 8, 16


def added_lanes(out, doc_col):
    lane = lax.broadcasted_iota(jnp.int32, out.shape, 1) % HEAD
    other = jnp.where(lane == doc_col[...], 0.0, -1e30)
    ones = jnp.where((lane >= TERMS) & (lane < TERMS + 3), 1.0, 0.0)
    out[...] = jnp.where(lane < DOCS, other, ones).astype(BF16)


def document_rows(doc_row):
    row = lax.broadcasted_iota(jnp.int32, (TERMS, doc_row.shape[1]), 0)
    return jnp.where(row == doc_row[...], 1.0, 0.0).astype(BF16)


def with_lanes(ref, added, head):
    lane = lax.broadcasted_iota(jnp.int32, (1, PAIR), 1)
    return jnp.where((lane // HEAD) == head, ref[...], added[...])


def with_rows(out, ref, head, rows):
    own, other = head * HEAD, (1 - head) * HEAD
    out[own : own + HEAD, :] = ref[own : own + HEAD, :]
    out[other : other + HEAD, :] = jnp.zeros((HEAD, out.shape[1]), BF16)
    for n, value in enumerate(rows):
        if value is not None:
            at = other + n * TERMS
            out[at : at + value.shape[0], :] = value


def attend_kernel(q_t, k, v_t, doc_row, doc_col, mix_t, log_sum, added, ahead):
    @pl.when(pl.program_id(0) == 0)
    def _():
        added_lanes(added, doc_col)

    docs = document_rows(doc_row)
    for h in range(2):
        with_rows(ahead.at[h], q_t, h, [docs])

    for h in range(2):
        rows = slice(h * HEAD, (h + 1) * HEAD)
        scores = dot_nn(with_lanes(k, added, h), ahead[h])
        top = jnp.max(scores, axis=0, keepdims=True)
        weights = jnp.exp(scores - top)
        total = jnp.sum(weights, axis=0, keepdims=True)
        mixed = dot_nn(v_t[rows, :], weights.astype(BF16))
        mix_t[rows, :] = (mixed / total).astype(BF16)
        log_sum[0, h] = top + jnp.log(total)


def attend(q_t, k, v_t, doc_row, doc_col):
    length, width = k.shape
    pairs = width // PAIR
    flat = pl.BlockSpec((length, PAIR), lambda i: (0, i))
    turned = pl.BlockSpec((PAIR, length), lambda i: (i, 0))
    return pl.pallas_call(
        attend_kernel,
        grid=(pairs,),
        in_specs=[
            turned,
            flat,
            turned,
            pl.BlockSpec((1, length), lambda i: (0, 0)),
            pl.BlockSpec((length, 1), lambda i: (0, 0)),
        ],
        out_specs=[turned, pl.BlockSpec((1, 2, 1, length), lambda i: (i, 0, 0, 0))],
        out_shape=[shape((width, length), BF16), shape((pairs, 2, 1, length), F32)],
        scratch_shapes=[pltpu.VMEM((length, PAIR), BF16), pltpu.VMEM((2, PAIR, length), BF16)],
        compiler_params=params(),
        cost_estimate=cost(16 * length * length * width, 8e6),
        name="attend",
    )(q_t, k, v_t, doc_row, doc_col)


def load_out_weight(me, vo, refs, buf, sems):
    rows = buf.shape[0] // vo.count
    copies = [
        pltpu.make_async_copy(
            block.at[pl.ds(rows, rows), :], buf.at[pl.ds(row_at(me, j, rows), rows), :], sems.at[n]
        )
        for block, j, n in vo.blocks(refs)
    ]
    start_all(copies)
    return copies


def middle_kernel(vo, me, *refs):
    x_refs, g_refs, refs = refs[:4], refs[4:8], refs[8:]
    (mix_t, vec), refs = refs[:2], refs[2:]
    mul, add = norm_scale(vec, GAIN_2, SCALE_2), vec_row(vec, SHIFT_2)
    gate_one, gate_two = vec_row(vec, GATE_1), vec_row(vec, GATE_2)
    pieces, refs = refs[: len(vo.parts)], refs[len(vo.parts) :]
    (att, n_two, n_two_t, d_down, d_down_t, d_bias, mix), (w_buf, x_buf, sems) = refs[:7], refs[7:]
    copies = load_out_weight(me, vo, pieces, w_buf, sems)
    scaled = pick(g_refs, x_buf) * gate_two
    add_row(d_bias, 0, jnp.sum(scaled, axis=0, keepdims=True))
    scaled = scaled.astype(BF16)
    d_down[...] = scaled
    d_down_t[...] = scaled.T
    wait_all(copies)
    mixture = mix_t[...].T
    mix[...] = mixture
    attention = dot_nt(mixture, w_buf[...])
    att[...] = attention
    mid = pick(x_refs, x_buf) + gate_one * attention
    centred = mid - jnp.mean(mid, axis=-1, keepdims=True)
    spread = jnp.mean(centred * centred, axis=-1, keepdims=True)
    normed = (centred * lax.rsqrt(spread + EPSILON) * mul + add).astype(BF16)
    n_two[...] = normed
    n_two_t[...] = normed.T


def middle(me, x_parts, g_parts, mix_t, vec, vo):
    part, width = x_parts[0].shape
    length = 4 * part
    inner = mix_t.shape[0]
    flat, turned = shape((length, width), BF16), shape((width, length), BF16)
    return pl.pallas_call(
        partial(middle_kernel, vo),
        grid=(4,),
        out_shape=[shape((length, width), F32), flat, turned, flat, turned]
        + [shape((1, width), F32), shape((length, inner), BF16)],
        in_specs=[SMEM]
        + [VMEM] * 8
        + [col_block(inner, part), VMEM]
        + [ANY] * len(vo.parts),
        out_specs=[
            row_block(part, width),
            row_block(part, width),
            col_block(width, part),
            row_block(part, width),
            col_block(width, part),
            VMEM,
            row_block(part, inner),
        ],
        scratch_shapes=[
            pltpu.VMEM((width, inner), BF16),
            pltpu.VMEM((part, width), BF16),
            pltpu.SemaphoreType.DMA((vo.count,)),
        ],
        compiler_params=params(),
        cost_estimate=cost(2 * length * width * inner, 16e6),
        name="middle",
    )(me, *x_parts, *g_parts, mix_t, vec, *vo.parts)


def spread_rows(me, value, stage, keep, send=None):
    blocks, rows = stage.shape[0], stage.shape[1]
    for j in range(blocks):
        stage[j] = value[j * rows : (j + 1) * rows, :].astype(BF16)
    for j in range(blocks):
        block = stage[me[0] ^ j]
        if j % 2 == 0:
            keep(j // 2, block)
        else:
            send(j // 2, block)


def writer(ref, *lead):
    def put(slot, block):
        ref[(lead[0], slot, *lead[1:])] = block

    return put


def split_writer(ref, *lead):
    def put(slot, block):
        half = block.shape[-1] // 2
        for s in range(2):
            ref[(s, slot, *lead)] = block[:, s * half : (s + 1) * half]

    return put


C_ROOT = 0.7978845608028654
C_CUBE = 0.044715


def feed_kernel(up, dn, steps, first, me, *refs):
    (n_two, n_two_t, d_down, d_down_t, bias), refs = refs[:5], refs[5:]
    if not first:
        (down_in, d_n_in), refs = refs[:2], refs[2:]
    parts = len(up.parts)
    up_refs, down_refs, refs = refs[:parts], refs[parts : 2 * parts], refs[2 * parts :]
    (down, d_n, d_bias, *grads), (w_buf, stage, sems) = refs[:-3], refs[-3:]
    step = pl.program_id(0)
    rows = up_refs[0].shape[1]
    chunk = w_buf.shape[3]
    offset = 0 if first else steps * chunk

    def copies(s):
        out = []
        for m, (held, group) in enumerate(((up, up_refs), (dn, down_refs))):
            for block, j, n in held.blocks(group):
                out.append(
                    pltpu.make_async_copy(
                        block.at[:, pl.ds(offset + s * chunk, chunk)],
                        w_buf.at[m, s, pl.ds(row_at(me, j, rows), rows), :],
                        sems.at[m, s, n],
                    )
                )
        return out

    @pl.when(step == 0)
    def _():
        for s in range(steps):
            for copy in copies(s):
                copy.start()
        if first:
            down[...] = jnp.zeros_like(down)
            d_n[...] = jnp.zeros_like(d_n)
        else:
            down[...] = down_in[...]
            d_n[...] = d_n_in[...]

    for s in range(steps):

        @pl.when(step == s)
        def _():
            for copy in copies(s):
                copy.wait()

    w_up = w_buf[0, step]
    w_down_t = w_buf[1, step]
    h = dot_nn(n_two[...], w_up) + bias[0]
    square = h * h
    t = jnp.tanh(C_ROOT * h * (1.0 + C_CUBE * square))
    half = 0.5 + 0.5 * t
    act = (h * half).astype(BF16)
    slope = half + (0.5 * C_ROOT) * h * (1.0 - t * t) * (1.0 + (3.0 * C_CUBE) * square)
    d_h = (dot_nn(d_down[...], w_down_t) * slope).astype(BF16)
    d_bias[0] = jnp.sum(d_h.astype(F32), axis=0, keepdims=True)
    down[...] += dot_nt(act, w_down_t)
    d_n[...] += dot_nt(d_h, w_up)
    for m, grad in ((0, dot_nn(n_two_t[...], d_h)), (1, dot_nn(d_down_t[...], act))):
        spread_rows(me, grad, stage, *(writer(ref, m) for ref in grads))


def feed(me, n_two, n_two_t, d_down, d_down_t, bias, up, dn, start, before, units):
    blocks = up.count
    length, width = n_two.shape
    chunk = 512 if units % 512 == 0 else units
    steps = units // chunk
    first = before is None
    rows = width // blocks
    one = pl.Buffered(1)
    flat = pl.BlockSpec((length, width), lambda i: (0, 0), pipeline_mode=one)
    turned = pl.BlockSpec((width, length), lambda i: (0, 0), pipeline_mode=one)
    held = pl.BlockSpec((length, width), lambda i: (0, 0))
    half = max(blocks // 2, 1)
    grad = pl.BlockSpec((2, half, rows, chunk), lambda i: (0, 0, 0, i))
    grads = 1 if blocks == 1 else 2
    bias_spec = pl.BlockSpec((1, 1, chunk), lambda i: (i + start // chunk, 0, 0))
    return pl.pallas_call(
        partial(feed_kernel, up, dn, steps, first),
        grid=(steps,),
        in_specs=[SMEM, flat, turned, flat, turned, bias_spec]
        + ([] if first else [flat, flat])
        + [ANY] * (2 * len(up.parts)),
        out_specs=[held, held, pl.BlockSpec((1, 1, chunk), lambda i: (i, 0, 0))] + [grad] * grads,
        out_shape=[shape((length, width), F32)] * 2
        + [shape((steps, 1, chunk), F32)]
        + [shape((2, half, rows, units), BF16)] * grads,
        scratch_shapes=[
            pltpu.VMEM((2, steps, width, chunk), BF16),
            pltpu.VMEM((blocks, rows, chunk), BF16),
            pltpu.SemaphoreType.DMA((2, steps, blocks)),
        ],
        compiler_params=params(),
        cost_estimate=cost(12 * length * width * units, 20e6),
        name="feed",
    )(
        me,
        n_two,
        n_two_t,
        d_down,
        d_down_t,
        bias.reshape(-1, 1, chunk),
        *(() if first else before),
        *up.parts,
        *dn.parts,
    )


def turn_kernel(vo, me, *refs):
    x_refs, g_refs, refs = refs[:4], refs[4:8], refs[8:]
    (att, down, d_n, vec), refs = refs[:4], refs[4:]
    mul, bias = norm_scale(vec, GAIN_2, SCALE_2), vec_row(vec, BIAS_OUT)
    gate_one, gate_two = vec_row(vec, GATE_1), vec_row(vec, GATE_2)
    pieces, refs = refs[: len(vo.parts)], refs[len(vo.parts) :]
    out_refs, (d_mid, d_mix_t, sums, d_att_t), (w_buf, x_buf, sems) = (
        refs[:4],
        refs[4:8],
        refs[8:],
    )
    copies = load_out_weight(me, vo, pieces, w_buf, sems)
    g = pick(g_refs, x_buf)
    attention = att[...]
    mid = pick(x_refs, x_buf) + gate_one * attention
    branch = down[...] + bias
    put(out_refs, (mid + gate_two * branch).astype(BF16))
    centred = mid - jnp.mean(mid, axis=-1, keepdims=True)
    inverse = lax.rsqrt(jnp.mean(centred * centred, axis=-1, keepdims=True) + EPSILON)
    unit = centred * inverse
    dn = d_n[...]
    dn_unit = dn * unit
    du = dn * mul
    dm = g + inverse * (
        du
        - jnp.mean(du, axis=-1, keepdims=True)
        - unit * jnp.mean(dn_unit * mul, axis=-1, keepdims=True)
    )
    d_mid[...] = dm
    for n, term in enumerate((g * branch, dn_unit, dn, dm * attention)):
        add_row(sums, n, jnp.sum(term, axis=0, keepdims=True))
    d_att = (dm * gate_one).astype(BF16)
    d_att_t[...] = d_att.T
    wait_all(copies)
    d_mix_t[...] = dot_nn(d_att, w_buf[...]).astype(BF16).T


def turn(me, x_parts, g_parts, att, down, d_n, vec, vo):
    part, width = x_parts[0].shape
    length = 4 * part
    inner = vo.parts[0].shape[2]
    return pl.pallas_call(
        partial(turn_kernel, vo),
        grid=(4,),
        out_shape=[shape((part, width), BF16)] * 4
        + [
            shape((length, width), F32),
            shape((inner, length), BF16),
            shape((4, width), F32),
            shape((width, length), BF16),
        ],
        in_specs=[SMEM]
        + [VMEM] * 8
        + [row_block(part, width)] * 3
        + [VMEM]
        + [ANY] * len(vo.parts),
        out_specs=[VMEM] * 4
        + [
            row_block(part, width),
            col_block(inner, part),
            VMEM,
            col_block(width, part),
        ],
        scratch_shapes=[
            pltpu.VMEM((width, inner), BF16),
            pltpu.VMEM((part, width), BF16),
            pltpu.SemaphoreType.DMA((vo.count,)),
        ],
        compiler_params=params(),
        cost_estimate=cost(2 * length * width * inner, 24e6),
        name="turn",
    )(
        me, *x_parts, *g_parts, att, down, d_n, vec, *vo.parts
    )


def attend_back_kernel(
    k, v, q_t, k_t, d_mix_t, mix_t, log_sum, doc_row, doc_col, cos_t, sin_t,
    dq, dk, dv, added, ahead, dq_acc, dk_acc, dv_acc,
):
    @pl.when(pl.program_id(0) == 0)
    def _():
        added_lanes(added, doc_col)

    length = k.shape[0]
    block = 256 if length % 256 == 0 else length
    docs = document_rows(doc_row)
    for h in range(2):
        rows = slice(h * HEAD, (h + 1) * HEAD)
        row_dot = jnp.sum(
            d_mix_t[rows, :].astype(F32) * mix_t[rows, :].astype(F32), axis=0, keepdims=True
        )
        with_rows(ahead.at[h, 0], q_t, h, [docs, three_terms(-log_sum[0, h])])
        with_rows(ahead.at[h, 1], d_mix_t, h, [None, three_terms(-row_dot)])

    for h in range(2):
        rows = slice(h * HEAD, (h + 1) * HEAD)
        keys, values = with_lanes(k, added, h), with_lanes(v, added, h)
        for b in range(length // block):
            c = slice(b * block, (b + 1) * block)
            probs = jnp.exp(dot_nn(keys, ahead[h, 0, :, c]))
            d_scores = (probs * dot_nn(values, ahead[h, 1, :, c])).astype(BF16)
            dv_part = dot_nt(d_mix_t[rows, c], probs.astype(BF16))
            dk_part = dot_nt(q_t[rows, c], d_scores)
            if b == 0:
                dv_acc[rows, :] = dv_part
                dk_acc[rows, :] = dk_part
            else:
                dv_acc[rows, :] += dv_part
                dk_acc[rows, :] += dk_part
            dq_acc[rows, c] = dot_nn(k_t[rows, :], d_scores)

    half = HEAD // 2
    for acc, out, factor in ((dq_acc, dq, HEAD**-0.5), (dk_acc, dk, 1.0)):
        turned = []
        for h in range(2):
            a = acc[h * HEAD : h * HEAD + half, :] * factor
            b = acc[h * HEAD + half : (h + 1) * HEAD, :] * factor
            turned.append(a * cos_t[...] + b * sin_t[...])
            turned.append(b * cos_t[...] - a * sin_t[...])
        out[...] = jnp.concatenate(turned, axis=0).astype(BF16).T
    dv[...] = dv_acc[...].astype(BF16).T


def attend_back(k, v, q_t, k_t, d_mix_t, mix_t, log_sum, doc_row, doc_col, cos_t, sin_t):
    length, width = k.shape
    count = width // PAIR
    flat = pl.BlockSpec((length, PAIR), lambda i: (0, i))
    turned = pl.BlockSpec((PAIR, length), lambda i: (i, 0))
    fixed = lambda a: pl.BlockSpec(a.shape, lambda i: (0, 0))
    return pl.pallas_call(
        attend_back_kernel,
        grid=(count,),
        in_specs=[flat] * 2
        + [turned] * 4
        + [pl.BlockSpec((1, 2, 1, length), lambda i: (i, 0, 0, 0))]
        + [fixed(a) for a in (doc_row, doc_col, cos_t, sin_t)],
        out_specs=[flat] * 3,
        out_shape=[shape((length, width), BF16)] * 3,
        scratch_shapes=[
            pltpu.VMEM((length, PAIR), BF16),
            pltpu.VMEM((2, 2, PAIR, length), BF16),
        ]
        + [pltpu.VMEM((PAIR, length), F32)] * 3,
        compiler_params=params(),
        cost_estimate=cost(28 * length * length * width, 14e6),
        name="attend_back",
    )(k, v, q_t, k_t, d_mix_t, mix_t, log_sum, doc_row, doc_col, cos_t, sin_t)


def first_kernel(qk, vo, me, *refs):
    x_refs, refs = refs[:4], refs[4:]
    (d_mid, vec, dq, dk, dv), refs = refs[:5], refs[5:]
    mul = norm_scale(vec, GAIN_1, SCALE_1)
    held, refs = refs[: 2 * len(qk.parts)], refs[2 * len(qk.parts) :]
    out_refs, (sums, w_buf, x_buf, sems) = refs[:4], refs[4:]
    copies = qkv_copies(me, qk, vo, held, w_buf, sems, w_buf.shape[1] // qk.count)
    start_all(copies)
    x = pick(x_refs, x_buf)
    centred = x - jnp.mean(x, axis=-1, keepdims=True)
    inverse = lax.rsqrt(jnp.mean(centred * centred, axis=-1, keepdims=True) + EPSILON)
    unit = centred * inverse
    wait_all(copies)
    dn = dot_nt(dq[...], w_buf[0]) + dot_nt(dk[...], w_buf[1]) + dot_nt(dv[...], w_buf[2])
    dn_unit = dn * unit
    du = dn * mul
    put(
        out_refs,
        (
            d_mid[...]
            + inverse
            * (
                du
                - jnp.mean(du, axis=-1, keepdims=True)
                - unit * jnp.mean(dn_unit * mul, axis=-1, keepdims=True)
            )
        ).astype(BF16),
    )
    for n, term in enumerate((dn_unit, dn)):
        add_row(sums, n, jnp.sum(term, axis=0, keepdims=True))


def first(me, x_parts, d_mid, vec, dq, dk, dv, qk, vo):
    part, width = x_parts[0].shape
    length = 4 * part
    cols = dq.shape[1]
    return pl.pallas_call(
        partial(first_kernel, qk, vo),
        grid=(4,),
        out_shape=[shape((part, width), BF16)] * 4 + [shape((2, width), F32)],
        in_specs=[SMEM]
        + [VMEM] * 4
        + [row_block(part, width), VMEM]
        + [row_block(part, cols)] * 3
        + [ANY] * (2 * len(qk.parts)),
        out_specs=[VMEM] * 5,
        scratch_shapes=[
            pltpu.VMEM((3, width, cols), BF16),
            pltpu.VMEM((part, width), BF16),
            pltpu.SemaphoreType.DMA((3, qk.count)),
        ],
        compiler_params=params(),
        cost_estimate=cost(6 * length * width * cols, 20e6),
        name="first",
    )(me, *x_parts, d_mid, vec, dq, dk, dv, *qk.parts, *vo.parts)


def modulate_kernel(qk, vo, zones, me, act, *refs):
    parts = len(qk.parts)
    qk_refs, vo_refs, (vec, bias, ada, small, sems) = refs[:parts], refs[parts:-5], refs[-5:]
    count = qk.count
    rows = ada.shape[0] // count
    cut = rows // 2
    copies = []
    for h, (held, group) in enumerate(((qk, qk_refs), (vo, vo_refs))):
        for block, j, n in held.blocks(group):
            at = row_at(me, j, rows) + h * cut
            copies.append(
                pltpu.make_async_copy(
                    block.at[pl.ds(2 * rows, cut), :], ada.at[pl.ds(at, cut), :], sems.at[h, n]
                )
            )
            if h:
                copies.append(
                    pltpu.make_async_copy(
                        block.at[pl.ds(2 * rows + cut, 16), :],
                        small.at[pl.ds(row_at(me, j, 16), 16), :],
                        sems.at[2, n],
                    )
                )
    for copy in copies:
        copy.start()
    for copy in copies:
        copy.wait()
    kinds = ada.shape[1] // act.shape[1]
    act3 = three_terms(act[...])
    across = vec.shape[1] // rows
    vec[...] = jnp.zeros_like(vec)
    for k in range(kinds):
        lanes = slice(k * act.shape[1], (k + 1) * act.shape[1])
        found = jnp.sum(dot_nt(act3, ada[:, lanes]), axis=0, keepdims=True)
        for d in range(count):
            m = d * kinds + k
            at = (m % across) * rows
            extra = small[d * 16 : (d + 1) * 16, :].astype(F32)
            vec[m // across : m // across + 1, at : at + rows] = (
                found[:, d * rows : (d + 1) * rows] + extra[1:2, k * rows : (k + 1) * rows]
            )
    for d in range(count):
        extra = small[d * 16 : (d + 1) * 16, :].astype(F32)
        here = slice(d * rows, (d + 1) * rows)
        for n in range(3):
            vec[BIAS_OUT + n : BIAS_OUT + n + 1, here] = extra[2:3, n * rows : (n + 1) * rows]
        for n in range(zones):
            far = (n - zones // 2) % zones
            at = n * (extra.shape[1] // zones)
            bias[far : far + 1, here] = extra[0:1, at : at + rows]


def modulate(me, act, qk, vo, zones, rows):
    width = qk.parts[0].shape[2]
    return pl.pallas_call(
        partial(modulate_kernel, qk, vo, zones),
        out_shape=[
            shape((16, width), F32),
            shape((zones, width), F32),
            shape((qk.count * rows, width), BF16),
        ],
        in_specs=[SMEM, VMEM] + [ANY] * (len(qk.parts) + len(vo.parts)),
        out_specs=[VMEM] * 3,
        scratch_shapes=[
            pltpu.VMEM((qk.count * 16, width), BF16),
            pltpu.SemaphoreType.DMA((3, qk.count)),
        ],
        compiler_params=params(),
        cost_estimate=cost(2e7, 4e6),
        name="modulate",
    )(me, act, *qk.parts, *vo.parts)


def gather_up_kernel(
    count, me, vec, ada, sums, sums_one, d_bias_down, bias_grad, act, cond, keep, send, d_cond, out, spread
):
    width = vec.shape[1]
    rows = width // count
    size = act.shape[1]
    kinds = ada.shape[1] // size
    norm_1, norm_2 = sums_one[0:1, :], sums[1:2, :]
    d_mod = (
        sums_one[1:2, :],
        norm_1 * vec_row(vec, GAIN_1),
        sums[3:4, :],
        sums[2:3, :],
        norm_2 * vec_row(vec, GAIN_2),
        sums[0:1, :],
    )
    others = (
        norm_1 * (1.0 + vec_row(vec, SCALE_1)),
        norm_2 * (1.0 + vec_row(vec, SCALE_2)),
        d_bias_down[...],
    )
    out[...] = jnp.zeros_like(out)
    base = (kinds + 3) * rows
    for d in range(count):
        here = slice(d * rows, (d + 1) * rows)
        for k in range(kinds):
            m = d * kinds + k
            at = (m % count) * rows
            piece = d_mod[m // count][:, at : at + rows]
            out[d, :, k * rows : (k + 1) * rows] = piece
            spread[k : k + 1, here] = piece
        for n, value in enumerate(others):
            at = (kinds + n) * rows
            out[d, :, at : at + rows] = value[:, here]
        for n in range(bias_grad.shape[0]):
            at = base + n * rows
            out[d, :, at : at + rows] = bias_grad[n : n + 1, here]
        out[d, :, out.shape[2] - size :] = act[...]
    total = jnp.zeros(act.shape, F32)
    for k in range(kinds):
        three = three_terms(spread[k : k + 1, :])
        total += jnp.sum(dot_nn(three, ada[:, k * size : (k + 1) * size]), axis=0, keepdims=True)
    c = cond[...]
    sig = 1.0 / (1.0 + jnp.exp(-c))
    d_cond[...] = total * (sig * (1.0 + c * (1.0 - sig)))

    for j in range(count // 2):
        keep[j] = out[me[0] ^ (2 * j)]
        send[j] = out[me[0] ^ (2 * j + 1)]


def gather_up(me, vec, ada, sums, sums_one, d_bias_down, bias_grad, act, cond, count, length):
    return pl.pallas_call(
        partial(gather_up_kernel, count),
        out_shape=[shape((count // 2, 1, length), F32)] * 2 + [shape(act.shape, F32)],
        in_specs=[SMEM] + [VMEM] * 8,
        out_specs=[VMEM] * 3,
        scratch_shapes=[
            pltpu.VMEM((count, 1, length), F32),
            pltpu.VMEM((8, vec.shape[1]), F32),
        ],
        compiler_params=params(),
        cost_estimate=cost(2e7, 4e6),
        name="gather_up",
    )(me, vec, ada, sums, sums_one, d_bias_down, bias_grad, act, cond)


def weight_grads_kernel(me, n_t, d_att_t, dq, dk, dv, mix_t, *refs):
    *grads, left, right, stage, sems = refs
    copies = [
        pltpu.make_async_copy(ref, held, sems.at[n])
        for n, (ref, held) in enumerate(
            (
                (n_t, left.at[0]),
                (dq, right.at[0]),
                (dk, right.at[1]),
                (dv, right.at[2]),
                (d_att_t, left.at[1]),
                (mix_t, right.at[3]),
            )
        )
    ]
    start_all(copies)
    wait_all(copies[:2])
    at_step(1, copies[2].wait)
    at_step(2, copies[3].wait)

    def last():
        copies[4].wait()
        copies[5].wait()

    at_step(3, last)
    step = pl.program_id(0)
    grad = dot_nn(left[jnp.where(step == 3, 1, 0)], right[step])
    spread_rows(me, grad, stage, *(split_writer(ref, 0) for ref in grads))


def weight_grads(me, n_t, d_att_t, dq, dk, dv, mix, blocks):
    width, length = n_t.shape
    cols = dq.shape[1]
    rows = width // blocks
    half = max(blocks // 2, 1)
    grads = 1 if blocks == 1 else 2
    return pl.pallas_call(
        weight_grads_kernel,
        grid=(4,),
        out_shape=[shape((2, half, 4, rows, cols // 2), BF16)] * grads,
        in_specs=[SMEM] + [ANY] * 6,
        out_specs=[
            pl.BlockSpec((2, half, 1, rows, cols // 2), lambda i: (0, 0, i, 0, 0))
        ]
        * grads,
        scratch_shapes=[
            pltpu.VMEM((2, width, length), BF16),
            pltpu.VMEM((4, length, cols), BF16),
            pltpu.VMEM((blocks, rows, cols), BF16),
            pltpu.SemaphoreType.DMA((6,)),
        ],
        compiler_params=params(),
        cost_estimate=cost(8 * length * width * cols, 14e6),
        name="weight_grads",
    )(me, n_t, d_att_t, dq, dk, dv, mix)


class Group:
    def __init__(self, dp_count, tensor_count, per_dp):
        self.dp, self.tensor, self.per_dp = dp_count, tensor_count, per_dp
        self.d, self.r = lax.axis_index("dp"), lax.axis_index("tensor")
        self.paired = dp_count == 8

    def bit(self, v, b):
        return lax.ppermute(v, "dp", [(i, i ^ (1 << b)) for i in range(self.dp)])

    def step(self, v, k):
        return lax.ppermute(v, "dp", [(i, i ^ k) for i in range(self.dp)])

    def z(self, v, k):
        return lax.ppermute(v, "tensor", [(i, i ^ k) for i in range(self.tensor)])

    def owns(self, d, r):
        return 0 <= r - d % 2 < self.per_dp

    def for_owner(self, rows, zero_idle):
        mine = self.r - self.d % 2
        top = self.per_dp - 1
        own = lax.dynamic_index_in_dim(rows, jnp.clip(mine, 0, top), 0, keepdims=False)
        if zero_idle:
            own = jnp.where((mine >= 0) & (mine <= top), own, jnp.zeros_like(own))
        parts = [own]
        for k in range(1, self.tensor):
            want = (self.r ^ k) - self.d % 2
            parts.append(
                lax.dynamic_index_in_dim(rows, jnp.clip(want, 0, top), 0, keepdims=False)
            )
        return parts

    def ship(self, v, k, to_owner):
        pairs = [
            (d * self.tensor + r, d * self.tensor + (r ^ k))
            for d in range(self.dp)
            for r in range(self.tensor)
            if self.owns(d, r ^ k if to_owner else r)
        ]
        return lax.ppermute(v, BOTH, pairs)

    def held_rows(self, came):
        stack = jnp.stack(came)
        return jnp.stack(
            [
                lax.dynamic_index_in_dim(stack, self.r ^ (j + self.d % 2), 0, keepdims=False)
                for j in range(self.per_dp)
            ]
        )

    def z_pair(self, v, got):
        return jnp.concatenate([v, got], axis=-1)

    def gather_pair(self, v, got, order):
        pair = jnp.stack([v, got])
        return [pair, self.bit(pair, order[1])]

    def gather_cores(self, parts, order):
        one, two = (1 << b for b in order)
        rels = [(0, one), (two, one ^ two)]
        rels += [tuple(j ^ 1 for j in rel) for rel in rels]
        return Held(parts + [self.bit(p, 0) for p in parts], rels)

    def gather_cores_joined(self, pairs, orders):
        near = jnp.concatenate([p for pair in pairs for p in pair])
        far = self.bit(near, 0)
        held = []
        for n, order in enumerate(orders):
            one, two = (1 << b for b in order)
            rel = (0, one, two, one ^ two)
            held.append(Held([near, far], [rel, tuple(j ^ 1 for j in rel)], 4 * n))
        return held

    def whole(self, v, axis):
        return lax.all_gather(v, "dp", axis=axis, tiled=True)


class Flight:
    def __init__(self, value):
        self.value = value


class Sum:
    def __init__(self, group, keep, send=None):
        self.group, self.stage, self.flights, self.terms = group, 0, [], []
        if not group.paired:
            value = keep[:, 0].astype(F32)
            value = lax.psum_scatter(value, "dp", scatter_dimension=value.ndim - 2, tiled=True)
            self.total = [value[0], value[1]]
            return
        self.terms = [[keep], [keep]]
        flight = Flight(group.bit(send, 0))
        self.flights = [(flight, 0), (flight, 1)]

    def settle(self):
        for terms, (flight, at) in zip(self.terms, self.flights):
            terms.append(flight.value if self.stage == 0 else flight.value[at])
        if self.flights and self.stage == 2:
            self.total = [sum(t[0].astype(F32) for t in terms) for terms in self.terms]
        self.flights = []

    def split(self):
        out = []
        for n, order in enumerate(((1, 2), (2, 1))):
            b = order[self.stage]
            if self.stage:
                stay, go = [t[:1] for t in self.terms[n]], [t[1:] for t in self.terms[n]]
            else:
                sides = [t.reshape(2, 2, 2, *t.shape[2:]) for t in self.terms[n]]
                if b == 1:
                    stay, go = [t[n, :, 0] for t in sides], [t[n, :, 1] for t in sides]
                else:
                    stay, go = [t[n, 0] for t in sides], [t[n, 1] for t in sides]
            self.terms[n] = stay
            out.append((b, sum(t.astype(F32) for t in go).astype(BF16)))
        self.stage += 1
        self.flights = [None, None]
        return out


def exchange(*sums):
    links = {}
    for t in sums:
        t.settle()
        if t.group.paired:
            for n, (b, go) in enumerate(t.split()):
                links.setdefault(b, []).append((t, n, go))
    for b, items in links.items():
        blocks = [go for _, _, go in items]
        blocks = blocks[0] if len(blocks) == 1 else jnp.concatenate(blocks)
        flight, at = Flight(items[0][0].group.bit(blocks, b)), 0
        for t, n, go in items:
            t.flights[n] = (flight, slice(at, at + go.shape[0]))
            at += go.shape[0]


def tie(value, *sums):
    flights = {id(f): f for t in sums for f, _ in t.flights}
    flights = list(flights.values())
    value, arrived = lax.optimization_barrier((value, [f.value for f in flights]))
    for flight, v in zip(flights, arrived):
        flight.value = v
    return value


def silu_slope(c):
    sig = jax.nn.sigmoid(c)
    return sig * (1.0 + c * (1.0 - sig))


def shards(
    inputs, condition, doc_ids, positions, w_qkv, w_out, w_up, bias_up, w_down, bias_down,
    gain_one, gain_two, w_ada, bias_ada, out_grad,
):
    dp_count = lax.axis_size("dp")
    tensor_count = lax.axis_size("tensor")
    per_dp, part, width = inputs.shape
    length = doc_ids.shape[1]
    rows = w_up.shape[0]
    group = Group(dp_count, tensor_count, per_dp)
    blocks = dp_count if group.paired else 1
    d, r = group.d, group.r
    me = jnp.where(group.paired, d, 0).astype(jnp.int32).reshape(1)
    mine = jnp.clip(r - d % 2, 0, per_dp - 1)
    own_row = lambda v: lax.dynamic_index_in_dim(v, mine, 0, keepdims=False)
    join = lambda parts: jnp.concatenate(parts, axis=-1)

    order = r ^ jnp.arange(tensor_count)
    mixed = lambda v: own_row(v).reshape(tensor_count, part)[order].reshape(-1)
    docs, places = mixed(doc_ids), mixed(positions)
    doc_row, doc_col = docs[None, :], docs[:, None]
    frequencies = 10000.0 ** (-2.0 * jnp.arange(HEAD // 2, dtype=F32) / HEAD)
    cos_flat, sin_a, sin_b, cos_t, sin_t = rotary(
        places.astype(F32)[None, :], frequencies[:, None]
    )

    cols, cond_size, mod_width = w_qkv.shape[2], w_ada.shape[0], w_ada.shape[1]
    ways = (1, 2), (2, 1)
    cond = own_row(condition).astype(F32)[None]
    act = jax.nn.silu(cond)
    early = jnp.concatenate([w_qkv.reshape(-1, cols), w_out.T])
    late = jnp.concatenate([w_up, w_down.T])
    if group.paired:
        early = jnp.concatenate([early, jnp.pad(bias_up, ((0, 15), (0, cols - rows)))])
    if group.paired:
        ada = w_ada.T.reshape(-1, rows, cond_size).transpose(1, 0, 2).reshape(rows, width)
        cut, top = rows // 2, 2 * rows
        wide = lambda v: jnp.pad(v, (0, width - v.shape[0]))[None]
    x_parts, g_parts = group.for_owner(inputs, False), group.for_owner(out_grad, True)
    early = group.z_pair(early, group.z(early, 2))
    early = join([early, group.z(early, 1)])
    turns = cos_flat, sin_a, sin_b, cos_t, sin_t, doc_row, doc_col
    late, early, x_parts, g_parts = lax.optimization_barrier((late, early, x_parts, g_parts))
    late_got = group.z(late, 2)
    if group.paired:
        small = jnp.concatenate(
            [
                early[2 * top : 2 * top + 1],
                wide(bias_ada),
                wide(jnp.concatenate([bias_down, gain_one, gain_two])),
                early[2 * top + 3 :],
            ]
        )
        firsts = (
            jnp.concatenate([early[:top], ada[:cut], jnp.zeros_like(small)]),
            jnp.concatenate([early[top : 2 * top], ada[cut:], small]),
        )
        came = [group.bit(v, way[0]) for v, way in zip(firsts, ways)]
        late_got, came = lax.optimization_barrier((late_got, came))
        late = group.z_pair(late, late_got)
        late_far = group.z(late, 1)
        near = [group.gather_pair(v, got, way) for v, got, way in zip(firsts, came, ways)]
        x_parts[2] = group.ship(x_parts[2], 2, True)
        late_far, near, x_parts, turns = lax.optimization_barrier((late_far, near, x_parts, turns))
        cos_flat, sin_a, sin_b, cos_t, sin_t, doc_row, doc_col = turns
        for n in (3, 1):
            x_parts[n] = group.ship(x_parts[n], n, True)
        late = join([late_far, late])
        qk, vo = group.gather_cores_joined(near, ways)
        lates = late[:rows], late[rows:]
        came = [group.bit(v, way[0]) for v, way in zip(lates, ways)]
        vec, bias_hidden, ada_all = modulate(me, act, qk, vo, tensor_count, rows)
        x_parts, g_parts, came, vec = lax.optimization_barrier((x_parts, g_parts, came, vec))
        for n in range(1, tensor_count):
            g_parts[n] = group.ship(g_parts[n], n, True)
        near = [group.gather_pair(v, got, way) for v, got, way in zip(lates, came, ways)]
    else:
        for n in range(1, tensor_count):
            x_parts[n] = group.ship(x_parts[n], n, True)
            g_parts[n] = group.ship(g_parts[n], n, True)
        late = group.z_pair(late, late_got)
        late = join([group.z(late, 1), late])
        flat = lambda v: group.whole(v.reshape(2, rows, width), 1).reshape(1, 2 * width, width)
        qk, vo = Held([flat(early[: 2 * rows])], [(0,)]), Held([flat(early[2 * rows :])], [(0,)])
        up, dn = (Held([group.whole(v, 0)[None]], [(0,)]) for v in (late[:rows], late[rows:]))
        w_all = group.whole(w_ada, 1)
        modulation = jnp.dot(
            act, w_all.astype(F32), precision=PRECISE, preferred_element_type=F32
        ) + group.whole(bias_ada, 0).astype(F32)
        small = group.whole(jnp.stack([bias_down, gain_one, gain_two]), 1).astype(F32)
        vec = jnp.concatenate([modulation.reshape(6, width), small, jnp.zeros((7, width), F32)])
        bias_hidden = group.whole(bias_up, 1)
        bias_hidden = jnp.concatenate([group.z(bias_hidden, k) for k in (1, 3, 0, 2)]).astype(F32)

    n_t, k, v, q_t, k_t, v_t = qkv(me, x_parts, vec, cos_flat, sin_a, sin_b, qk, vo)
    mix_t, log_sum = attend(q_t, k, v_t, doc_row, doc_col)
    if group.paired:
        mix_t, near, g_parts = lax.optimization_barrier((mix_t, near, g_parts))
        up, dn = (group.gather_cores(p, way) for p, way in zip(near, ways))
    att, n_two, n_two_t, d_down, d_down_t, d_bias_down, mix = middle(
        me, x_parts, g_parts, mix_t, vec, vo
    )
    size = w_up.shape[1]
    feed_args = (me, n_two, n_two_t, d_down, d_down_t, bias_hidden, up, dn)

    down, d_n, d_bias_a, *grads = feed(*feed_args, 0, None, 2 * size)
    sum_a = Sum(group, *grads)
    down, d_n, d_bias_b, *grads = feed(*feed_args, 2 * size, (down, d_n), 2 * size)
    down = tie(down, sum_a)
    exchange(sum_a)
    sum_b = Sum(group, *grads)
    *out_parts, d_mid, d_mix_t, sums, d_att_t = turn(
        me, x_parts, g_parts, att, down, d_n, vec, vo
    )
    d_mix_t, out_parts = tie((d_mix_t, out_parts), sum_a, sum_b)
    came = out_parts[:1] + [group.ship(out_parts[n], n, False) for n in range(1, tensor_count)]
    exchange(sum_a, sum_b)
    dq, dk, dv = attend_back(
        k, v, q_t, k_t, d_mix_t, mix_t, log_sum, doc_row, doc_col, cos_t, sin_t
    )
    dq, came = tie((dq, came), sum_a, sum_b)
    block_out = group.held_rows(came)
    sum_a.settle()
    exchange(sum_b)
    far_up = group.z(sum_a.total[0].astype(BF16), 1)
    grads = weight_grads(me, n_t, d_att_t, dq, dk, dv, mix, blocks)
    d_mid, grads, far_up, last = tie((d_mid, grads, far_up, sum_a.total[1]), sum_b)
    far_dn = group.z(last.astype(BF16), 1)
    sum_w = Sum(group, *grads)
    *in_parts, sums_one = first(me, x_parts, d_mid, vec, dq, dk, dv, qk, vo)

    in_parts, far_dn = tie((in_parts, far_dn), sum_w)
    exchange(sum_w)
    came = in_parts[:1] + [group.ship(in_parts[n], n, False) for n in range(1, tensor_count)]
    sum_b.settle()
    near = jnp.stack(sum_b.total) + jnp.stack([far_up, far_dn]).astype(F32)
    sums_one, near = tie((sums_one, near), sum_w)
    exchange(sum_w)
    d_bias = jnp.concatenate([d_bias_b.reshape(2, -1), d_bias_a.reshape(2, -1)])
    edge = mod_width + 3 * rows
    if group.paired:
        length = edge + tensor_count * rows + 2 * cond_size
        keep, send, d_cond = gather_up(
            me, vec, ada_all, sums, sums_one, d_bias_down, d_bias, act, cond, dp_count,
            length - length % cond_size,
        )
    else:
        d_gate_2, norm_2, d_shift_2, d_gate_1 = (sums[n : n + 1] for n in range(4))
        norm_1, d_shift_1 = sums_one[:1], sums_one[1:]
        d_mod = [
            d_shift_1, norm_1 * vec[GAIN_1], d_gate_1, d_shift_2, norm_2 * vec[GAIN_2], d_gate_2
        ]
        others = [norm_1 * (1.0 + vec[SCALE_1]), norm_2 * (1.0 + vec[SCALE_2]), d_bias_down]
        sliced = lambda t: t.reshape(dp_count, -1)
        d_mod = jnp.concatenate(d_mod, axis=1)
        d_cond = lax.dot_general(
            d_mod,
            w_all.astype(F32),
            (((1,), (1,)), ((), ())),
            precision=PRECISE,
            preferred_element_type=F32,
        ) * silu_slope(cond)
        table = jnp.concatenate(
            [sliced(d_mod)]
            + [sliced(t) for t in others]
            + [sliced(t) for t in d_bias]
            + [jnp.broadcast_to(act, (dp_count, cond_size))],
            axis=1,
        )
    half = near.shape[-1] // 2
    if group.paired:
        step = [keep, group.bit(send, 0)]
        step, came, near = tie((step, came, near), sum_w)
        sum_w.settle()
        step = jnp.concatenate(step, axis=1)
        step = [step[0]] + [group.step(step[n], 2 * n) for n in range(1, dp_count // 2)]
    else:
        step = [lax.all_to_all(table, "dp", split_axis=0, concat_axis=0, tiled=True)]
    feeds = group.z(near[..., half:].astype(BF16), 2)
    near_w, far_w = sum_w.total
    far_w = group.z(far_w.astype(BF16), 1)
    step, far_w, feeds, came = lax.optimization_barrier((step, far_w, feeds, came))
    near_w = near_w + far_w.astype(F32)
    grad = group.z(near_w[..., cols:].astype(BF16), 2)
    length = step[0].shape[-1]
    d_cond = jnp.pad(d_cond, ((0, 0), (0, length - cond_size)))
    arrived = jnp.concatenate([t.reshape(-1, length) for t in step] + [d_cond])
    arrived = jnp.stack([arrived] + [group.z(arrived, k) for k in range(1, tensor_count)])
    grad = near_w[..., :cols] + grad.astype(F32)
    grad_qkv, grad_out = grad[:3], grad[3].T
    grad_up, grad_down = near[..., :half] + feeds.astype(F32)
    input_grad = group.held_rows(came)
    place = jnp.asarray([0, 2, 1, 3])[order]
    arrived = arrived[order]
    conds = arrived[:, dp_count, :cond_size]
    arrived = arrived[:, :dp_count]
    totals = jnp.sum(arrived[..., :edge], axis=(0, 1))
    biases = arrived[..., edge : edge + tensor_count * rows].reshape(
        tensor_count, dp_count, tensor_count, rows
    )
    wanted = (jnp.arange(tensor_count) == place[:, None])[:, None, :, None]
    grad_bias_up = jnp.sum(jnp.where(wanted, biases, 0.0), axis=(0, 1, 2))
    grad_bias_ada = totals[:mod_width]
    grad_gain_one, grad_gain_two, grad_bias_down = (
        totals[mod_width + n * rows : mod_width + (n + 1) * rows] for n in range(3)
    )
    arrived = arrived.reshape(dp_count * tensor_count, -1)
    grad_ada = lax.dot_general(
        arrived[:, -cond_size:],
        arrived[:, :mod_width],
        (((0,), (0,)), ((), ())),
        precision=PRECISE,
        preferred_element_type=F32,
    )
    cond_grad = jnp.take(conds, jnp.arange(per_dp) + d % 2, axis=0)
    return (
        block_out,
        input_grad,
        cond_grad,
        grad_qkv,
        grad_out,
        grad_up,
        grad_bias_up[None],
        grad_down.T,
        grad_bias_down,
        grad_gain_one,
        grad_gain_two,
        grad_ada,
        grad_bias_ada,
    )


def solution(mesh):
    return jax.shard_map(
        shards,
        mesh=mesh,
        in_specs=(
            P("dp", "tensor", None),
            P("dp", None),
            P("dp", None),
            P("dp", None),
            P(None, "dp", "tensor"),
            P("tensor", "dp"),
            P("dp", "tensor"),
            P("tensor", "dp"),
            P("tensor", "dp"),
            P("dp"),
            P("dp"),
            P("dp"),
            P(None, "dp"),
            P("dp"),
            P("dp", "tensor", None),
        ),
        out_specs=(
            P("dp", "tensor", None),
            P("dp", "tensor", None),
            P("dp", None),
            P(None, "dp", "tensor"),
            P("tensor", "dp"),
            P("dp", "tensor"),
            P("tensor", "dp"),
            P("tensor", "dp"),
            P("dp"),
            P("dp"),
            P("dp"),
            P(None, "dp"),
            P("dp"),
        ),
        check_vma=False,
    )
```

```python
from functools import partial

import jax
import jax.numpy as jnp
import numpy as np
from jax import lax
from jax.experimental import pallas as pl
from jax.experimental.pallas import tpu as pltpu
from jax.sharding import PartitionSpec as P

HEAD = 64
PRECISE = lax.Precision.HIGHEST
EPSILON = 1e-05
SHIFT_1, SCALE_1, GATE_1, SHIFT_2, SCALE_2, GATE_2, BIAS_OUT, GAIN_1, GAIN_2 = range(9)
F32 = jnp.float32
BF16 = jnp.bfloat16
PAIR = 2 * HEAD
BOTH = ("dp", "tensor")
ANY = pl.BlockSpec(memory_space=pl.ANY)
VMEM = pl.BlockSpec(memory_space=pltpu.VMEM)
SMEM = pl.BlockSpec(memory_space=pltpu.SMEM)


def dot_nn(a, b):
    return jnp.dot(a, b, preferred_element_type=F32)


def dot_nt(a, b):
    return lax.dot_general(a, b, (((1,), (1,)), ((), ())), preferred_element_type=F32)


VMEM_MIB = {'feed': 48, 'turn': 48, 'attend_back': 48, 'weight_grads': 48}


def params(name):
    return pltpu.CompilerParams(vmem_limit_bytes=VMEM_MIB.get(name, 58) << 20)


def cost(flops, nbytes, trans=0):
    return pl.CostEstimate(flops=int(flops), bytes_accessed=int(nbytes), transcendentals=int(trans))


def shape(dims, kind):
    return jax.ShapeDtypeStruct(tuple(dims), kind)


def row_at(me_ref, index, rows):
    return pl.multiple_of((me_ref[0] ^ index) * rows, rows)


def at_step(n, act):
    pl.when(pl.program_id(0) == n)(act)


def pick(refs, out, each=1):
    rows = refs[0].shape[0]
    for n, ref in enumerate(refs):
        at = pl.ds(n % each * rows, rows)
        at_step(n // each, lambda ref=ref, at=at: out.__setitem__((at, slice(None)), ref[...]))
    return out[...].astype(F32)


def put(refs, value):
    for n, ref in enumerate(refs):
        at_step(n, lambda ref=ref: ref.__setitem__(..., value))


def add_row(ref, n, value):
    at_step(0, lambda: ref.__setitem__((slice(n, n + 1), slice(None)), jnp.zeros_like(value)))
    ref[n : n + 1, :] += value


def start_all(copies):
    def act():
        for copy in copies:
            copy.start()

    at_step(0, act)


def wait_all(copies):
    def act():
        for copy in copies:
            copy.wait()

    at_step(0, act)


def row_block(rows, cols):
    return pl.BlockSpec((rows, cols), lambda i: (i, 0))


def col_block(rows, cols):
    return pl.BlockSpec((rows, cols), lambda i: (0, i))


def vec_row(vec, n):
    return vec[n : n + 1, :]


def norm_scale(vec, gain, scale):
    return vec_row(vec, gain) * (1.0 + vec_row(vec, scale))


def rotary_kernel(places, frequencies, cos_flat, sin_a, sin_b, cos_t, sin_t):
    angle = frequencies[...] * places[...]
    cosine, sine = jnp.cos(angle), jnp.sin(angle)
    cos_t[...], sin_t[...] = cosine, sine
    nothing = jnp.zeros_like(sine)
    cos_flat[...] = jnp.concatenate([cosine] * 4, axis=0).T
    sin_a[...] = jnp.concatenate([-sine, nothing] * 2, axis=0).T
    sin_b[...] = jnp.concatenate([nothing, sine] * 2, axis=0).T


def rotary(places, frequencies):
    length, half = places.shape[1], frequencies.shape[0]
    return pl.pallas_call(
        rotary_kernel,
        out_shape=[shape((length, 4 * half), F32)] * 3 + [shape((half, length), F32)] * 2,
        in_specs=[VMEM] * 2,
        out_specs=[VMEM] * 5,
        compiler_params=params("rotary"),
        cost_estimate=cost(6e6, 2e6),
        name="rotary",
    )(places, frequencies)


class Held:
    def __init__(self, parts, rels, offset=0):
        self.parts, self.rels, self.offset = parts, rels, offset

    def blocks(self, refs):
        n = 0
        for ref, rel in zip(refs, self.rels):
            for i, j in enumerate(rel):
                yield ref.at[i + self.offset], j, n
                n += 1

    @property
    def count(self):
        return sum(len(rel) for rel in self.rels)


def qkv_copies(me, qk, vo, refs, w_buf, sems, rows):
    out = []
    parts = len(qk.parts)
    for held, group, planes in ((qk, refs[:parts], (0, 1)), (vo, refs[parts:], (2,))):
        for block, j, n in held.blocks(group):
            for c, plane in enumerate(planes):
                out.append(
                    pltpu.make_async_copy(
                        block.at[pl.ds(c * rows, rows), :],
                        w_buf.at[plane, pl.ds(row_at(me, j, rows), rows), :],
                        sems.at[plane, n],
                    )
                )
    return out


def qkv_kernel(qk, vo, me, *refs):
    x_refs, refs = refs[:4], refs[4:]
    (vec, cosine, sin_a, sin_b), refs = refs[:4], refs[4:]
    mul, add = norm_scale(vec, GAIN_1, SCALE_1), vec_row(vec, SHIFT_1)
    held, refs = refs[: 2 * len(qk.parts)], refs[2 * len(qk.parts) :]
    (n_t, k_out, v_out, q_t, k_t, v_t), (w_buf, x_buf, sems) = refs[:6], refs[6:]
    copies = qkv_copies(me, qk, vo, held, w_buf, sems, w_buf.shape[1] // qk.count)
    start_all(copies)
    x = pick(x_refs, x_buf, 2)
    centred = x - jnp.mean(x, axis=-1, keepdims=True)
    spread = jnp.mean(centred * centred, axis=-1, keepdims=True)
    normed = (centred * lax.rsqrt(spread + EPSILON) * mul + add).astype(BF16)
    n_t[...] = normed.T
    wait_all(copies)
    width = k_out.shape[1]
    for c, (flat, turned, factor) in enumerate(((None, q_t, HEAD**-0.5), (k_out, k_t, 1.0))):
        proj = dot_nn(normed, w_buf[c])
        for p in range(width // PAIR):
            lanes = slice(p * PAIR, (p + 1) * PAIR)
            r = proj[:, lanes]
            spun = (
                r * cosine[...]
                + pltpu.roll(r, PAIR - HEAD // 2, 1) * sin_a[...]
                + pltpu.roll(r, HEAD // 2, 1) * sin_b[...]
            )
            spun = spun.astype(BF16) * BF16(factor)
            if flat is not None:
                flat[:, lanes] = spun
            turned[lanes, :] = spun.T
    values = dot_nn(normed, w_buf[2]).astype(BF16)
    v_out[...] = values
    v_t[...] = values.T


def qkv(me, x_parts, vec, cosine, sin_a, sin_b, qk, vo):
    part, width = x_parts[0].shape
    length = 4 * part
    cols = qk.parts[0].shape[2]
    flat, turned = shape((length, cols), BF16), shape((cols, length), BF16)
    return pl.pallas_call(
        partial(qkv_kernel, qk, vo),
        grid=(2,),
        out_shape=[shape((width, length), BF16), flat, flat, turned, turned, turned],
        in_specs=[SMEM]
        + [VMEM] * 5
        + [row_block(2 * part, PAIR)] * 3
        + [ANY] * (2 * len(qk.parts)),
        out_specs=[col_block(width, 2 * part)]
        + [row_block(2 * part, cols)] * 2
        + [col_block(cols, 2 * part)] * 3,
        scratch_shapes=[
            pltpu.VMEM((3, width, cols), BF16),
            pltpu.VMEM((2 * part, width), BF16),
            pltpu.SemaphoreType.DMA((3, qk.count)),
        ],
        compiler_params=params("qkv"),
        cost_estimate=cost(6 * length * width * cols, 16e6),
        name="qkv",
    )(me, *x_parts, vec, cosine, sin_a, sin_b, *qk.parts, *vo.parts)


def three_terms(v):
    rows = []
    for _ in range(3):
        rows.append(v.astype(BF16).astype(F32))
        v = v - rows[-1]
    rows += [jnp.zeros_like(v)] * 5
    return jnp.concatenate(rows, axis=0).astype(BF16)


DOCS, TERMS = 8, 16


def added_lanes(out, doc_col):
    lane = lax.broadcasted_iota(jnp.int32, out.shape, 1) % HEAD
    other = jnp.where(lane == doc_col[...], 0.0, -1e30)
    ones = jnp.where((lane >= TERMS) & (lane < TERMS + 3), 1.0, 0.0)
    out[...] = jnp.where(lane < DOCS, other, ones).astype(BF16)


def document_rows(doc_row):
    row = lax.broadcasted_iota(jnp.int32, (TERMS, doc_row.shape[1]), 0)
    return jnp.where(row == doc_row[...], 1.0, 0.0).astype(BF16)


def with_lanes(ref, added, head):
    lane = lax.broadcasted_iota(jnp.int32, (1, PAIR), 1)
    return jnp.where((lane // HEAD) == head, ref[...], added[...])


def with_rows(out, ref, head, rows):
    own, other = head * HEAD, (1 - head) * HEAD
    out[own : own + HEAD, :] = ref[own : own + HEAD, :]
    out[other : other + HEAD, :] = jnp.zeros((HEAD, out.shape[1]), BF16)
    for n, value in enumerate(rows):
        if value is not None:
            at = other + n * TERMS
            out[at : at + value.shape[0], :] = value


def attend_kernel(q_t, k, v_t, doc_row, doc_col, mix_t, log_sum, added, ahead):
    @pl.when(pl.program_id(0) == 0)
    def _():
        added_lanes(added, doc_col)

    docs = document_rows(doc_row)
    for h in range(2):
        with_rows(ahead.at[h], q_t, h, [docs])

    for h in range(2):
        rows = slice(h * HEAD, (h + 1) * HEAD)
        scores = dot_nn(with_lanes(k, added, h), ahead[h])
        top = jnp.max(scores, axis=0, keepdims=True)
        weights = jnp.exp(scores - top)
        total = jnp.sum(weights, axis=0, keepdims=True)
        mixed = dot_nn(v_t[rows, :], weights.astype(BF16))
        mix_t[rows, :] = (mixed / total).astype(BF16)
        log_sum[0, h] = top + jnp.log(total)


def attend(q_t, k, v_t, doc_row, doc_col):
    length, width = k.shape
    pairs = width // PAIR
    flat = pl.BlockSpec((length, PAIR), lambda i: (0, i))
    turned = pl.BlockSpec((PAIR, length), lambda i: (i, 0))
    return pl.pallas_call(
        attend_kernel,
        grid=(pairs,),
        in_specs=[
            turned,
            flat,
            turned,
            pl.BlockSpec((1, length), lambda i: (0, 0)),
            pl.BlockSpec((length, 1), lambda i: (0, 0)),
        ],
        out_specs=[turned, pl.BlockSpec((1, 2, 1, length), lambda i: (i, 0, 0, 0))],
        out_shape=[shape((width, length), BF16), shape((pairs, 2, 1, length), F32)],
        scratch_shapes=[pltpu.VMEM((length, PAIR), BF16), pltpu.VMEM((2, PAIR, length), BF16)],
        compiler_params=params("attend"),
        cost_estimate=cost(16 * length * length * width, 8e6),
        name="attend",
    )(q_t, k, v_t, doc_row, doc_col)


def load_out_weight(me, vo, refs, buf, sems):
    rows = buf.shape[0] // vo.count
    copies = [
        pltpu.make_async_copy(
            block.at[pl.ds(rows, rows), :], buf.at[pl.ds(row_at(me, j, rows), rows), :], sems.at[n]
        )
        for block, j, n in vo.blocks(refs)
    ]
    start_all(copies)
    return copies


def middle_kernel(vo, me, *refs):
    x_refs, g_refs, refs = refs[:4], refs[4:8], refs[8:]
    (mix_t, vec), refs = refs[:2], refs[2:]
    mul, add = norm_scale(vec, GAIN_2, SCALE_2), vec_row(vec, SHIFT_2)
    gate_one, gate_two = vec_row(vec, GATE_1), vec_row(vec, GATE_2)
    pieces, refs = refs[: len(vo.parts)], refs[len(vo.parts) :]
    (att, n_two, n_two_t, d_down, d_down_t, d_bias, mix), (w_buf, x_buf, sems) = refs[:7], refs[7:]
    copies = load_out_weight(me, vo, pieces, w_buf, sems)
    scaled = pick(g_refs, x_buf) * gate_two
    add_row(d_bias, 0, jnp.sum(scaled, axis=0, keepdims=True))
    scaled = scaled.astype(BF16)
    d_down[...] = scaled
    d_down_t[...] = scaled.T
    wait_all(copies)
    mixture = mix_t[...].T
    mix[...] = mixture
    attention = dot_nt(mixture, w_buf[...])
    att[...] = attention
    mid = pick(x_refs, x_buf) + gate_one * attention
    centred = mid - jnp.mean(mid, axis=-1, keepdims=True)
    spread = jnp.mean(centred * centred, axis=-1, keepdims=True)
    normed = (centred * lax.rsqrt(spread + EPSILON) * mul + add).astype(BF16)
    n_two[...] = normed
    n_two_t[...] = normed.T


def middle(me, x_parts, g_parts, mix_t, vec, vo):
    part, width = x_parts[0].shape
    length = 4 * part
    inner = mix_t.shape[0]
    flat, turned = shape((length, width), BF16), shape((width, length), BF16)
    return pl.pallas_call(
        partial(middle_kernel, vo),
        grid=(4,),
        out_shape=[shape((length, width), F32), flat, turned, flat, turned]
        + [shape((1, width), F32), shape((length, inner), BF16)],
        in_specs=[SMEM]
        + [VMEM] * 8
        + [col_block(inner, part), VMEM]
        + [ANY] * len(vo.parts),
        out_specs=[
            row_block(part, width),
            row_block(part, width),
            col_block(width, part),
            row_block(part, width),
            col_block(width, part),
            VMEM,
            row_block(part, inner),
        ],
        scratch_shapes=[
            pltpu.VMEM((width, inner), BF16),
            pltpu.VMEM((part, width), BF16),
            pltpu.SemaphoreType.DMA((vo.count,)),
        ],
        compiler_params=params("middle"),
        cost_estimate=cost(2 * length * width * inner, 16e6),
        name="middle",
    )(me, *x_parts, *g_parts, mix_t, vec, *vo.parts)


def spread_rows(me, value, stage, keep, send=None):
    blocks, rows = stage.shape[0], stage.shape[1]
    for j in range(blocks):
        stage[j] = value[j * rows : (j + 1) * rows, :].astype(BF16)
    for j in range(blocks):
        block = stage[me[0] ^ j]
        if j % 2 == 0:
            keep(j // 2, block)
        else:
            send(j // 2, block)


def slot_of(stream, slot, count):
    if stream == 0 and count == 4:
        slot = (0, 2, 1, 3)[slot]
    return slot


def writer(ref, stream):
    def put(slot, block):
        ref[stream, slot_of(stream, slot, ref.shape[1])] = block

    return put


def split_writer(ref, *lead):
    def put(slot, block):
        half = block.shape[-1] // 2
        for s in range(2):
            ref[(s, slot_of(s, slot, ref.shape[1]), *lead)] = block[:, s * half : (s + 1) * half]

    return put


C_ROOT = 0.7978845608028654
C_CUBE = 0.044715


def feed_kernel(up, dn, steps, first, me, *refs):
    (n_two, n_two_t, d_down, d_down_t, bias), refs = refs[:5], refs[5:]
    if not first:
        (down_in, d_n_in), refs = refs[:2], refs[2:]
    parts = len(up.parts)
    up_refs, down_refs, refs = refs[:parts], refs[parts : 2 * parts], refs[2 * parts :]
    (down, d_n, d_bias, *grads), (w_buf, stage, sems) = refs[:-3], refs[-3:]
    step = pl.program_id(0)
    rows = up_refs[0].shape[1]
    chunk = w_buf.shape[3]
    offset = 0 if first else steps * chunk

    def copies(s):
        out = []
        for m, (held, group) in enumerate(((up, up_refs), (dn, down_refs))):
            for block, j, n in held.blocks(group):
                out.append(
                    pltpu.make_async_copy(
                        block.at[:, pl.ds(offset + s * chunk, chunk)],
                        w_buf.at[m, s, pl.ds(row_at(me, j, rows), rows), :],
                        sems.at[m, s, n],
                    )
                )
        return out

    @pl.when(step == 0)
    def _():
        for s in range(steps):
            for copy in copies(s):
                copy.start()
        if first:
            down[...] = jnp.zeros_like(down)
            d_n[...] = jnp.zeros_like(d_n)
        else:
            down[...] = down_in[...]
            d_n[...] = d_n_in[...]

    for s in range(steps):

        @pl.when(step == s)
        def _():
            for copy in copies(s):
                copy.wait()

    w_up = w_buf[0, step]
    w_down_t = w_buf[1, step]
    h = dot_nn(n_two[...], w_up) + bias[0]
    square = h * h
    t = jnp.tanh(C_ROOT * h * (1.0 + C_CUBE * square))
    half = 0.5 + 0.5 * t
    act = (h * half).astype(BF16)
    slope = half + (0.5 * C_ROOT) * h * (1.0 - t * t) * (1.0 + (3.0 * C_CUBE) * square)
    d_h = (dot_nn(d_down[...], w_down_t) * slope).astype(BF16)
    d_bias[0] = jnp.sum(d_h.astype(F32), axis=0, keepdims=True)
    down[...] += dot_nt(act, w_down_t)
    d_n[...] += dot_nt(d_h, w_up)
    for m, grad in ((0, dot_nn(n_two_t[...], d_h)), (1, dot_nn(d_down_t[...], act))):
        spread_rows(me, grad, stage, *(writer(ref, m) for ref in grads))


def feed(me, n_two, n_two_t, d_down, d_down_t, bias, up, dn, start, before, units):
    blocks = up.count
    length, width = n_two.shape
    chunk = 512 if units % 512 == 0 else units
    steps = units // chunk
    first = before is None
    rows = width // blocks
    one = pl.Buffered(1)
    flat = pl.BlockSpec((length, width), lambda i: (0, 0), pipeline_mode=one)
    turned = pl.BlockSpec((width, length), lambda i: (0, 0), pipeline_mode=one)
    held = pl.BlockSpec((length, width), lambda i: (0, 0))
    half = max(blocks // 2, 1)
    grad = pl.BlockSpec((2, half, rows, chunk), lambda i: (0, 0, 0, i))
    grads = 1 if blocks == 1 else 2
    bias_spec = pl.BlockSpec((1, 1, chunk), lambda i: (i + start // chunk, 0, 0))
    return pl.pallas_call(
        partial(feed_kernel, up, dn, steps, first),
        grid=(steps,),
        in_specs=[SMEM, flat, turned, flat, turned, bias_spec]
        + ([] if first else [flat, flat])
        + [ANY] * (2 * len(up.parts)),
        out_specs=[held, held, pl.BlockSpec((1, 1, chunk), lambda i: (i, 0, 0))] + [grad] * grads,
        out_shape=[shape((length, width), F32)] * 2
        + [shape((steps, 1, chunk), F32)]
        + [shape((2, half, rows, units), BF16)] * grads,
        scratch_shapes=[
            pltpu.VMEM((2, steps, width, chunk), BF16),
            pltpu.VMEM((blocks, rows, chunk), BF16),
            pltpu.SemaphoreType.DMA((2, steps, blocks)),
        ],
        compiler_params=params("feed"),
        cost_estimate=cost(12 * length * width * units, 20e6),
        name="feed",
    )(
        me,
        n_two,
        n_two_t,
        d_down,
        d_down_t,
        bias.reshape(-1, 1, chunk),
        *(() if first else before),
        *up.parts,
        *dn.parts,
    )


def turn_kernel(vo, me, *refs):
    x_refs, g_refs, refs = refs[:4], refs[4:8], refs[8:]
    (att, down, d_n, vec), refs = refs[:4], refs[4:]
    mul, bias = norm_scale(vec, GAIN_2, SCALE_2), vec_row(vec, BIAS_OUT)
    gate_one, gate_two = vec_row(vec, GATE_1), vec_row(vec, GATE_2)
    pieces, refs = refs[: len(vo.parts)], refs[len(vo.parts) :]
    out_refs, (d_mid, d_mix_t, sums, d_att_t), (w_buf, x_buf, sems) = (
        refs[:4],
        refs[4:8],
        refs[8:],
    )
    copies = load_out_weight(me, vo, pieces, w_buf, sems)
    g = pick(g_refs, x_buf)
    attention = att[...]
    mid = pick(x_refs, x_buf) + gate_one * attention
    branch = down[...] + bias
    put(out_refs, (mid + gate_two * branch).astype(BF16))
    centred = mid - jnp.mean(mid, axis=-1, keepdims=True)
    inverse = lax.rsqrt(jnp.mean(centred * centred, axis=-1, keepdims=True) + EPSILON)
    unit = centred * inverse
    dn = d_n[...]
    dn_unit = dn * unit
    du = dn * mul
    dm = g + inverse * (
        du
        - jnp.mean(du, axis=-1, keepdims=True)
        - unit * jnp.mean(dn_unit * mul, axis=-1, keepdims=True)
    )
    d_mid[...] = dm
    for n, term in enumerate((g * branch, dn_unit, dn, dm * attention)):
        add_row(sums, n, jnp.sum(term, axis=0, keepdims=True))
    d_att = (dm * gate_one).astype(BF16)
    d_att_t[...] = d_att.T
    wait_all(copies)
    d_mix_t[...] = dot_nn(d_att, w_buf[...]).astype(BF16).T


def turn(me, x_parts, g_parts, att, down, d_n, vec, vo):
    part, width = x_parts[0].shape
    length = 4 * part
    inner = vo.parts[0].shape[2]
    return pl.pallas_call(
        partial(turn_kernel, vo),
        grid=(4,),
        out_shape=[shape((part, width), BF16)] * 4
        + [
            shape((length, width), F32),
            shape((inner, length), BF16),
            shape((4, width), F32),
            shape((width, length), BF16),
        ],
        in_specs=[SMEM]
        + [VMEM] * 8
        + [row_block(part, width)] * 3
        + [VMEM]
        + [ANY] * len(vo.parts),
        out_specs=[VMEM] * 4
        + [
            row_block(part, width),
            col_block(inner, part),
            VMEM,
            col_block(width, part),
        ],
        scratch_shapes=[
            pltpu.VMEM((width, inner), BF16),
            pltpu.VMEM((part, width), BF16),
            pltpu.SemaphoreType.DMA((vo.count,)),
        ],
        compiler_params=params("turn"),
        cost_estimate=cost(2 * length * width * inner, 24e6),
        name="turn",
    )(
        me, *x_parts, *g_parts, att, down, d_n, vec, *vo.parts
    )


def attend_back_kernel(
    k, v, q_t, k_t, d_mix_t, mix_t, log_sum, doc_row, doc_col, cos_t, sin_t,
    dq, dk, dv, added, ahead, dq_acc, dk_acc, dv_acc,
):
    @pl.when(pl.program_id(0) == 0)
    def _():
        added_lanes(added, doc_col)

    length = k.shape[0]
    block = 256 if length % 256 == 0 else length
    docs = document_rows(doc_row)
    for h in range(2):
        rows = slice(h * HEAD, (h + 1) * HEAD)
        row_dot = jnp.sum(
            d_mix_t[rows, :].astype(F32) * mix_t[rows, :].astype(F32), axis=0, keepdims=True
        )
        with_rows(ahead.at[h, 0], q_t, h, [docs, three_terms(-log_sum[0, h])])
        with_rows(ahead.at[h, 1], d_mix_t, h, [None, three_terms(-row_dot)])

    for h in range(2):
        rows = slice(h * HEAD, (h + 1) * HEAD)
        keys, values = with_lanes(k, added, h), with_lanes(v, added, h)
        for b in range(length // block):
            c = slice(b * block, (b + 1) * block)
            probs = jnp.exp(dot_nn(keys[c], ahead[h, 0]))
            d_scores = (probs * dot_nn(values[c], ahead[h, 1])).astype(BF16)
            dv_acc[rows, c] = dot_nt(d_mix_t[rows, :], probs.astype(BF16))
            dk_acc[rows, c] = dot_nt(q_t[rows, :], d_scores)
            dq_part = dot_nn(k_t[rows, c], d_scores)
            if b == 0:
                dq_acc[rows, :] = dq_part
            else:
                dq_acc[rows, :] += dq_part

    half = HEAD // 2
    for acc, out, factor in ((dq_acc, dq, HEAD**-0.5), (dk_acc, dk, 1.0)):
        turned = []
        for h in range(2):
            a = acc[h * HEAD : h * HEAD + half, :] * factor
            b = acc[h * HEAD + half : (h + 1) * HEAD, :] * factor
            turned.append(a * cos_t[...] + b * sin_t[...])
            turned.append(b * cos_t[...] - a * sin_t[...])
        out[...] = jnp.concatenate(turned, axis=0).astype(BF16).T
    dv[...] = dv_acc[...].astype(BF16).T


def attend_back(k, v, q_t, k_t, d_mix_t, mix_t, log_sum, doc_row, doc_col, cos_t, sin_t):
    length, width = k.shape
    count = width // PAIR
    flat = pl.BlockSpec((length, PAIR), lambda i: (0, i))
    turned = pl.BlockSpec((PAIR, length), lambda i: (i, 0))
    fixed = lambda a: pl.BlockSpec(a.shape, lambda i: (0, 0))
    return pl.pallas_call(
        attend_back_kernel,
        grid=(count,),
        in_specs=[flat] * 2
        + [turned] * 4
        + [pl.BlockSpec((1, 2, 1, length), lambda i: (i, 0, 0, 0))]
        + [fixed(a) for a in (doc_row, doc_col, cos_t, sin_t)],
        out_specs=[flat] * 3,
        out_shape=[shape((length, width), BF16)] * 3,
        scratch_shapes=[
            pltpu.VMEM((length, PAIR), BF16),
            pltpu.VMEM((2, 2, PAIR, length), BF16),
        ]
        + [pltpu.VMEM((PAIR, length), F32)] * 3,
        compiler_params=params("attend_back"),
        cost_estimate=cost(28 * length * length * width, 14e6),
        name="attend_back",
    )(k, v, q_t, k_t, d_mix_t, mix_t, log_sum, doc_row, doc_col, cos_t, sin_t)


def first_kernel(qk, vo, me, *refs):
    x_refs, refs = refs[:4], refs[4:]
    (d_mid, vec, dq, dk, dv), refs = refs[:5], refs[5:]
    mul = norm_scale(vec, GAIN_1, SCALE_1)
    held, refs = refs[: 2 * len(qk.parts)], refs[2 * len(qk.parts) :]
    out_refs, (sums, w_buf, x_buf, sems) = refs[:4], refs[4:]
    copies = qkv_copies(me, qk, vo, held, w_buf, sems, w_buf.shape[1] // qk.count)
    start_all(copies)
    x = pick(x_refs, x_buf)
    centred = x - jnp.mean(x, axis=-1, keepdims=True)
    inverse = lax.rsqrt(jnp.mean(centred * centred, axis=-1, keepdims=True) + EPSILON)
    unit = centred * inverse
    wait_all(copies)
    dn = dot_nt(dq[...], w_buf[0]) + dot_nt(dk[...], w_buf[1]) + dot_nt(dv[...], w_buf[2])
    dn_unit = dn * unit
    du = dn * mul
    put(
        out_refs,
        (
            d_mid[...]
            + inverse
            * (
                du
                - jnp.mean(du, axis=-1, keepdims=True)
                - unit * jnp.mean(dn_unit * mul, axis=-1, keepdims=True)
            )
        ).astype(BF16),
    )
    for n, term in enumerate((dn_unit, dn)):
        add_row(sums, n, jnp.sum(term, axis=0, keepdims=True))


def first(me, x_parts, d_mid, vec, dq, dk, dv, qk, vo):
    part, width = x_parts[0].shape
    length = 4 * part
    cols = dq.shape[1]
    return pl.pallas_call(
        partial(first_kernel, qk, vo),
        grid=(4,),
        out_shape=[shape((part, width), BF16)] * 4 + [shape((2, width), F32)],
        in_specs=[SMEM]
        + [VMEM] * 4
        + [row_block(part, width), VMEM]
        + [row_block(part, cols)] * 3
        + [ANY] * (2 * len(qk.parts)),
        out_specs=[VMEM] * 5,
        scratch_shapes=[
            pltpu.VMEM((3, width, cols), BF16),
            pltpu.VMEM((part, width), BF16),
            pltpu.SemaphoreType.DMA((3, qk.count)),
        ],
        compiler_params=params("first"),
        cost_estimate=cost(6 * length * width * cols, 20e6),
        name="first",
    )(me, *x_parts, d_mid, vec, dq, dk, dv, *qk.parts, *vo.parts)


def modulate_kernel(qk, vo, zones, me, act, *refs):
    parts = len(qk.parts)
    qk_refs, vo_refs, (vec, bias, ada, small, sems) = refs[:parts], refs[parts:-5], refs[-5:]
    count = qk.count
    rows = ada.shape[0] // count
    cut = rows // 2
    copies = []
    for h, (held, group) in enumerate(((qk, qk_refs), (vo, vo_refs))):
        for block, j, n in held.blocks(group):
            at = row_at(me, j, rows) + h * cut
            copies.append(
                pltpu.make_async_copy(
                    block.at[pl.ds(2 * rows, cut), :], ada.at[pl.ds(at, cut), :], sems.at[h, n]
                )
            )
            if h:
                copies.append(
                    pltpu.make_async_copy(
                        block.at[pl.ds(2 * rows + cut, 16), :],
                        small.at[pl.ds(row_at(me, j, 16), 16), :],
                        sems.at[2, n],
                    )
                )
    for copy in copies:
        copy.start()
    for copy in copies:
        copy.wait()
    kinds = ada.shape[1] // act.shape[1]
    act3 = three_terms(act[...])
    across = vec.shape[1] // rows
    vec[...] = jnp.zeros_like(vec)
    for k in range(kinds):
        lanes = slice(k * act.shape[1], (k + 1) * act.shape[1])
        found = jnp.sum(dot_nt(act3, ada[:, lanes]), axis=0, keepdims=True)
        for d in range(count):
            m = d * kinds + k
            at = (m % across) * rows
            extra = small[d * 16 : (d + 1) * 16, :].astype(F32)
            vec[m // across : m // across + 1, at : at + rows] = (
                found[:, d * rows : (d + 1) * rows] + extra[1:2, k * rows : (k + 1) * rows]
            )
    for d in range(count):
        extra = small[d * 16 : (d + 1) * 16, :].astype(F32)
        here = slice(d * rows, (d + 1) * rows)
        for n in range(3):
            vec[BIAS_OUT + n : BIAS_OUT + n + 1, here] = extra[2:3, n * rows : (n + 1) * rows]
        for n in range(zones):
            far = (n - zones // 2) % zones
            at = n * (extra.shape[1] // zones)
            bias[far : far + 1, here] = extra[0:1, at : at + rows]


def modulate(me, act, qk, vo, zones, rows):
    width = qk.parts[0].shape[2]
    return pl.pallas_call(
        partial(modulate_kernel, qk, vo, zones),
        out_shape=[
            shape((16, width), F32),
            shape((zones, width), F32),
            shape((qk.count * rows, width), BF16),
        ],
        in_specs=[SMEM, VMEM] + [ANY] * (len(qk.parts) + len(vo.parts)),
        out_specs=[VMEM] * 3,
        scratch_shapes=[
            pltpu.VMEM((qk.count * 16, width), BF16),
            pltpu.SemaphoreType.DMA((3, qk.count)),
        ],
        compiler_params=params("modulate"),
        cost_estimate=cost(2e7, 4e6),
        name="modulate",
    )(me, act, *qk.parts, *vo.parts)


def gather_up_kernel(
    count, me, vec, ada, sums, sums_one, d_bias_down, d_bias_b, d_bias_a, act, cond,
    keep, send, d_cond, out, spread, bias_grad
):
    width = vec.shape[1]
    rows = width // count
    size = act.shape[1]
    kinds = ada.shape[1] // size
    norm_1, norm_2 = sums_one[0:1, :], sums[1:2, :]
    d_mod = (
        sums_one[1:2, :],
        norm_1 * vec_row(vec, GAIN_1),
        sums[3:4, :],
        sums[2:3, :],
        norm_2 * vec_row(vec, GAIN_2),
        sums[0:1, :],
    )
    others = (
        norm_1 * (1.0 + vec_row(vec, SCALE_1)),
        norm_2 * (1.0 + vec_row(vec, SCALE_2)),
        d_bias_down[...],
    )
    out[...] = jnp.zeros_like(out)
    chunk = d_bias_a.shape[2]
    for n, ref in enumerate((d_bias_b, d_bias_a)):
        for c in range(ref.shape[0]):
            at = c * chunk
            while at < (c + 1) * chunk:
                zone = at // width
                to = min((c + 1) * chunk, (zone + 1) * width)
                bias_grad[2 * n + zone : 2 * n + zone + 1, at - zone * width : to - zone * width] = (
                    ref[c][:, at - c * chunk : to - c * chunk]
                )
                at = to
    base = (kinds + 3) * rows
    for d in range(count):
        here = slice(d * rows, (d + 1) * rows)
        for k in range(kinds):
            m = d * kinds + k
            at = (m % count) * rows
            piece = d_mod[m // count][:, at : at + rows]
            out[d, :, k * rows : (k + 1) * rows] = piece
            spread[k : k + 1, here] = piece
        for n, value in enumerate(others):
            at = (kinds + n) * rows
            out[d, :, at : at + rows] = value[:, here]
        for n in range(bias_grad.shape[0]):
            at = base + n * rows
            out[d, :, at : at + rows] = bias_grad[n : n + 1, here]
        out[d, :, out.shape[2] - size :] = act[...]
    total = jnp.zeros(act.shape, F32)
    for k in range(kinds):
        three = three_terms(spread[k : k + 1, :])
        total += jnp.sum(dot_nn(three, ada[:, k * size : (k + 1) * size]), axis=0, keepdims=True)
    c = cond[...]
    sig = 1.0 / (1.0 + jnp.exp(-c))
    d_cond[...] = total * (sig * (1.0 + c * (1.0 - sig)))

    for j in range(count // 2):
        keep[j] = out[me[0] ^ (2 * j)]
        send[j] = out[me[0] ^ (2 * j + 1)]


def gather_up(me, vec, ada, sums, sums_one, d_bias_down, d_bias_b, d_bias_a, act, cond, count, length):
    return pl.pallas_call(
        partial(gather_up_kernel, count),
        out_shape=[shape((count // 2, 1, length), F32)] * 2 + [shape(act.shape, F32)],
        in_specs=[SMEM] + [VMEM] * 9,
        out_specs=[VMEM] * 3,
        scratch_shapes=[
            pltpu.VMEM((count, 1, length), F32),
            pltpu.VMEM((8, vec.shape[1]), F32),
            pltpu.VMEM((4, vec.shape[1]), F32),
        ],
        compiler_params=params("gather_up"),
        cost_estimate=cost(2e7, 4e6),
        name="gather_up",
    )(me, vec, ada, sums, sums_one, d_bias_down, d_bias_b, d_bias_a, act, cond)


def weight_grads_kernel(me, n_t, d_att_t, dq, dk, dv, mix_t, *refs):
    *grads, left, right, stage, sems = refs
    copies = [
        pltpu.make_async_copy(ref, held, sems.at[n])
        for n, (ref, held) in enumerate(
            (
                (n_t, left.at[0]),
                (dq, right.at[0]),
                (dk, right.at[1]),
                (dv, right.at[2]),
                (d_att_t, left.at[1]),
                (mix_t, right.at[3]),
            )
        )
    ]
    start_all(copies)
    wait_all(copies[:2])
    at_step(1, copies[2].wait)
    at_step(2, copies[3].wait)

    def last():
        copies[4].wait()
        copies[5].wait()

    at_step(3, last)
    step = pl.program_id(0)
    grad = dot_nn(left[jnp.where(step == 3, 1, 0)], right[step])
    spread_rows(me, grad, stage, *(split_writer(ref, 0) for ref in grads))


def weight_grads(me, n_t, d_att_t, dq, dk, dv, mix, blocks):
    width, length = n_t.shape
    cols = dq.shape[1]
    rows = width // blocks
    half = max(blocks // 2, 1)
    grads = 1 if blocks == 1 else 2
    return pl.pallas_call(
        weight_grads_kernel,
        grid=(4,),
        out_shape=[shape((2, half, 4, rows, cols // 2), BF16)] * grads,
        in_specs=[SMEM] + [ANY] * 6,
        out_specs=[
            pl.BlockSpec((2, half, 1, rows, cols // 2), lambda i: (0, 0, i, 0, 0))
        ]
        * grads,
        scratch_shapes=[
            pltpu.VMEM((2, width, length), BF16),
            pltpu.VMEM((4, length, cols), BF16),
            pltpu.VMEM((blocks, rows, cols), BF16),
            pltpu.SemaphoreType.DMA((6,)),
        ],
        compiler_params=params("weight_grads"),
        cost_estimate=cost(8 * length * width * cols, 14e6),
        name="weight_grads",
    )(me, n_t, d_att_t, dq, dk, dv, mix)


class Group:
    def __init__(self, dp_count, tensor_count, per_dp):
        self.dp, self.tensor, self.per_dp = dp_count, tensor_count, per_dp
        self.d, self.r = lax.axis_index("dp"), lax.axis_index("tensor")
        self.paired = dp_count == 8

    def bit(self, v, b):
        return lax.ppermute(v, "dp", [(i, i ^ (1 << b)) for i in range(self.dp)])

    def step(self, v, k):
        return lax.ppermute(v, "dp", [(i, i ^ k) for i in range(self.dp)])

    def z(self, v, k):
        return lax.ppermute(v, "tensor", [(i, i ^ k) for i in range(self.tensor)])

    def owns(self, d, r):
        return 0 <= r - d % 2 < self.per_dp

    def for_owner(self, rows, zero_idle):
        mine = self.r - self.d % 2
        top = self.per_dp - 1
        own = lax.dynamic_index_in_dim(rows, jnp.clip(mine, 0, top), 0, keepdims=False)
        if zero_idle:
            own = jnp.where((mine >= 0) & (mine <= top), own, jnp.zeros_like(own))
        parts = [own]
        for k in range(1, self.tensor):
            want = (self.r ^ k) - self.d % 2
            parts.append(
                lax.dynamic_index_in_dim(rows, jnp.clip(want, 0, top), 0, keepdims=False)
            )
        return parts

    def ship(self, v, k, to_owner):
        pairs = [
            (d * self.tensor + r, d * self.tensor + (r ^ k))
            for d in range(self.dp)
            for r in range(self.tensor)
            if self.owns(d, r ^ k if to_owner else r)
        ]
        return lax.ppermute(v, BOTH, pairs)

    def held_rows(self, came):
        stack = jnp.stack(came)
        return jnp.stack(
            [
                lax.dynamic_index_in_dim(stack, self.r ^ (j + self.d % 2), 0, keepdims=False)
                for j in range(self.per_dp)
            ]
        )

    def z_pair(self, v, got):
        return jnp.concatenate([v, got], axis=-1)

    def gather_pair(self, v, got, order):
        pair = jnp.stack([v, got])
        return [pair, self.bit(pair, order[1])]

    def gather_cores(self, parts, order):
        one, two = (1 << b for b in order)
        rels = [(0, one), (two, one ^ two)]
        rels += [tuple(j ^ 1 for j in rel) for rel in rels]
        return Held(parts + [self.bit(p, 0) for p in parts], rels)

    def gather_cores_joined(self, pairs, orders):
        near = jnp.concatenate([p for pair in pairs for p in pair])
        far = self.bit(near, 0)
        held = []
        for n, order in enumerate(orders):
            one, two = (1 << b for b in order)
            rel = (0, one, two, one ^ two)
            held.append(Held([near, far], [rel, tuple(j ^ 1 for j in rel)], 4 * n))
        return held

    def whole(self, v, axis):
        return lax.all_gather(v, "dp", axis=axis, tiled=True)


class Flight:
    def __init__(self, value):
        self.value = value


class Sum:
    def __init__(self, group, keep, send=None):
        self.group, self.stage, self.flights, self.terms = group, 0, [], []
        if not group.paired:
            value = keep[:, 0].astype(F32)
            value = lax.psum_scatter(value, "dp", scatter_dimension=value.ndim - 2, tiled=True)
            self.total = [value[0], value[1]]
            return
        self.terms = [[keep], [keep]]
        flight = Flight(group.bit(send, 0))
        self.flights = [(flight, 0), (flight, 1)]

    def settle(self):
        for terms, (flight, at) in zip(self.terms, self.flights):
            terms.append(flight.value if self.stage == 0 else flight.value[at])
        if self.flights and self.stage == 2:
            self.total = [sum(t[0].astype(F32) for t in terms) for terms in self.terms]
        self.flights = []

    def split(self):
        out = []
        for n, order in enumerate(((1, 2), (2, 1))):
            b = order[self.stage]
            if self.stage:
                stay, go = [t[:1] for t in self.terms[n]], [t[1:] for t in self.terms[n]]
            else:
                stay, go = [t[n, :2] for t in self.terms[n]], [t[n, 2:] for t in self.terms[n]]
            self.terms[n] = stay
            out.append((b, sum(t.astype(F32) for t in go).astype(BF16)))
        self.stage += 1
        self.flights = [None, None]
        return out


def exchange(*sums):
    links = {}
    for t in sums:
        t.settle()
        if t.group.paired:
            for n, (b, go) in enumerate(t.split()):
                links.setdefault(b, []).append((t, n, go))
    for b, items in links.items():
        blocks = [go for _, _, go in items]
        blocks = blocks[0] if len(blocks) == 1 else jnp.concatenate(blocks)
        flight, at = Flight(items[0][0].group.bit(blocks, b)), 0
        for t, n, go in items:
            t.flights[n] = (flight, slice(at, at + go.shape[0]))
            at += go.shape[0]


def tie(value, *sums):
    flights = {id(f): f for t in sums for f, _ in t.flights}
    flights = list(flights.values())
    value, arrived = lax.optimization_barrier((value, [f.value for f in flights]))
    for flight, v in zip(flights, arrived):
        flight.value = v
    return value


def silu_slope(c):
    sig = jax.nn.sigmoid(c)
    return sig * (1.0 + c * (1.0 - sig))


def shards(
    inputs, condition, doc_ids, positions, w_qkv, w_out, w_up, bias_up, w_down, bias_down,
    gain_one, gain_two, w_ada, bias_ada, out_grad,
):
    dp_count = lax.axis_size("dp")
    tensor_count = lax.axis_size("tensor")
    per_dp, part, width = inputs.shape
    length = doc_ids.shape[1]
    rows = w_up.shape[0]
    group = Group(dp_count, tensor_count, per_dp)
    blocks = dp_count if group.paired else 1
    d, r = group.d, group.r
    me = jnp.where(group.paired, d, 0).astype(jnp.int32).reshape(1)
    mine = jnp.clip(r - d % 2, 0, per_dp - 1)
    own_row = lambda v: lax.dynamic_index_in_dim(v, mine, 0, keepdims=False)
    join = lambda parts: jnp.concatenate(parts, axis=-1)

    order = r ^ jnp.arange(tensor_count)
    mixed = lambda v: own_row(v).reshape(tensor_count, part)[order].reshape(-1)
    docs, places = mixed(doc_ids), mixed(positions)
    doc_row, doc_col = docs[None, :], docs[:, None]
    frequencies = 10000.0 ** (-2.0 * jnp.arange(HEAD // 2, dtype=F32) / HEAD)
    cos_flat, sin_a, sin_b, cos_t, sin_t = rotary(
        places.astype(F32)[None, :], frequencies[:, None]
    )

    cols, cond_size, mod_width = w_qkv.shape[2], w_ada.shape[0], w_ada.shape[1]
    ways = (1, 2), (2, 1)
    cond = own_row(condition).astype(F32)[None]
    act = jax.nn.silu(cond)
    early = jnp.concatenate([w_qkv.reshape(-1, cols), w_out.T])
    late = jnp.concatenate([w_up, w_down.T])
    if group.paired:
        early = jnp.concatenate([early, jnp.pad(bias_up, ((0, 15), (0, cols - rows)))])
    if group.paired:
        ada = w_ada.T.reshape(-1, rows, cond_size).transpose(1, 0, 2).reshape(rows, width)
        cut, top = rows // 2, 2 * rows
        wide = lambda v: jnp.pad(v, (0, width - v.shape[0]))[None]
    x_parts, g_parts = group.for_owner(inputs, False), group.for_owner(out_grad, True)
    early = group.z_pair(early, group.z(early, 2))
    early = join([early, group.z(early, 1)])
    turns = cos_flat, sin_a, sin_b, cos_t, sin_t, doc_row, doc_col
    late, early, x_parts, g_parts = lax.optimization_barrier((late, early, x_parts, g_parts))
    late_got = group.z(late, 2)
    if group.paired:
        small = jnp.concatenate(
            [
                early[2 * top : 2 * top + 1],
                wide(bias_ada),
                wide(jnp.concatenate([bias_down, gain_one, gain_two])),
                early[2 * top + 3 :],
            ]
        )
        firsts = (
            jnp.concatenate([early[:top], ada[:cut], jnp.zeros_like(small)]),
            jnp.concatenate([early[top : 2 * top], ada[cut:], small]),
        )
        came = [group.bit(v, way[0]) for v, way in zip(firsts, ways)]
        late_got, came = lax.optimization_barrier((late_got, came))
        late = group.z_pair(late, late_got)
        late_far = group.z(late, 1)
        near = [group.gather_pair(v, got, way) for v, got, way in zip(firsts, came, ways)]
        x_parts[2] = group.ship(x_parts[2], 2, True)
        late_far, near, x_parts, turns = lax.optimization_barrier((late_far, near, x_parts, turns))
        cos_flat, sin_a, sin_b, cos_t, sin_t, doc_row, doc_col = turns
        for n in (3, 1):
            x_parts[n] = group.ship(x_parts[n], n, True)
        qk, vo = group.gather_cores_joined(near, ways)
        lates = join([late_far[:rows], late[:rows]]), join([late_far[rows:], late[rows:]])
        came = [group.bit(v, way[0]) for v, way in zip(lates, ways)]
        vec, bias_hidden, ada_all = modulate(me, act, qk, vo, tensor_count, rows)
        x_parts, g_parts, came, vec = lax.optimization_barrier((x_parts, g_parts, came, vec))
        for n in range(1, tensor_count):
            g_parts[n] = group.ship(g_parts[n], n, True)
        near = [group.gather_pair(v, got, way) for v, got, way in zip(lates, came, ways)]
    else:
        for n in range(1, tensor_count):
            x_parts[n] = group.ship(x_parts[n], n, True)
            g_parts[n] = group.ship(g_parts[n], n, True)
        late = group.z_pair(late, late_got)
        late = join([group.z(late, 1), late])
        flat = lambda v: group.whole(v.reshape(2, rows, width), 1).reshape(1, 2 * width, width)
        qk, vo = Held([flat(early[: 2 * rows])], [(0,)]), Held([flat(early[2 * rows :])], [(0,)])
        up, dn = (Held([group.whole(v, 0)[None]], [(0,)]) for v in (late[:rows], late[rows:]))
        w_all = group.whole(w_ada, 1)
        modulation = jnp.dot(
            act, w_all.astype(F32), precision=PRECISE, preferred_element_type=F32
        ) + group.whole(bias_ada, 0).astype(F32)
        small = group.whole(jnp.stack([bias_down, gain_one, gain_two]), 1).astype(F32)
        vec = jnp.concatenate([modulation.reshape(6, width), small, jnp.zeros((7, width), F32)])
        bias_hidden = group.whole(bias_up, 1)
        bias_hidden = jnp.concatenate([group.z(bias_hidden, k) for k in (1, 3, 0, 2)]).astype(F32)

    n_t, k, v, q_t, k_t, v_t = qkv(me, x_parts, vec, cos_flat, sin_a, sin_b, qk, vo)
    mix_t, log_sum = attend(q_t, k, v_t, doc_row, doc_col)
    if group.paired:
        mix_t, near, g_parts = lax.optimization_barrier((mix_t, near, g_parts))
        up, dn = (group.gather_cores(p, way) for p, way in zip(near, ways))
    att, n_two, n_two_t, d_down, d_down_t, d_bias_down, mix = middle(
        me, x_parts, g_parts, mix_t, vec, vo
    )
    size = w_up.shape[1]
    feed_args = (me, n_two, n_two_t, d_down, d_down_t, bias_hidden, up, dn)

    down, d_n, d_bias_a, *grads = feed(*feed_args, 0, None, 2 * size)
    sum_a = Sum(group, *grads)
    down, d_n, d_bias_b, *grads = feed(*feed_args, 2 * size, (down, d_n), 2 * size)
    down = tie(down, sum_a)
    exchange(sum_a)
    sum_b = Sum(group, *grads)
    *out_parts, d_mid, d_mix_t, sums, d_att_t = turn(
        me, x_parts, g_parts, att, down, d_n, vec, vo
    )
    d_mix_t, out_parts = tie((d_mix_t, out_parts), sum_a, sum_b)
    came = out_parts[:1] + [group.ship(out_parts[n], n, False) for n in range(1, tensor_count)]
    exchange(sum_a, sum_b)
    dq, dk, dv = attend_back(
        k, v, q_t, k_t, d_mix_t, mix_t, log_sum, doc_row, doc_col, cos_t, sin_t
    )
    dq, came = tie((dq, came), sum_a, sum_b)
    block_out = group.held_rows(came)
    sum_a.settle()
    exchange(sum_b)
    far_up = group.z(sum_a.total[0].astype(BF16), 1)
    grads = weight_grads(me, n_t, d_att_t, dq, dk, dv, mix, blocks)
    d_mid, grads, far_up, last = tie((d_mid, grads, far_up, sum_a.total[1]), sum_b)
    far_dn = group.z(last.astype(BF16), 1)
    sum_w = Sum(group, *grads)
    *in_parts, sums_one = first(me, x_parts, d_mid, vec, dq, dk, dv, qk, vo)

    in_parts, far_dn = tie((in_parts, far_dn), sum_w)
    exchange(sum_w)
    came = in_parts[:1] + [group.ship(in_parts[n], n, False) for n in range(1, tensor_count)]
    sum_b.settle()
    near = jnp.stack(sum_b.total) + jnp.stack([far_up, far_dn]).astype(F32)
    sums_one, near = tie((sums_one, near), sum_w)
    exchange(sum_w)
    edge = mod_width + 3 * rows
    if group.paired:
        length = edge + tensor_count * rows + 2 * cond_size
        keep, send, d_cond = gather_up(
            me, vec, ada_all, sums, sums_one, d_bias_down, d_bias_b, d_bias_a, act, cond, dp_count,
            length - length % cond_size,
        )
    else:
        d_gate_2, norm_2, d_shift_2, d_gate_1 = (sums[n : n + 1] for n in range(4))
        norm_1, d_shift_1 = sums_one[:1], sums_one[1:]
        d_mod = [
            d_shift_1, norm_1 * vec[GAIN_1], d_gate_1, d_shift_2, norm_2 * vec[GAIN_2], d_gate_2
        ]
        others = [norm_1 * (1.0 + vec[SCALE_1]), norm_2 * (1.0 + vec[SCALE_2]), d_bias_down]
        sliced = lambda t: t.reshape(dp_count, -1)
        d_mod = jnp.concatenate(d_mod, axis=1)
        d_cond = lax.dot_general(
            d_mod,
            w_all.astype(F32),
            (((1,), (1,)), ((), ())),
            precision=PRECISE,
            preferred_element_type=F32,
        ) * silu_slope(cond)
        table = jnp.concatenate(
            [sliced(d_mod)]
            + [sliced(t) for t in others]
            + [sliced(t) for half in (d_bias_b, d_bias_a) for t in half.reshape(2, -1)]
            + [jnp.broadcast_to(act, (dp_count, cond_size))],
            axis=1,
        )
    half = near.shape[-1] // 2
    if group.paired:
        step = [keep, group.bit(send, 0)]
        step, came, near = tie((step, came, near), sum_w)
        sum_w.settle()
        step = jnp.concatenate(step, axis=1)
        step = [step[0]] + [group.step(step[n], 2 * n) for n in range(1, dp_count // 2)]
    else:
        step = [lax.all_to_all(table, "dp", split_axis=0, concat_axis=0, tiled=True)]
    feeds = group.z(near[..., half:].astype(BF16), 2)
    near_w, far_w = sum_w.total
    far_w = group.z(far_w.astype(BF16), 1)
    step, far_w, feeds, came = lax.optimization_barrier((step, far_w, feeds, came))
    near_w = near_w + far_w.astype(F32)
    grad = group.z(near_w[..., cols:].astype(BF16), 2)
    length = step[0].shape[-1]
    d_cond = jnp.pad(d_cond, ((0, 0), (0, length - cond_size)))
    arrived = jnp.concatenate([t.reshape(-1, length) for t in step] + [d_cond])
    arrived = jnp.stack([arrived] + [group.z(arrived, k) for k in range(1, tensor_count)])
    grad = near_w[..., :cols] + grad.astype(F32)
    grad_qkv, grad_out = grad[:3], grad[3].T
    grad_up, grad_down = near[..., :half] + feeds.astype(F32)
    input_grad = group.held_rows(came)
    place = jnp.asarray([0, 2, 1, 3])[order]
    arrived = arrived[order]
    conds = arrived[:, dp_count, :cond_size]
    arrived = arrived[:, :dp_count]
    totals = jnp.sum(arrived[..., :edge], axis=(0, 1))
    biases = arrived[..., edge : edge + tensor_count * rows].reshape(
        tensor_count, dp_count, tensor_count, rows
    )
    wanted = (jnp.arange(tensor_count) == place[:, None])[:, None, :, None]
    grad_bias_up = jnp.sum(jnp.where(wanted, biases, 0.0), axis=(0, 1, 2))
    grad_bias_ada = totals[:mod_width]
    grad_gain_one, grad_gain_two, grad_bias_down = (
        totals[mod_width + n * rows : mod_width + (n + 1) * rows] for n in range(3)
    )
    arrived = arrived.reshape(dp_count * tensor_count, -1)
    grad_ada = lax.dot_general(
        arrived[:, -cond_size:],
        arrived[:, :mod_width],
        (((0,), (0,)), ((), ())),
        precision=PRECISE,
        preferred_element_type=F32,
    )
    cond_grad = jnp.take(conds, jnp.arange(per_dp) + d % 2, axis=0)
    return (
        block_out,
        input_grad,
        cond_grad,
        grad_qkv,
        grad_out,
        grad_up,
        grad_bias_up[None],
        grad_down.T,
        grad_bias_down,
        grad_gain_one,
        grad_gain_two,
        grad_ada,
        grad_bias_ada,
    )


def solution(mesh):
    return jax.shard_map(
        shards,
        mesh=mesh,
        in_specs=(
            P("dp", "tensor", None),
            P("dp", None),
            P("dp", None),
            P("dp", None),
            P(None, "dp", "tensor"),
            P("tensor", "dp"),
            P("dp", "tensor"),
            P("tensor", "dp"),
            P("tensor", "dp"),
            P("dp"),
            P("dp"),
            P("dp"),
            P(None, "dp"),
            P("dp"),
            P("dp", "tensor", None),
        ),
        out_specs=(
            P("dp", "tensor", None),
            P("dp", "tensor", None),
            P("dp", None),
            P(None, "dp", "tensor"),
            P("tensor", "dp"),
            P("dp", "tensor"),
            P("tensor", "dp"),
            P("tensor", "dp"),
            P("dp"),
            P("dp"),
            P("dp"),
            P(None, "dp"),
            P("dp"),
        ),
        check_vma=False,
    )
```

```python
from functools import partial

import jax
import jax.numpy as jnp
import numpy as np
from jax import lax
from jax.experimental import pallas as pl
from jax.experimental.pallas import tpu as pltpu
from jax.sharding import PartitionSpec as P

HEAD = 64
PRECISE = lax.Precision.HIGHEST
EPSILON = 1e-05
SHIFT_1, SCALE_1, GATE_1, SHIFT_2, SCALE_2, GATE_2, BIAS_OUT, GAIN_1, GAIN_2 = range(9)
F32 = jnp.float32
BF16 = jnp.bfloat16
PAIR = 2 * HEAD
BOTH = ("dp", "tensor")
ANY = pl.BlockSpec(memory_space=pl.ANY)
VMEM = pl.BlockSpec(memory_space=pltpu.VMEM)
SMEM = pl.BlockSpec(memory_space=pltpu.SMEM)


def dot_nn(a, b):
    return jnp.dot(a, b, preferred_element_type=F32)


def dot_nt(a, b):
    return lax.dot_general(a, b, (((1,), (1,)), ((), ())), preferred_element_type=F32)


VMEM_MIB = {'feed': 48, 'turn': 48, 'attend_back': 48, 'weight_grads': 48}


def params(name):
    return pltpu.CompilerParams(vmem_limit_bytes=VMEM_MIB.get(name, 58) << 20)


def cost(flops, nbytes, trans=0):
    return pl.CostEstimate(flops=int(flops), bytes_accessed=int(nbytes), transcendentals=int(trans))


def shape(dims, kind):
    return jax.ShapeDtypeStruct(tuple(dims), kind)


def row_at(me_ref, index, rows):
    return pl.multiple_of((me_ref[0] ^ index) * rows, rows)


def at_step(n, act):
    pl.when(pl.program_id(0) == n)(act)


def pick(refs, out, each=1):
    rows = refs[0].shape[0]
    for n, ref in enumerate(refs):
        at = pl.ds(n % each * rows, rows)
        at_step(n // each, lambda ref=ref, at=at: out.__setitem__((at, slice(None)), ref[...]))


def copy_out(refs, source):
    for n, ref in enumerate(refs):
        at_step(n, lambda ref=ref: ref.__setitem__(..., source[...]))


STEP = 256


def over_rows(count, act):
    size = min(STEP, count)

    @pl.loop(0, count // size)
    def _(i):
        act(pl.ds(pl.multiple_of(i * size, size), size))


def normed(x):
    centred = x - jnp.mean(x, axis=-1, keepdims=True)
    inverse = lax.rsqrt(jnp.mean(centred * centred, axis=-1, keepdims=True) + EPSILON)
    return centred * inverse, inverse


def clear_rows(ref):
    at_step(0, lambda: ref.__setitem__(..., jnp.zeros(ref.shape, ref.dtype)))


def add_row(ref, n, value):
    ref[n : n + 1, :] += value


def start_all(copies):
    def act():
        for copy in copies:
            copy.start()

    at_step(0, act)


def wait_all(copies):
    def act():
        for copy in copies:
            copy.wait()

    at_step(0, act)


def row_block(rows, cols):
    return pl.BlockSpec((rows, cols), lambda i: (i, 0))


def col_block(rows, cols):
    return pl.BlockSpec((rows, cols), lambda i: (0, i))


def vec_row(vec, n):
    return vec[n : n + 1, :]


def norm_scale(vec, gain, scale):
    return vec_row(vec, gain) * (1.0 + vec_row(vec, scale))


def rotary_kernel(places, frequencies, cos_flat, sin_a, sin_b, cos_t, sin_t):
    angle = frequencies[...] * places[...]
    cosine, sine = jnp.cos(angle), jnp.sin(angle)
    cos_t[...], sin_t[...] = cosine, sine
    nothing = jnp.zeros_like(sine)
    cos_flat[...] = jnp.concatenate([cosine] * 4, axis=0).T
    sin_a[...] = jnp.concatenate([-sine, nothing] * 2, axis=0).T
    sin_b[...] = jnp.concatenate([nothing, sine] * 2, axis=0).T


def rotary(places, frequencies):
    length, half = places.shape[1], frequencies.shape[0]
    return pl.pallas_call(
        rotary_kernel,
        out_shape=[shape((length, 4 * half), F32)] * 3 + [shape((half, length), F32)] * 2,
        in_specs=[VMEM] * 2,
        out_specs=[VMEM] * 5,
        compiler_params=params("rotary"),
        cost_estimate=cost(6e6, 2e6),
        name="rotary",
    )(places, frequencies)


class Held:
    def __init__(self, parts, rels, offset=0):
        self.parts, self.rels, self.offset = parts, rels, offset

    def blocks(self, refs):
        n = 0
        for ref, rel in zip(refs, self.rels):
            for i, j in enumerate(rel):
                yield ref.at[i + self.offset], j, n
                n += 1

    @property
    def count(self):
        return sum(len(rel) for rel in self.rels)


def qkv_copies(me, qk, vo, refs, w_buf, sems, rows):
    out = []
    parts = len(qk.parts)
    for held, group, planes in ((qk, refs[:parts], (0, 1)), (vo, refs[parts:], (2,))):
        for block, j, n in held.blocks(group):
            for c, plane in enumerate(planes):
                out.append(
                    pltpu.make_async_copy(
                        block.at[pl.ds(c * rows, rows), :],
                        w_buf.at[plane, pl.ds(row_at(me, j, rows), rows), :],
                        sems.at[plane, n],
                    )
                )
    return out


def qkv_kernel(qk, vo, me, *refs):
    x_refs, refs = refs[:4], refs[4:]
    (vec, cosine, sin_a, sin_b), refs = refs[:4], refs[4:]
    mul, add = norm_scale(vec, GAIN_1, SCALE_1), vec_row(vec, SHIFT_1)
    held, refs = refs[: 2 * len(qk.parts)], refs[2 * len(qk.parts) :]
    (n_t, k_out, v_out, q_t, k_t, v_t), (w_buf, x_buf, sems) = refs[:6], refs[6:]
    copies = qkv_copies(me, qk, vo, held, w_buf, sems, w_buf.shape[1] // qk.count)
    start_all(copies)
    pick(x_refs, x_buf, 2)

    def norm(rows):
        unit, _ = normed(x_buf[rows, :].astype(F32))
        x_buf[rows, :] = (unit * mul + add).astype(BF16)

    over_rows(x_buf.shape[0], norm)
    tokens = x_buf[...]
    n_t[...] = tokens.T
    wait_all(copies)
    width = k_out.shape[1]
    for c, (flat, turned, factor) in enumerate(((None, q_t, HEAD**-0.5), (k_out, k_t, 1.0))):
        proj = dot_nn(tokens, w_buf[c])
        for p in range(width // PAIR):
            lanes = slice(p * PAIR, (p + 1) * PAIR)
            r = proj[:, lanes]
            spun = (
                r * cosine[...]
                + pltpu.roll(r, PAIR - HEAD // 2, 1) * sin_a[...]
                + pltpu.roll(r, HEAD // 2, 1) * sin_b[...]
            )
            spun = spun.astype(BF16) * BF16(factor)
            if flat is not None:
                flat[:, lanes] = spun
            turned[lanes, :] = spun.T
    values = dot_nn(tokens, w_buf[2]).astype(BF16)
    v_out[...] = values
    v_t[...] = values.T


def qkv(me, x_parts, vec, cosine, sin_a, sin_b, qk, vo):
    part, width = x_parts[0].shape
    length = 4 * part
    cols = qk.parts[0].shape[2]
    flat, turned = shape((length, cols), BF16), shape((cols, length), BF16)
    return pl.pallas_call(
        partial(qkv_kernel, qk, vo),
        grid=(2,),
        out_shape=[shape((width, length), BF16), flat, flat, turned, turned, turned],
        in_specs=[SMEM]
        + [VMEM] * 5
        + [row_block(2 * part, PAIR)] * 3
        + [ANY] * (2 * len(qk.parts)),
        out_specs=[col_block(width, 2 * part)]
        + [row_block(2 * part, cols)] * 2
        + [col_block(cols, 2 * part)] * 3,
        scratch_shapes=[
            pltpu.VMEM((3, width, cols), BF16),
            pltpu.VMEM((2 * part, width), BF16),
            pltpu.SemaphoreType.DMA((3, qk.count)),
        ],
        compiler_params=params("qkv"),
        cost_estimate=cost(6 * length * width * cols, 16e6),
        name="qkv",
    )(me, *x_parts, vec, cosine, sin_a, sin_b, *qk.parts, *vo.parts)


def three_terms(v):
    rows = []
    for _ in range(3):
        rows.append(v.astype(BF16).astype(F32))
        v = v - rows[-1]
    rows += [jnp.zeros_like(v)] * 5
    return jnp.concatenate(rows, axis=0).astype(BF16)


DOCS, TERMS = 8, 16


def added_lanes(out, doc_col):
    lane = lax.broadcasted_iota(jnp.int32, out.shape, 1) % HEAD
    other = jnp.where(lane == doc_col[...], 0.0, -1e30)
    ones = jnp.where((lane >= TERMS) & (lane < TERMS + 3), 1.0, 0.0)
    out[...] = jnp.where(lane < DOCS, other, ones).astype(BF16)


def document_rows(doc_row):
    row = lax.broadcasted_iota(jnp.int32, (TERMS, doc_row.shape[1]), 0)
    return jnp.where(row == doc_row[...], 1.0, 0.0).astype(BF16)


def with_lanes(ref, added, head):
    lane = lax.broadcasted_iota(jnp.int32, (1, PAIR), 1)
    return jnp.where((lane // HEAD) == head, ref[...], added[...])


def with_rows(out, ref, head, rows):
    own, other = head * HEAD, (1 - head) * HEAD
    out[own : own + HEAD, :] = ref[own : own + HEAD, :]
    out[other : other + HEAD, :] = jnp.zeros((HEAD, out.shape[1]), BF16)
    for n, value in enumerate(rows):
        if value is not None:
            at = other + n * TERMS
            out[at : at + value.shape[0], :] = value


def attend_kernel(q_t, k, v_t, doc_row, doc_col, mix_t, log_sum, added, ahead):
    @pl.when(pl.program_id(0) == 0)
    def _():
        added_lanes(added, doc_col)

    docs = document_rows(doc_row)
    for h in range(2):
        with_rows(ahead.at[h], q_t, h, [docs])

    for h in range(2):
        rows = slice(h * HEAD, (h + 1) * HEAD)
        scores = dot_nn(with_lanes(k, added, h), ahead[h])
        top = jnp.max(scores, axis=0, keepdims=True)
        weights = jnp.exp(scores - top)
        total = jnp.sum(weights, axis=0, keepdims=True)
        mixed = dot_nn(v_t[rows, :], weights.astype(BF16))
        mix_t[rows, :] = (mixed / total).astype(BF16)
        log_sum[0, h] = top + jnp.log(total)


def attend(q_t, k, v_t, doc_row, doc_col):
    length, width = k.shape
    pairs = width // PAIR
    flat = pl.BlockSpec((length, PAIR), lambda i: (0, i))
    turned = pl.BlockSpec((PAIR, length), lambda i: (i, 0))
    return pl.pallas_call(
        attend_kernel,
        grid=(pairs,),
        in_specs=[
            turned,
            flat,
            turned,
            pl.BlockSpec((1, length), lambda i: (0, 0)),
            pl.BlockSpec((length, 1), lambda i: (0, 0)),
        ],
        out_specs=[turned, pl.BlockSpec((1, 2, 1, length), lambda i: (i, 0, 0, 0))],
        out_shape=[shape((width, length), BF16), shape((pairs, 2, 1, length), F32)],
        scratch_shapes=[pltpu.VMEM((length, PAIR), BF16), pltpu.VMEM((2, PAIR, length), BF16)],
        compiler_params=params("attend"),
        cost_estimate=cost(16 * length * length * width, 8e6),
        name="attend",
    )(q_t, k, v_t, doc_row, doc_col)


def load_out_weight(me, vo, refs, buf, sems):
    rows = buf.shape[0] // vo.count
    copies = [
        pltpu.make_async_copy(
            block.at[pl.ds(rows, rows), :], buf.at[pl.ds(row_at(me, j, rows), rows), :], sems.at[n]
        )
        for block, j, n in vo.blocks(refs)
    ]
    start_all(copies)
    return copies


def middle_kernel(vo, me, *refs):
    x_refs, g_refs, refs = refs[:4], refs[4:8], refs[8:]
    (mix_t, vec), refs = refs[:2], refs[2:]
    mul, add = norm_scale(vec, GAIN_2, SCALE_2), vec_row(vec, SHIFT_2)
    gate_one, gate_two = vec_row(vec, GATE_1), vec_row(vec, GATE_2)
    pieces, refs = refs[: len(vo.parts)], refs[len(vo.parts) :]
    (att, n_two, n_two_t, d_down, d_down_t, d_bias, mix), (w_buf, x_buf, sems) = refs[:7], refs[7:]
    copies = load_out_weight(me, vo, pieces, w_buf, sems)
    pick(g_refs, x_buf)

    def scale(rows):
        scaled = x_buf[rows, :].astype(F32) * gate_two
        add_row(d_bias, 0, jnp.sum(scaled, axis=0, keepdims=True))
        d_down[rows, :] = scaled.astype(BF16)

    clear_rows(d_bias)
    over_rows(x_buf.shape[0], scale)
    d_down_t[...] = d_down[...].T
    pick(x_refs, x_buf)
    wait_all(copies)
    mix[...] = mix_t[...].T
    att[...] = dot_nt(mix[...], w_buf[...])

    def norm(rows):
        unit, _ = normed(x_buf[rows, :].astype(F32) + gate_one * att[rows, :])
        n_two[rows, :] = (unit * mul + add).astype(BF16)

    over_rows(x_buf.shape[0], norm)
    n_two_t[...] = n_two[...].T


def middle(me, x_parts, g_parts, mix_t, vec, vo):
    part, width = x_parts[0].shape
    length = 4 * part
    inner = mix_t.shape[0]
    flat, turned = shape((length, width), BF16), shape((width, length), BF16)
    return pl.pallas_call(
        partial(middle_kernel, vo),
        grid=(4,),
        out_shape=[shape((length, width), F32), flat, turned, flat, turned]
        + [shape((1, width), F32), shape((length, inner), BF16)],
        in_specs=[SMEM]
        + [VMEM] * 8
        + [col_block(inner, part), VMEM]
        + [ANY] * len(vo.parts),
        out_specs=[
            row_block(part, width),
            row_block(part, width),
            col_block(width, part),
            row_block(part, width),
            col_block(width, part),
            VMEM,
            row_block(part, inner),
        ],
        scratch_shapes=[
            pltpu.VMEM((width, inner), BF16),
            pltpu.VMEM((part, width), BF16),
            pltpu.SemaphoreType.DMA((vo.count,)),
        ],
        compiler_params=params("middle"),
        cost_estimate=cost(2 * length * width * inner, 16e6),
        name="middle",
    )(me, *x_parts, *g_parts, mix_t, vec, *vo.parts)


def spread_rows(me, value, stage, keep, send=None):
    blocks, rows = stage.shape[0], stage.shape[1]
    for j in range(blocks):
        stage[j] = value[j * rows : (j + 1) * rows, :].astype(BF16)
    for j in range(blocks):
        block = stage[me[0] ^ j]
        if j % 2 == 0:
            keep(j // 2, block)
        else:
            send(j // 2, block)


def slot_of(stream, slot, count):
    if stream == 0 and count == 4:
        slot = (0, 2, 1, 3)[slot]
    return slot


def writer(ref, stream):
    def put(slot, block):
        ref[stream, slot_of(stream, slot, ref.shape[1])] = block

    return put


def split_writer(ref, *lead):
    def put(slot, block):
        half = block.shape[-1] // 2
        for s in range(2):
            ref[(s, slot_of(s, slot, ref.shape[1]), *lead)] = block[:, s * half : (s + 1) * half]

    return put


C_ROOT = 0.7978845608028654
C_CUBE = 0.044715


def feed_kernel(up, dn, steps, first, me, *refs):
    (n_two, n_two_t, d_down, d_down_t, bias), refs = refs[:5], refs[5:]
    if not first:
        (down_in, d_n_in), refs = refs[:2], refs[2:]
    parts = len(up.parts)
    up_refs, down_refs, refs = refs[:parts], refs[parts : 2 * parts], refs[2 * parts :]
    (down, d_n, d_bias, *grads), (w_buf, stage, sems) = refs[:-3], refs[-3:]
    step = pl.program_id(0)
    rows = up_refs[0].shape[1]
    chunk = w_buf.shape[3]
    offset = 0 if first else steps * chunk

    def copies(s):
        out = []
        for m, (held, group) in enumerate(((up, up_refs), (dn, down_refs))):
            for block, j, n in held.blocks(group):
                out.append(
                    pltpu.make_async_copy(
                        block.at[:, pl.ds(offset + s * chunk, chunk)],
                        w_buf.at[m, s, pl.ds(row_at(me, j, rows), rows), :],
                        sems.at[m, s, n],
                    )
                )
        return out

    @pl.when(step == 0)
    def _():
        for s in range(steps):
            for copy in copies(s):
                copy.start()
        if first:
            down[...] = jnp.zeros_like(down)
            d_n[...] = jnp.zeros_like(d_n)
        else:
            down[...] = down_in[...]
            d_n[...] = d_n_in[...]

    for s in range(steps):

        @pl.when(step == s)
        def _():
            for copy in copies(s):
                copy.wait()

    w_up = w_buf[0, step]
    w_down_t = w_buf[1, step]
    h = dot_nn(n_two[...], w_up) + bias[0]
    square = h * h
    t = jnp.tanh(C_ROOT * h * (1.0 + C_CUBE * square))
    half = 0.5 + 0.5 * t
    act = (h * half).astype(BF16)
    slope = half + (0.5 * C_ROOT) * h * (1.0 - t * t) * (1.0 + (3.0 * C_CUBE) * square)
    d_h = (dot_nn(d_down[...], w_down_t) * slope).astype(BF16)
    d_bias[0] = jnp.sum(d_h.astype(F32), axis=0, keepdims=True)
    down[...] += dot_nt(act, w_down_t)
    d_n[...] += dot_nt(d_h, w_up)
    for m, grad in ((0, dot_nn(n_two_t[...], d_h)), (1, dot_nn(d_down_t[...], act))):
        spread_rows(me, grad, stage, *(writer(ref, m) for ref in grads))


def feed(me, n_two, n_two_t, d_down, d_down_t, bias, up, dn, start, before, units):
    blocks = up.count
    length, width = n_two.shape
    chunk = 512 if units % 512 == 0 else units
    steps = units // chunk
    first = before is None
    rows = width // blocks
    one = pl.Buffered(1)
    flat = pl.BlockSpec((length, width), lambda i: (0, 0), pipeline_mode=one)
    turned = pl.BlockSpec((width, length), lambda i: (0, 0), pipeline_mode=one)
    held = pl.BlockSpec((length, width), lambda i: (0, 0))
    half = max(blocks // 2, 1)
    grad = pl.BlockSpec((2, half, rows, chunk), lambda i: (0, 0, 0, i))
    grads = 1 if blocks == 1 else 2
    bias_spec = pl.BlockSpec((1, 1, chunk), lambda i: (i + start // chunk, 0, 0))
    return pl.pallas_call(
        partial(feed_kernel, up, dn, steps, first),
        grid=(steps,),
        in_specs=[SMEM, flat, turned, flat, turned, bias_spec]
        + ([] if first else [flat, flat])
        + [ANY] * (2 * len(up.parts)),
        out_specs=[held, held, pl.BlockSpec((1, 1, chunk), lambda i: (i, 0, 0))] + [grad] * grads,
        out_shape=[shape((length, width), F32)] * 2
        + [shape((steps, 1, chunk), F32)]
        + [shape((2, half, rows, units), BF16)] * grads,
        scratch_shapes=[
            pltpu.VMEM((2, steps, width, chunk), BF16),
            pltpu.VMEM((blocks, rows, chunk), BF16),
            pltpu.SemaphoreType.DMA((2, steps, blocks)),
        ],
        compiler_params=params("feed"),
        cost_estimate=cost(12 * length * width * units, 20e6),
        name="feed",
    )(
        me,
        n_two,
        n_two_t,
        d_down,
        d_down_t,
        bias.reshape(-1, 1, chunk),
        *(() if first else before),
        *up.parts,
        *dn.parts,
    )


def turn_kernel(vo, me, *refs):
    x_refs, g_refs, refs = refs[:4], refs[4:8], refs[8:]
    (att, down, d_n, vec), refs = refs[:4], refs[4:]
    mul, bias = norm_scale(vec, GAIN_2, SCALE_2), vec_row(vec, BIAS_OUT)
    gate_one, gate_two = vec_row(vec, GATE_1), vec_row(vec, GATE_2)
    pieces, refs = refs[: len(vo.parts)], refs[len(vo.parts) :]
    out_refs, (d_mid, d_mix_t, sums, d_att_t), (w_buf, x_buf, g_buf, d_att, sems) = (
        refs[:4],
        refs[4:8],
        refs[8:],
    )
    copies = load_out_weight(me, vo, pieces, w_buf, sems)
    pick(g_refs, g_buf)
    pick(x_refs, x_buf)
    clear_rows(sums)

    def back(rows):
        g = g_buf[rows, :].astype(F32)
        attention = att[rows, :]
        mid = x_buf[rows, :].astype(F32) + gate_one * attention
        branch = down[rows, :] + bias
        x_buf[rows, :] = (mid + gate_two * branch).astype(BF16)
        add_row(sums, 0, jnp.sum(g * branch, axis=0, keepdims=True))
        unit, inverse = normed(mid)
        dn = d_n[rows, :]
        dn_unit = dn * unit
        add_row(sums, 1, jnp.sum(dn_unit, axis=0, keepdims=True))
        add_row(sums, 2, jnp.sum(dn, axis=0, keepdims=True))
        du = dn * mul
        dm = g + inverse * (
            du
            - jnp.mean(du, axis=-1, keepdims=True)
            - unit * jnp.mean(dn_unit * mul, axis=-1, keepdims=True)
        )
        d_mid[rows, :] = dm
        add_row(sums, 3, jnp.sum(dm * attention, axis=0, keepdims=True))
        d_att[rows, :] = (dm * gate_one).astype(BF16)

    over_rows(x_buf.shape[0], back)
    copy_out(out_refs, x_buf)
    d_att_t[...] = d_att[...].T
    wait_all(copies)
    d_mix_t[...] = dot_nn(d_att[...], w_buf[...]).astype(BF16).T


def turn(me, x_parts, g_parts, att, down, d_n, vec, vo):
    part, width = x_parts[0].shape
    length = 4 * part
    inner = vo.parts[0].shape[2]
    return pl.pallas_call(
        partial(turn_kernel, vo),
        grid=(4,),
        out_shape=[shape((part, width), BF16)] * 4
        + [
            shape((length, width), F32),
            shape((inner, length), BF16),
            shape((4, width), F32),
            shape((width, length), BF16),
        ],
        in_specs=[SMEM]
        + [VMEM] * 8
        + [row_block(part, width)] * 3
        + [VMEM]
        + [ANY] * len(vo.parts),
        out_specs=[VMEM] * 4
        + [
            row_block(part, width),
            col_block(inner, part),
            VMEM,
            col_block(width, part),
        ],
        scratch_shapes=[
            pltpu.VMEM((width, inner), BF16),
            pltpu.VMEM((part, width), BF16),
            pltpu.VMEM((part, width), BF16),
            pltpu.VMEM((part, width), BF16),
            pltpu.SemaphoreType.DMA((vo.count,)),
        ],
        compiler_params=params("turn"),
        cost_estimate=cost(2 * length * width * inner, 24e6),
        name="turn",
    )(
        me, *x_parts, *g_parts, att, down, d_n, vec, *vo.parts
    )


def attend_back_kernel(
    k, v, q_t, k_t, d_mix_t, mix_t, log_sum, doc_row, doc_col, cos_t, sin_t,
    dq, dk, dv, added, ahead, dq_acc, dk_acc, dv_acc,
):
    @pl.when(pl.program_id(0) == 0)
    def _():
        added_lanes(added, doc_col)

    length = k.shape[0]
    block = 256 if length % 256 == 0 else length
    docs = document_rows(doc_row)
    for h in range(2):
        rows = slice(h * HEAD, (h + 1) * HEAD)
        row_dot = jnp.sum(
            d_mix_t[rows, :].astype(F32) * mix_t[rows, :].astype(F32), axis=0, keepdims=True
        )
        with_rows(ahead.at[h, 0], q_t, h, [docs, three_terms(-log_sum[0, h])])
        with_rows(ahead.at[h, 1], d_mix_t, h, [None, three_terms(-row_dot)])

    for h in range(2):
        rows = slice(h * HEAD, (h + 1) * HEAD)
        keys, values = with_lanes(k, added, h), with_lanes(v, added, h)
        for b in range(length // block):
            c = slice(b * block, (b + 1) * block)
            probs = jnp.exp(dot_nn(keys[c], ahead[h, 0]))
            d_scores = (probs * dot_nn(values[c], ahead[h, 1])).astype(BF16)
            dv_acc[rows, c] = dot_nt(d_mix_t[rows, :], probs.astype(BF16))
            dk_acc[rows, c] = dot_nt(q_t[rows, :], d_scores)
            dq_part = dot_nn(k_t[rows, c], d_scores)
            if b == 0:
                dq_acc[rows, :] = dq_part
            else:
                dq_acc[rows, :] += dq_part

    half = HEAD // 2
    for acc, out, factor in ((dq_acc, dq, HEAD**-0.5), (dk_acc, dk, 1.0)):
        turned = []
        for h in range(2):
            a = acc[h * HEAD : h * HEAD + half, :] * factor
            b = acc[h * HEAD + half : (h + 1) * HEAD, :] * factor
            turned.append(a * cos_t[...] + b * sin_t[...])
            turned.append(b * cos_t[...] - a * sin_t[...])
        out[...] = jnp.concatenate(turned, axis=0).astype(BF16).T
    dv[...] = dv_acc[...].astype(BF16).T


def attend_back(k, v, q_t, k_t, d_mix_t, mix_t, log_sum, doc_row, doc_col, cos_t, sin_t):
    length, width = k.shape
    count = width // PAIR
    flat = pl.BlockSpec((length, PAIR), lambda i: (0, i))
    turned = pl.BlockSpec((PAIR, length), lambda i: (i, 0))
    fixed = lambda a: pl.BlockSpec(a.shape, lambda i: (0, 0))
    return pl.pallas_call(
        attend_back_kernel,
        grid=(count,),
        in_specs=[flat] * 2
        + [turned] * 4
        + [pl.BlockSpec((1, 2, 1, length), lambda i: (i, 0, 0, 0))]
        + [fixed(a) for a in (doc_row, doc_col, cos_t, sin_t)],
        out_specs=[flat] * 3,
        out_shape=[shape((length, width), BF16)] * 3,
        scratch_shapes=[
            pltpu.VMEM((length, PAIR), BF16),
            pltpu.VMEM((2, 2, PAIR, length), BF16),
        ]
        + [pltpu.VMEM((PAIR, length), F32)] * 3,
        compiler_params=params("attend_back"),
        cost_estimate=cost(28 * length * length * width, 14e6),
        name="attend_back",
    )(k, v, q_t, k_t, d_mix_t, mix_t, log_sum, doc_row, doc_col, cos_t, sin_t)


def first_kernel(qk, vo, me, *refs):
    x_refs, refs = refs[:4], refs[4:]
    (d_mid, vec, dq, dk, dv), refs = refs[:5], refs[5:]
    mul = norm_scale(vec, GAIN_1, SCALE_1)
    held, refs = refs[: 2 * len(qk.parts)], refs[2 * len(qk.parts) :]
    out_refs, (sums, w_buf, x_buf, d_n, sems) = refs[:4], refs[4:]
    copies = qkv_copies(me, qk, vo, held, w_buf, sems, w_buf.shape[1] // qk.count)
    start_all(copies)
    pick(x_refs, x_buf)
    clear_rows(sums)
    wait_all(copies)
    d_n[...] = dot_nt(dq[...], w_buf[0]) + dot_nt(dk[...], w_buf[1]) + dot_nt(dv[...], w_buf[2])

    def back(rows):
        unit, inverse = normed(x_buf[rows, :].astype(F32))
        dn = d_n[rows, :]
        dn_unit = dn * unit
        du = dn * mul
        x_buf[rows, :] = (
            d_mid[rows, :]
            + inverse
            * (
                du
                - jnp.mean(du, axis=-1, keepdims=True)
                - unit * jnp.mean(dn_unit * mul, axis=-1, keepdims=True)
            )
        ).astype(BF16)
        add_row(sums, 0, jnp.sum(dn_unit, axis=0, keepdims=True))
        add_row(sums, 1, jnp.sum(dn, axis=0, keepdims=True))

    over_rows(x_buf.shape[0], back)
    copy_out(out_refs, x_buf)


def first(me, x_parts, d_mid, vec, dq, dk, dv, qk, vo):
    part, width = x_parts[0].shape
    length = 4 * part
    cols = dq.shape[1]
    return pl.pallas_call(
        partial(first_kernel, qk, vo),
        grid=(4,),
        out_shape=[shape((part, width), BF16)] * 4 + [shape((2, width), F32)],
        in_specs=[SMEM]
        + [VMEM] * 4
        + [row_block(part, width), VMEM]
        + [row_block(part, cols)] * 3
        + [ANY] * (2 * len(qk.parts)),
        out_specs=[VMEM] * 5,
        scratch_shapes=[
            pltpu.VMEM((3, width, cols), BF16),
            pltpu.VMEM((part, width), BF16),
            pltpu.VMEM((part, width), F32),
            pltpu.SemaphoreType.DMA((3, qk.count)),
        ],
        compiler_params=params("first"),
        cost_estimate=cost(6 * length * width * cols, 20e6),
        name="first",
    )(me, *x_parts, d_mid, vec, dq, dk, dv, *qk.parts, *vo.parts)


def modulate_kernel(qk, vo, zones, me, act, *refs):
    parts = len(qk.parts)
    qk_refs, vo_refs, (vec, bias, ada, small, sems) = refs[:parts], refs[parts:-5], refs[-5:]
    count = qk.count
    rows = ada.shape[0] // count
    cut = rows // 2
    copies = []
    for h, (held, group) in enumerate(((qk, qk_refs), (vo, vo_refs))):
        for block, j, n in held.blocks(group):
            at = row_at(me, j, rows) + h * cut
            copies.append(
                pltpu.make_async_copy(
                    block.at[pl.ds(2 * rows, cut), :], ada.at[pl.ds(at, cut), :], sems.at[h, n]
                )
            )
            if h:
                copies.append(
                    pltpu.make_async_copy(
                        block.at[pl.ds(2 * rows + cut, 16), :],
                        small.at[pl.ds(row_at(me, j, 16), 16), :],
                        sems.at[2, n],
                    )
                )
    for copy in copies:
        copy.start()
    for copy in copies:
        copy.wait()
    kinds = ada.shape[1] // act.shape[1]
    act3 = three_terms(act[...])
    across = vec.shape[1] // rows
    vec[...] = jnp.zeros_like(vec)
    for k in range(kinds):
        lanes = slice(k * act.shape[1], (k + 1) * act.shape[1])
        found = jnp.sum(dot_nt(act3, ada[:, lanes]), axis=0, keepdims=True)
        for d in range(count):
            m = d * kinds + k
            at = (m % across) * rows
            extra = small[d * 16 : (d + 1) * 16, :].astype(F32)
            vec[m // across : m // across + 1, at : at + rows] = (
                found[:, d * rows : (d + 1) * rows] + extra[1:2, k * rows : (k + 1) * rows]
            )
    for d in range(count):
        extra = small[d * 16 : (d + 1) * 16, :].astype(F32)
        here = slice(d * rows, (d + 1) * rows)
        for n in range(3):
            vec[BIAS_OUT + n : BIAS_OUT + n + 1, here] = extra[2:3, n * rows : (n + 1) * rows]
        for n in range(zones):
            far = (n - zones // 2) % zones
            at = n * (extra.shape[1] // zones)
            bias[far : far + 1, here] = extra[0:1, at : at + rows]


def modulate(me, act, qk, vo, zones, rows):
    width = qk.parts[0].shape[2]
    return pl.pallas_call(
        partial(modulate_kernel, qk, vo, zones),
        out_shape=[
            shape((16, width), F32),
            shape((zones, width), F32),
            shape((qk.count * rows, width), BF16),
        ],
        in_specs=[SMEM, VMEM] + [ANY] * (len(qk.parts) + len(vo.parts)),
        out_specs=[VMEM] * 3,
        scratch_shapes=[
            pltpu.VMEM((qk.count * 16, width), BF16),
            pltpu.SemaphoreType.DMA((3, qk.count)),
        ],
        compiler_params=params("modulate"),
        cost_estimate=cost(2e7, 4e6),
        name="modulate",
    )(me, act, *qk.parts, *vo.parts)


def gather_up_kernel(
    count, me, vec, ada, sums, sums_one, d_bias_down, d_bias_b, d_bias_a, act, cond,
    keep, send, d_cond, out, spread, bias_grad
):
    width = vec.shape[1]
    rows = width // count
    size = act.shape[1]
    kinds = ada.shape[1] // size
    norm_1, norm_2 = sums_one[0:1, :], sums[1:2, :]
    d_mod = (
        sums_one[1:2, :],
        norm_1 * vec_row(vec, GAIN_1),
        sums[3:4, :],
        sums[2:3, :],
        norm_2 * vec_row(vec, GAIN_2),
        sums[0:1, :],
    )
    others = (
        norm_1 * (1.0 + vec_row(vec, SCALE_1)),
        norm_2 * (1.0 + vec_row(vec, SCALE_2)),
        d_bias_down[...],
    )
    out[...] = jnp.zeros_like(out)
    chunk = d_bias_a.shape[2]
    for n, ref in enumerate((d_bias_b, d_bias_a)):
        for c in range(ref.shape[0]):
            at = c * chunk
            while at < (c + 1) * chunk:
                zone = at // width
                to = min((c + 1) * chunk, (zone + 1) * width)
                bias_grad[2 * n + zone : 2 * n + zone + 1, at - zone * width : to - zone * width] = (
                    ref[c][:, at - c * chunk : to - c * chunk]
                )
                at = to
    base = (kinds + 3) * rows
    for d in range(count):
        here = slice(d * rows, (d + 1) * rows)
        for k in range(kinds):
            m = d * kinds + k
            at = (m % count) * rows
            piece = d_mod[m // count][:, at : at + rows]
            out[d, :, k * rows : (k + 1) * rows] = piece
            spread[k : k + 1, here] = piece
        for n, value in enumerate(others):
            at = (kinds + n) * rows
            out[d, :, at : at + rows] = value[:, here]
        for n in range(bias_grad.shape[0]):
            at = base + n * rows
            out[d, :, at : at + rows] = bias_grad[n : n + 1, here]
        out[d, :, out.shape[2] - size :] = act[...]
    total = jnp.zeros(act.shape, F32)
    for k in range(kinds):
        three = three_terms(spread[k : k + 1, :])
        total += jnp.sum(dot_nn(three, ada[:, k * size : (k + 1) * size]), axis=0, keepdims=True)
    c = cond[...]
    sig = 1.0 / (1.0 + jnp.exp(-c))
    d_cond[...] = total * (sig * (1.0 + c * (1.0 - sig)))

    for j in range(count // 2):
        keep[j] = out[me[0] ^ (2 * j)]
        send[j] = out[me[0] ^ (2 * j + 1)]


def gather_up(me, vec, ada, sums, sums_one, d_bias_down, d_bias_b, d_bias_a, act, cond, count, length):
    return pl.pallas_call(
        partial(gather_up_kernel, count),
        out_shape=[shape((count // 2, 1, length), F32)] * 2 + [shape(act.shape, F32)],
        in_specs=[SMEM] + [VMEM] * 9,
        out_specs=[VMEM] * 3,
        scratch_shapes=[
            pltpu.VMEM((count, 1, length), F32),
            pltpu.VMEM((8, vec.shape[1]), F32),
            pltpu.VMEM((4, vec.shape[1]), F32),
        ],
        compiler_params=params("gather_up"),
        cost_estimate=cost(2e7, 4e6),
        name="gather_up",
    )(me, vec, ada, sums, sums_one, d_bias_down, d_bias_b, d_bias_a, act, cond)


def weight_grads_kernel(me, n_t, d_att_t, dq, dk, dv, mix_t, *refs):
    *grads, left, right, stage, sems = refs
    copies = [
        pltpu.make_async_copy(ref, held, sems.at[n])
        for n, (ref, held) in enumerate(
            (
                (n_t, left.at[0]),
                (dq, right.at[0]),
                (dk, right.at[1]),
                (dv, right.at[2]),
                (d_att_t, left.at[1]),
                (mix_t, right.at[3]),
            )
        )
    ]
    start_all(copies)
    wait_all(copies[:2])
    at_step(1, copies[2].wait)
    at_step(2, copies[3].wait)

    def last():
        copies[4].wait()
        copies[5].wait()

    at_step(3, last)
    step = pl.program_id(0)
    grad = dot_nn(left[jnp.where(step == 3, 1, 0)], right[step])
    spread_rows(me, grad, stage, *(split_writer(ref, 0) for ref in grads))


def weight_grads(me, n_t, d_att_t, dq, dk, dv, mix, blocks):
    width, length = n_t.shape
    cols = dq.shape[1]
    rows = width // blocks
    half = max(blocks // 2, 1)
    grads = 1 if blocks == 1 else 2
    return pl.pallas_call(
        weight_grads_kernel,
        grid=(4,),
        out_shape=[shape((2, half, 4, rows, cols // 2), BF16)] * grads,
        in_specs=[SMEM] + [ANY] * 6,
        out_specs=[
            pl.BlockSpec((2, half, 1, rows, cols // 2), lambda i: (0, 0, i, 0, 0))
        ]
        * grads,
        scratch_shapes=[
            pltpu.VMEM((2, width, length), BF16),
            pltpu.VMEM((4, length, cols), BF16),
            pltpu.VMEM((blocks, rows, cols), BF16),
            pltpu.SemaphoreType.DMA((6,)),
        ],
        compiler_params=params("weight_grads"),
        cost_estimate=cost(8 * length * width * cols, 14e6),
        name="weight_grads",
    )(me, n_t, d_att_t, dq, dk, dv, mix)


class Group:
    def __init__(self, dp_count, tensor_count, per_dp):
        self.dp, self.tensor, self.per_dp = dp_count, tensor_count, per_dp
        self.d, self.r = lax.axis_index("dp"), lax.axis_index("tensor")
        self.paired = dp_count == 8

    def bit(self, v, b):
        return lax.ppermute(v, "dp", [(i, i ^ (1 << b)) for i in range(self.dp)])

    def step(self, v, k):
        return lax.ppermute(v, "dp", [(i, i ^ k) for i in range(self.dp)])

    def z(self, v, k):
        return lax.ppermute(v, "tensor", [(i, i ^ k) for i in range(self.tensor)])

    def owns(self, d, r):
        return 0 <= r - d % 2 < self.per_dp

    def for_owner(self, rows, zero_idle):
        mine = self.r - self.d % 2
        top = self.per_dp - 1
        own = lax.dynamic_index_in_dim(rows, jnp.clip(mine, 0, top), 0, keepdims=False)
        if zero_idle:
            own = jnp.where((mine >= 0) & (mine <= top), own, jnp.zeros_like(own))
        parts = [own]
        for k in range(1, self.tensor):
            want = (self.r ^ k) - self.d % 2
            parts.append(
                lax.dynamic_index_in_dim(rows, jnp.clip(want, 0, top), 0, keepdims=False)
            )
        return parts

    def ship(self, v, k, to_owner):
        pairs = [
            (d * self.tensor + r, d * self.tensor + (r ^ k))
            for d in range(self.dp)
            for r in range(self.tensor)
            if self.owns(d, r ^ k if to_owner else r)
        ]
        return lax.ppermute(v, BOTH, pairs)

    def held_rows(self, came):
        stack = jnp.stack(came)
        return jnp.stack(
            [
                lax.dynamic_index_in_dim(stack, self.r ^ (j + self.d % 2), 0, keepdims=False)
                for j in range(self.per_dp)
            ]
        )

    def z_pair(self, v, got):
        return jnp.concatenate([v, got], axis=-1)

    def gather_pair(self, v, got, order):
        pair = jnp.stack([v, got])
        return [pair, self.bit(pair, order[1])]

    def gather_cores(self, parts, order):
        one, two = (1 << b for b in order)
        rels = [(0, one), (two, one ^ two)]
        rels += [tuple(j ^ 1 for j in rel) for rel in rels]
        return Held(parts + [self.bit(p, 0) for p in parts], rels)

    def gather_cores_joined(self, pairs, orders):
        near = jnp.concatenate([p for pair in pairs for p in pair])
        far = self.bit(near, 0)
        held = []
        for n, order in enumerate(orders):
            one, two = (1 << b for b in order)
            rel = (0, one, two, one ^ two)
            held.append(Held([near, far], [rel, tuple(j ^ 1 for j in rel)], 4 * n))
        return held

    def whole(self, v, axis):
        return lax.all_gather(v, "dp", axis=axis, tiled=True)


class Flight:
    def __init__(self, value):
        self.value = value


class Sum:
    def __init__(self, group, keep, send=None):
        self.group, self.stage, self.flights, self.terms = group, 0, [], []
        if not group.paired:
            value = keep[:, 0].astype(F32)
            value = lax.psum_scatter(value, "dp", scatter_dimension=value.ndim - 2, tiled=True)
            self.total = [value[0], value[1]]
            return
        self.terms = [[keep], [keep]]
        flight = Flight(group.bit(send, 0))
        self.flights = [(flight, 0), (flight, 1)]

    def settle(self):
        for terms, (flight, at) in zip(self.terms, self.flights):
            terms.append(flight.value if self.stage == 0 else flight.value[at])
        if self.flights and self.stage == 2:
            self.total = [sum(t[0].astype(F32) for t in terms) for terms in self.terms]
        self.flights = []

    def split(self):
        out = []
        for n, order in enumerate(((1, 2), (2, 1))):
            b = order[self.stage]
            if self.stage:
                stay, go = [t[:1] for t in self.terms[n]], [t[1:] for t in self.terms[n]]
            else:
                stay, go = [t[n, :2] for t in self.terms[n]], [t[n, 2:] for t in self.terms[n]]
            self.terms[n] = stay
            out.append((b, sum(t.astype(F32) for t in go).astype(BF16)))
        self.stage += 1
        self.flights = [None, None]
        return out


def exchange(*sums):
    links = {}
    for t in sums:
        t.settle()
        if t.group.paired:
            for n, (b, go) in enumerate(t.split()):
                links.setdefault(b, []).append((t, n, go))
    for b, items in links.items():
        blocks = [go for _, _, go in items]
        blocks = blocks[0] if len(blocks) == 1 else jnp.concatenate(blocks)
        flight, at = Flight(items[0][0].group.bit(blocks, b)), 0
        for t, n, go in items:
            t.flights[n] = (flight, slice(at, at + go.shape[0]))
            at += go.shape[0]


def tie(value, *sums):
    flights = {id(f): f for t in sums for f, _ in t.flights}
    flights = list(flights.values())
    value, arrived = lax.optimization_barrier((value, [f.value for f in flights]))
    for flight, v in zip(flights, arrived):
        flight.value = v
    return value


def silu_slope(c):
    sig = jax.nn.sigmoid(c)
    return sig * (1.0 + c * (1.0 - sig))


def shards(
    inputs, condition, doc_ids, positions, w_qkv, w_out, w_up, bias_up, w_down, bias_down,
    gain_one, gain_two, w_ada, bias_ada, out_grad,
):
    dp_count = lax.axis_size("dp")
    tensor_count = lax.axis_size("tensor")
    per_dp, part, width = inputs.shape
    length = doc_ids.shape[1]
    rows = w_up.shape[0]
    group = Group(dp_count, tensor_count, per_dp)
    blocks = dp_count if group.paired else 1
    d, r = group.d, group.r
    me = jnp.where(group.paired, d, 0).astype(jnp.int32).reshape(1)
    mine = jnp.clip(r - d % 2, 0, per_dp - 1)
    own_row = lambda v: lax.dynamic_index_in_dim(v, mine, 0, keepdims=False)
    join = lambda parts: jnp.concatenate(parts, axis=-1)

    order = r ^ jnp.arange(tensor_count)
    mixed = lambda v: own_row(v).reshape(tensor_count, part)[order].reshape(-1)
    docs, places = mixed(doc_ids), mixed(positions)
    doc_row, doc_col = docs[None, :], docs[:, None]
    frequencies = 10000.0 ** (-2.0 * jnp.arange(HEAD // 2, dtype=F32) / HEAD)
    cos_flat, sin_a, sin_b, cos_t, sin_t = rotary(
        places.astype(F32)[None, :], frequencies[:, None]
    )

    cols, cond_size, mod_width = w_qkv.shape[2], w_ada.shape[0], w_ada.shape[1]
    ways = (1, 2), (2, 1)
    cond = own_row(condition).astype(F32)[None]
    act = jax.nn.silu(cond)
    early = jnp.concatenate([w_qkv.reshape(-1, cols), w_out.T])
    late = jnp.concatenate([w_up, w_down.T])
    if group.paired:
        early = jnp.concatenate([early, jnp.pad(bias_up, ((0, 15), (0, cols - rows)))])
    if group.paired:
        ada = w_ada.T.reshape(-1, rows, cond_size).transpose(1, 0, 2).reshape(rows, width)
        cut, top = rows // 2, 2 * rows
        wide = lambda v: jnp.pad(v, (0, width - v.shape[0]))[None]
    x_parts, g_parts = group.for_owner(inputs, False), group.for_owner(out_grad, True)
    early = group.z_pair(early, group.z(early, 2))
    early = join([early, group.z(early, 1)])
    turns = cos_flat, sin_a, sin_b, cos_t, sin_t, doc_row, doc_col
    late, early, x_parts, g_parts = lax.optimization_barrier((late, early, x_parts, g_parts))
    late_got = group.z(late, 2)
    if group.paired:
        small = jnp.concatenate(
            [
                early[2 * top : 2 * top + 1],
                wide(bias_ada),
                wide(jnp.concatenate([bias_down, gain_one, gain_two])),
                early[2 * top + 3 :],
            ]
        )
        firsts = (
            jnp.concatenate([early[:top], ada[:cut], jnp.zeros_like(small)]),
            jnp.concatenate([early[top : 2 * top], ada[cut:], small]),
        )
        came = [group.bit(v, way[0]) for v, way in zip(firsts, ways)]
        late_got, came = lax.optimization_barrier((late_got, came))
        late = group.z_pair(late, late_got)
        late_far = group.z(late, 1)
        near = [group.gather_pair(v, got, way) for v, got, way in zip(firsts, came, ways)]
        x_parts[2] = group.ship(x_parts[2], 2, True)
        late_far, near, x_parts, turns = lax.optimization_barrier((late_far, near, x_parts, turns))
        cos_flat, sin_a, sin_b, cos_t, sin_t, doc_row, doc_col = turns
        for n in (3, 1):
            x_parts[n] = group.ship(x_parts[n], n, True)
        qk, vo = group.gather_cores_joined(near, ways)
        lates = join([late_far[:rows], late[:rows]]), join([late_far[rows:], late[rows:]])
        came = [group.bit(v, way[0]) for v, way in zip(lates, ways)]
        vec, bias_hidden, ada_all = modulate(me, act, qk, vo, tensor_count, rows)
        x_parts, g_parts, came, vec = lax.optimization_barrier((x_parts, g_parts, came, vec))
        for n in range(1, tensor_count):
            g_parts[n] = group.ship(g_parts[n], n, True)
        near = [group.gather_pair(v, got, way) for v, got, way in zip(lates, came, ways)]
    else:
        for n in range(1, tensor_count):
            x_parts[n] = group.ship(x_parts[n], n, True)
            g_parts[n] = group.ship(g_parts[n], n, True)
        late = group.z_pair(late, late_got)
        late = join([group.z(late, 1), late])
        flat = lambda v: group.whole(v.reshape(2, rows, width), 1).reshape(1, 2 * width, width)
        qk, vo = Held([flat(early[: 2 * rows])], [(0,)]), Held([flat(early[2 * rows :])], [(0,)])
        up, dn = (Held([group.whole(v, 0)[None]], [(0,)]) for v in (late[:rows], late[rows:]))
        w_all = group.whole(w_ada, 1)
        modulation = jnp.dot(
            act, w_all.astype(F32), precision=PRECISE, preferred_element_type=F32
        ) + group.whole(bias_ada, 0).astype(F32)
        small = group.whole(jnp.stack([bias_down, gain_one, gain_two]), 1).astype(F32)
        vec = jnp.concatenate([modulation.reshape(6, width), small, jnp.zeros((7, width), F32)])
        bias_hidden = group.whole(bias_up, 1)
        bias_hidden = jnp.concatenate([group.z(bias_hidden, k) for k in (1, 3, 0, 2)]).astype(F32)

    n_t, k, v, q_t, k_t, v_t = qkv(me, x_parts, vec, cos_flat, sin_a, sin_b, qk, vo)
    mix_t, log_sum = attend(q_t, k, v_t, doc_row, doc_col)
    if group.paired:
        mix_t, near, g_parts = lax.optimization_barrier((mix_t, near, g_parts))
        up, dn = (group.gather_cores(p, way) for p, way in zip(near, ways))
    att, n_two, n_two_t, d_down, d_down_t, d_bias_down, mix = middle(
        me, x_parts, g_parts, mix_t, vec, vo
    )
    size = w_up.shape[1]
    feed_args = (me, n_two, n_two_t, d_down, d_down_t, bias_hidden, up, dn)

    down, d_n, d_bias_a, *grads = feed(*feed_args, 0, None, 2 * size)
    sum_a = Sum(group, *grads)
    down, d_n, d_bias_b, *grads = feed(*feed_args, 2 * size, (down, d_n), 2 * size)
    down = tie(down, sum_a)
    exchange(sum_a)
    sum_b = Sum(group, *grads)
    *out_parts, d_mid, d_mix_t, sums, d_att_t = turn(
        me, x_parts, g_parts, att, down, d_n, vec, vo
    )
    d_mix_t, out_parts = tie((d_mix_t, out_parts), sum_a, sum_b)
    came = out_parts[:1] + [group.ship(out_parts[n], n, False) for n in range(1, tensor_count)]
    exchange(sum_a, sum_b)
    dq, dk, dv = attend_back(
        k, v, q_t, k_t, d_mix_t, mix_t, log_sum, doc_row, doc_col, cos_t, sin_t
    )
    dq, came = tie((dq, came), sum_a, sum_b)
    block_out = group.held_rows(came)
    sum_a.settle()
    exchange(sum_b)
    far_up = group.z(sum_a.total[0].astype(BF16), 1)
    grads = weight_grads(me, n_t, d_att_t, dq, dk, dv, mix, blocks)
    d_mid, grads, far_up, last = tie((d_mid, grads, far_up, sum_a.total[1]), sum_b)
    far_dn = group.z(last.astype(BF16), 1)
    sum_w = Sum(group, *grads)
    *in_parts, sums_one = first(me, x_parts, d_mid, vec, dq, dk, dv, qk, vo)

    in_parts, far_dn = tie((in_parts, far_dn), sum_w)
    exchange(sum_w)
    came = in_parts[:1] + [group.ship(in_parts[n], n, False) for n in range(1, tensor_count)]
    sum_b.settle()
    near = jnp.stack(sum_b.total) + jnp.stack([far_up, far_dn]).astype(F32)
    sums_one, near = tie((sums_one, near), sum_w)
    exchange(sum_w)
    edge = mod_width + 3 * rows
    if group.paired:
        length = edge + tensor_count * rows + 2 * cond_size
        keep, send, d_cond = gather_up(
            me, vec, ada_all, sums, sums_one, d_bias_down, d_bias_b, d_bias_a, act, cond, dp_count,
            length - length % cond_size,
        )
    else:
        d_gate_2, norm_2, d_shift_2, d_gate_1 = (sums[n : n + 1] for n in range(4))
        norm_1, d_shift_1 = sums_one[:1], sums_one[1:]
        d_mod = [
            d_shift_1, norm_1 * vec[GAIN_1], d_gate_1, d_shift_2, norm_2 * vec[GAIN_2], d_gate_2
        ]
        others = [norm_1 * (1.0 + vec[SCALE_1]), norm_2 * (1.0 + vec[SCALE_2]), d_bias_down]
        sliced = lambda t: t.reshape(dp_count, -1)
        d_mod = jnp.concatenate(d_mod, axis=1)
        d_cond = lax.dot_general(
            d_mod,
            w_all.astype(F32),
            (((1,), (1,)), ((), ())),
            precision=PRECISE,
            preferred_element_type=F32,
        ) * silu_slope(cond)
        table = jnp.concatenate(
            [sliced(d_mod)]
            + [sliced(t) for t in others]
            + [sliced(t) for half in (d_bias_b, d_bias_a) for t in half.reshape(2, -1)]
            + [jnp.broadcast_to(act, (dp_count, cond_size))],
            axis=1,
        )
    half = near.shape[-1] // 2
    if group.paired:
        step = [keep, group.bit(send, 0)]
        step, came, near = tie((step, came, near), sum_w)
        sum_w.settle()
        step = jnp.concatenate(step, axis=1)
        step = [step[0]] + [group.step(step[n], 2 * n) for n in range(1, dp_count // 2)]
    else:
        step = [lax.all_to_all(table, "dp", split_axis=0, concat_axis=0, tiled=True)]
    feeds = group.z(near[..., half:].astype(BF16), 2)
    near_w, far_w = sum_w.total
    far_w = group.z(far_w.astype(BF16), 1)
    step, far_w, feeds, came = lax.optimization_barrier((step, far_w, feeds, came))
    near_w = near_w + far_w.astype(F32)
    grad = group.z(near_w[..., cols:].astype(BF16), 2)
    length = step[0].shape[-1]
    d_cond = jnp.pad(d_cond, ((0, 0), (0, length - cond_size)))
    arrived = jnp.concatenate([t.reshape(-1, length) for t in step] + [d_cond])
    arrived = jnp.stack([arrived] + [group.z(arrived, k) for k in range(1, tensor_count)])
    grad = near_w[..., :cols] + grad.astype(F32)
    grad_qkv, grad_out = grad[:3], grad[3].T
    grad_up, grad_down = near[..., :half] + feeds.astype(F32)
    input_grad = group.held_rows(came)
    place = jnp.asarray([0, 2, 1, 3])[order]
    arrived = arrived[order]
    conds = arrived[:, dp_count, :cond_size]
    arrived = arrived[:, :dp_count]
    totals = jnp.sum(arrived[..., :edge], axis=(0, 1))
    biases = arrived[..., edge : edge + tensor_count * rows].reshape(
        tensor_count, dp_count, tensor_count, rows
    )
    wanted = (jnp.arange(tensor_count) == place[:, None])[:, None, :, None]
    grad_bias_up = jnp.sum(jnp.where(wanted, biases, 0.0), axis=(0, 1, 2))
    grad_bias_ada = totals[:mod_width]
    grad_gain_one, grad_gain_two, grad_bias_down = (
        totals[mod_width + n * rows : mod_width + (n + 1) * rows] for n in range(3)
    )
    arrived = arrived.reshape(dp_count * tensor_count, -1)
    grad_ada = lax.dot_general(
        arrived[:, -cond_size:],
        arrived[:, :mod_width],
        (((0,), (0,)), ((), ())),
        precision=PRECISE,
        preferred_element_type=F32,
    )
    cond_grad = jnp.take(conds, jnp.arange(per_dp) + d % 2, axis=0)
    return (
        block_out,
        input_grad,
        cond_grad,
        grad_qkv,
        grad_out,
        grad_up,
        grad_bias_up[None],
        grad_down.T,
        grad_bias_down,
        grad_gain_one,
        grad_gain_two,
        grad_ada,
        grad_bias_ada,
    )


def solution(mesh):
    return jax.shard_map(
        shards,
        mesh=mesh,
        in_specs=(
            P("dp", "tensor", None),
            P("dp", None),
            P("dp", None),
            P("dp", None),
            P(None, "dp", "tensor"),
            P("tensor", "dp"),
            P("dp", "tensor"),
            P("tensor", "dp"),
            P("tensor", "dp"),
            P("dp"),
            P("dp"),
            P("dp"),
            P(None, "dp"),
            P("dp"),
            P("dp", "tensor", None),
        ),
        out_specs=(
            P("dp", "tensor", None),
            P("dp", "tensor", None),
            P("dp", None),
            P(None, "dp", "tensor"),
            P("tensor", "dp"),
            P("dp", "tensor"),
            P("tensor", "dp"),
            P("tensor", "dp"),
            P("dp"),
            P("dp"),
            P("dp"),
            P(None, "dp"),
            P("dp"),
        ),
        check_vma=False,
    )
```
